32 devices in a mesh: dp: 8 (over z, x), tensor: 4 (over y, core).
Axes of the slice: x: 2, y: 2, z: 4, core: 2. Of those that a mesh axis runs over, the one named last changes fastest.
Arguments:
- prompt_tokens: bfloat16 [16, 768, 1024], P('dp', 'tensor'), may hold values from -6 to 6
- cont_tokens: bfloat16 [64, 768, 128], P('dp', 'tensor'), may hold values from -6 to 6
- group_map: int32 [64], P('dp'), may hold values from 0 to 15, as said below
- cont_lengths: int32 [64], P('dp'), may hold values from 64 to 128, as said below
- first_gain: float32 [768], P('tensor'), may hold values from 0.5 to 1.5
- first_bias: float32 [768], P('tensor'), may hold values from -1.25 to 1.25
- in_weight: bfloat16 [3, 768, 768], P(None, 'tensor'), may hold values from -0.21875 to 0.21875
- in_bias: float32 [3, 768], P(None, 'tensor'), may hold values from -1.25 to 1.25
- conv_kernel: float32 [3, 3, 768], P(None, None, 'tensor'), may hold values from -3 to 3
- conv_bias: float32 [3, 768], P(None, 'tensor'), may hold values from -1.25 to 1.25
- embed_weight: float32 [33, 64], replicated, may hold values from -1 to 1
- embed_bias: float32 [64], replicated, may hold values from -3 to 3
- inner_weight: float32 [64, 64], replicated, may hold values from -0.75 to 0.75
- inner_bias: float32 [64], replicated, may hold values from -3 to 3
- sine_freq: float32 [64], replicated, may hold values from 1 to 8
- filter_weight: float32 [64, 768], P(None, 'tensor'), may hold values from -0.0234375 to 0.0234375
- decay_rate: float32 [768], P('tensor'), may hold values from 0.3 to 40
- skip_gain: float32 [768], P('tensor'), may hold values from -6 to 6
- out_weight: bfloat16 [768, 768], P('tensor'), may hold values from -0.21875 to 0.21875
- out_bias: float32 [768], P('tensor'), may hold values from -1.25 to 1.25
- second_gain: float32 [768], P('tensor'), may hold values from 0.5 to 1.5
- second_bias: float32 [768], P('tensor'), may hold values from -1.25 to 1.25
- up_weight: bfloat16 [768, 3072], P(None, 'tensor'), may hold values from -0.21875 to 0.21875
- up_bias: float32 [3072], P('tensor'), may hold values from -1.25 to 1.25
- down_weight: bfloat16 [3072, 768], P('tensor'), may hold values from -0.109375 to 0.109375
- down_bias: float32 [768], P('tensor'), may hold values from -1.25 to 1.25
- prompt_cotan: bfloat16 [16, 768, 1024], P('dp', 'tensor'), may hold values from -6 to 6
- cont_cotan: bfloat16 [64, 768, 128], P('dp', 'tensor'), may hold values from -6 to 6
Outputs:
- prompt_out: bfloat16 [16, 768, 1024], P('dp', 'tensor')
- cont_out: bfloat16 [64, 768, 128], P('dp', 'tensor')
- prompt_grad: float32 [16, 768, 1024], P('dp', 'tensor')
- cont_grad: float32 [64, 768, 128], P('dp', 'tensor')
- first_gain_grad: float32 [768], P('tensor')
- first_bias_grad: float32 [768], P('tensor')
- in_weight_grad: float32 [3, 768, 768], P(None, 'tensor')
- in_bias_grad: float32 [3, 768], P(None, 'tensor')
- conv_kernel_grad: float32 [3, 3, 768], P(None, None, 'tensor')
- conv_bias_grad: float32 [3, 768], P(None, 'tensor')
- embed_weight_grad: float32 [33, 64], replicated
- embed_bias_grad: float32 [64], replicated
- inner_weight_grad: float32 [64, 64], replicated
- inner_bias_grad: float32 [64], replicated
- sine_freq_grad: float32 [64], replicated
- filter_weight_grad: float32 [64, 768], P(None, 'tensor')
- skip_gain_grad: float32 [768], P('tensor')
- out_weight_grad: float32 [768, 768], P('tensor')
- out_bias_grad: float32 [768], P('tensor')
- second_gain_grad: float32 [768], P('tensor')
- second_bias_grad: float32 [768], P('tensor')
- up_weight_grad: float32 [768, 3072], P(None, 'tensor')
- up_bias_grad: float32 [3072], P('tensor')
- down_weight_grad: float32 [3072, 768], P('tensor')
- down_bias_grad: float32 [768], P('tensor')
The draws below stay inside these ranges and needn't reach their ends.
Inputs may be any that keep to these rules, and one draw needn't show every extreme that they name: `group_map`: each continuation names one of the 2 groups whose prompts stand on the same dp index as the continuation, and each group is named by exactly 4 continuations. `cont_lengths`: on every dp index one continuation has all 128 tokens live.
All inputs are finite; a program needn't handle non-finite values.
Results may differ from the reference program's by a relative error of at most 0.018.
Values may be sent and summed in bfloat16 or wider, within the bound.
No kernel may reach another device: no remote copies, remote signals or barrier semaphores. Data moves between devices by JAX's collectives and lax.ppermute only.
A program may use at most 320 MiB of HBM per device.

```python
import math
from functools import partial
import jax
import jax.numpy as jnp
from jax import lax

D = 768
FF = 3072
FILT = 64
EMB = 33
KER = 3
PROMPT = 1024
CONT = 128
CONT_PER = 4
GRP_DEV = 2
CONT_DEV = 8
SEQ = 1152
GROUPS = 16
CONTS = 64


def permuted(key):
    return jax.random.permutation(key, CONT_DEV)


def draw_group_map(key, part):
    blocks = GROUPS // GRP_DEV
    orders = jax.vmap(permuted)(jax.random.split(jax.random.fold_in(key, 11), blocks))
    base = jnp.arange(blocks, dtype=jnp.int32)[:, None] * GRP_DEV
    return (base + orders.astype(jnp.int32) // CONT_PER).reshape(-1).astype(jnp.int32)


def draw_cont_lengths(key, part):
    blocks = GROUPS // GRP_DEV
    drawn = jax.random.randint(jax.random.fold_in(key, 21), (blocks, CONT_DEV), CONT // 2, CONT + 1)
    chosen = jax.random.randint(jax.random.fold_in(key, 22), (blocks, 1), 0, CONT_DEV)
    slots = jnp.arange(CONT_DEV, dtype=jnp.int32)[None, :]
    return jnp.where(slots == chosen, CONT, drawn).reshape(-1).astype(jnp.int32)


def level_of(stream_key, dims, shards, smallest, top_value):
    level, own = 1.0, jax.random.fold_in(stream_key, 6)
    for axis_at, shards_of in shards:
        heights = jnp.exp(jax.random.uniform(jax.random.fold_in(own, axis_at), (shards_of,), jnp.float32, smallest / len(shards), top_value / len(shards)))
        level = level * jnp.repeat(heights, dims[axis_at] // shards_of).reshape([-1 if axis == axis_at else 1 for axis in range(len(dims))])
    return level


def scatter_about(stream_key, extent, scale, limit, shards=(), kind=jnp.bfloat16):
    loudness = level_of(stream_key, extent, shards, -0.22, 0.18) if shards else 1.0
    result = jax.random.normal(stream_key, extent, jnp.float32) * scale * loudness
    return jnp.minimum(jnp.maximum(result, -limit), limit).astype(kind)


def setup_inputs(seed: int = 0) -> dict:
    streams_of = jax.random.split(jax.random.key(seed), 29)
    return {
        "prompt_tokens": scatter_about(streams_of[0], (GROUPS, D, PROMPT), 1.0, 6.0, ((0, 8), (1, 4))),
        "cont_tokens": scatter_about(streams_of[1], (CONTS, D, CONT), 1.0, 6.0, ((0, 8), (1, 4))),
        "group_map": draw_group_map(jax.random.fold_in(streams_of[28], 71), 0),
        "cont_lengths": draw_cont_lengths(jax.random.fold_in(streams_of[28], 71), 0),
        "first_gain": jnp.clip(1.0 + 0.1 * jax.random.normal(streams_of[4], (D,), jnp.float32), 0.5, 1.5),
        "first_bias": scatter_about(streams_of[5], (D,), 0.2, 1.25, ((0, 4),), jnp.float32),
        "in_weight": scatter_about(streams_of[6], (3, D, D), D ** -0.5, 0.21875, ((1, 4),)),
        "in_bias": scatter_about(streams_of[7], (3, D), 0.2, 1.25, ((1, 4),), jnp.float32),
        "conv_kernel": scatter_about(streams_of[8], (3, KER, D), 0.6, 3.0, ((2, 4),), jnp.float32),
        "conv_bias": scatter_about(streams_of[9], (3, D), 0.2, 1.25, ((1, 4),), jnp.float32),
        "embed_weight": scatter_about(streams_of[10], (EMB, FILT), EMB ** -0.5, 1.0, (), jnp.float32),
        "embed_bias": scatter_about(streams_of[11], (FILT,), 0.5, 3.0, (), jnp.float32),
        "inner_weight": scatter_about(streams_of[12], (FILT, FILT), FILT ** -0.5, 0.75, (), jnp.float32),
        "inner_bias": scatter_about(streams_of[13], (FILT,), 0.5, 3.0, (), jnp.float32),
        "sine_freq": jnp.clip(jnp.exp(jax.random.uniform(streams_of[14], (FILT,), jnp.float32, math.log(1.0), math.log(8.0))), 1.0, 8.0),
        "filter_weight": scatter_about(streams_of[15], (FILT, D), (FILT * PROMPT) ** -0.5, 0.0234375, ((1, 4),), jnp.float32),
        "decay_rate": jnp.clip(jnp.exp(math.log(40.0) - 4.8928522 * jax.random.uniform(streams_of[16], (D,), jnp.float32) ** level_of(streams_of[16], (D,), ((0, 4),), -0.2, 0.2)), 0.3, 40.0),
        "skip_gain": scatter_about(streams_of[17], (D,), 1.0, 6.0, ((0, 4),), jnp.float32),
        "out_weight": scatter_about(streams_of[18], (D, D), D ** -0.5, 0.21875, ((0, 4),)),
        "out_bias": scatter_about(streams_of[19], (D,), 0.2, 1.25, ((0, 4),), jnp.float32),
        "second_gain": jnp.clip(1.0 + 0.1 * jax.random.normal(streams_of[20], (D,), jnp.float32), 0.5, 1.5),
        "second_bias": scatter_about(streams_of[21], (D,), 0.2, 1.25, ((0, 4),), jnp.float32),
        "up_weight": scatter_about(streams_of[22], (D, FF), D ** -0.5, 0.21875, ((1, 4),)),
        "up_bias": scatter_about(streams_of[23], (FF,), 0.2, 1.25, ((0, 4),), jnp.float32),
        "down_weight": scatter_about(streams_of[24], (FF, D), FF ** -0.5, 0.109375, ((0, 4),)),
        "down_bias": scatter_about(streams_of[25], (D,), 0.2, 1.25, ((0, 4),), jnp.float32),
        "prompt_cotan": scatter_about(streams_of[26], (GROUPS, D, PROMPT), 1.0, 6.0, ((0, 8), (1, 4))),
        "cont_cotan": scatter_about(streams_of[27], (CONTS, D, CONT), 1.0, 6.0, ((0, 8), (1, 4))),
    }


epsilon = 1e-05
highest = lax.Precision.HIGHEST

@jax.custom_vjp
def low(v):
    return lax.optimization_barrier(v.astype(jnp.bfloat16)).astype(jnp.float32)

@jax.custom_vjp
def low_back(v):
    return v

def low_keep(v):
    return (low(v), None)

def low_pass(kept, grad):
    return (grad,)

def back_keep(v):
    return (v, None)

def back_low(kept, grad):
    return (low(grad),)
low.defvjp(low_keep, low_pass)
low_back.defvjp(back_keep, back_low)

def high_dot(left, right):
    return jnp.dot(left, right, precision=highest)

def layer_norm(values, gain, shift):
    center = lax.optimization_barrier(jnp.mean(values, axis=-1, keepdims=True))
    spread = lax.optimization_barrier(jnp.mean(values * values, axis=-1, keepdims=True)) - center * center
    return (values - center) * lax.rsqrt(spread + epsilon) * gain + shift

def embedding_table(length):
    steps = jnp.arange(length, dtype=jnp.float32)
    bands = (EMB - 1) // 2
    freqs = jnp.linspace(0.0001, bands - 1, bands, dtype=jnp.float32)
    angle = 2.0 * math.pi * steps[:, None] * freqs[None, :] / length
    return jnp.concatenate([steps[:, None] / (length - 1), jnp.cos(angle), -jnp.sin(angle)], axis=1)

def modulation(length, decay):
    steps = jnp.arange(length, dtype=jnp.float32) / (length - 1)
    return jnp.exp(-steps[:, None] * decay[None, :]) + 0.05

def filter_hidden(embed, embed_weight, embed_bias, inner_weight, inner_bias, sine_freq):
    first = jnp.sin(sine_freq * (high_dot(embed, embed_weight) + embed_bias))
    return jnp.sin(sine_freq * (high_dot(first, inner_weight) + inner_bias))

def short_conv(values, kernel, bias):
    length = values.shape[2]
    total = bias[:, None, None, :] + kernel[:, 0][:, None, None, :] * values
    for offset in range(1, kernel.shape[1]):
        shifted = jnp.pad(values, ((0, 0), (0, 0), (offset, 0), (0, 0)))[:, :, :length]
        total = total + kernel[:, offset][:, None, None, :] * shifted
    return total

def causal_conv(signal, response):
    length = signal.shape[0]
    size = 2 * length
    spectrum = jnp.fft.rfft(signal, n=size, axis=0) * jnp.fft.rfft(response[:length], n=size, axis=0)
    return jnp.fft.irfft(spectrum, n=size, axis=0)[:length]

def block_group(prompt_rows, cont_rows, live, embed, envelope, params):
    first_gain, first_bias, in_weight, in_bias, conv_kernel, conv_bias, embed_weight, embed_bias, inner_weight, inner_bias, sine_freq, filter_weight, skip_gain, out_weight, out_bias, second_gain, second_bias, up_weight, up_bias, down_weight, down_bias = params
    second = filter_hidden(embed, embed_weight, embed_bias, inner_weight, inner_bias, sine_freq)
    response = high_dot(second, filter_weight) * envelope
    rows = jnp.concatenate([prompt_rows, cont_rows.reshape(CONT_PER * CONT, D)], axis=0)
    normed = low(layer_norm(rows, first_gain, first_bias))
    projected = low_back(jnp.einsum('rd,ked->kre', normed, in_weight, precision=highest) + in_bias[:, None, :])
    zprompt = projected[:, None, :PROMPT]
    zcont = projected[:, PROMPT:].reshape(3, CONT_PER, CONT, D)
    conv_prompt = short_conv(zprompt, conv_kernel, conv_bias)[:, 0]
    history = jnp.broadcast_to(zprompt[:, :, PROMPT - (KER - 1):], (3, CONT_PER, KER - 1, D))
    conv_cont = short_conv(jnp.concatenate([history, zcont], axis=2), conv_kernel, conv_bias)[:, :, KER - 1:]
    gated_prompt = conv_prompt[2] * conv_prompt[1]
    gated_cont = conv_cont[2] * conv_cont[1]
    long_prompt = causal_conv(gated_prompt, response)
    joined = jnp.concatenate([jnp.broadcast_to(gated_prompt[None], (CONT_PER, PROMPT, D)), gated_cont], axis=1)
    long_cont = jax.vmap(causal_conv, in_axes=(0, None))(joined, response)[:, PROMPT:]
    mixed_prompt = (long_prompt + skip_gain * gated_prompt) * conv_prompt[0]
    mixed_cont = (long_cont + skip_gain * gated_cont) * conv_cont[0]
    mixed = low(jnp.concatenate([mixed_prompt, mixed_cont.reshape(CONT_PER * CONT, D)], axis=0))
    branch = low_back(high_dot(mixed, out_weight) + out_bias)
    resid = rows + branch
    normed_two = low(layer_norm(resid, second_gain, second_bias))
    hidden = low_back(high_dot(normed_two, up_weight) + up_bias)
    active = low(jax.nn.gelu(hidden, approximate=False))
    final = (resid + low_back(high_dot(active, down_weight) + down_bias)) * live[:, None]
    return (final[:PROMPT], final[PROMPT:].reshape(CONT_PER, CONT, D))

def reference(prompt_tokens, cont_tokens, group_map, cont_lengths, first_gain, first_bias, in_weight, in_bias, conv_kernel, conv_bias, embed_weight, embed_bias, inner_weight, inner_bias, sine_freq, filter_weight, decay_rate, skip_gain, out_weight, out_bias, second_gain, second_bias, up_weight, up_bias, down_weight, down_bias, prompt_cotan, cont_cotan):
    params = tuple((value.astype(jnp.float32) for value in (first_gain, first_bias, in_weight, in_bias, conv_kernel, conv_bias, embed_weight, embed_bias, inner_weight, inner_bias, sine_freq, filter_weight, skip_gain, out_weight, out_bias, second_gain, second_bias, up_weight, up_bias, down_weight, down_bias)))
    embed = embedding_table(SEQ)
    envelope = modulation(SEQ, decay_rate.astype(jnp.float32))
    order = jnp.argsort(group_map, stable=True).astype(jnp.int32).reshape(GROUPS, CONT_PER)
    positions = jnp.arange(CONT, dtype=jnp.int32)
    zeros = tuple((jnp.zeros_like(value) for value in params))

    def one_group(totals, index):
        members = order[index]
        live = jnp.concatenate([jnp.ones((PROMPT,), jnp.float32), (positions[None, :] < cont_lengths[members][:, None]).astype(jnp.float32).reshape(-1)])
        prompt_rows = prompt_tokens[index].astype(jnp.float32).T
        cont_rows = jnp.transpose(cont_tokens[members].astype(jnp.float32), (0, 2, 1))
        forward = partial(block_group, live=live, embed=embed, envelope=envelope)
        outputs, pullback = jax.vjp(lambda first, second, third: forward(first, second, params=third), prompt_rows, cont_rows, params)
        grads = pullback((prompt_cotan[index].astype(jnp.float32).T, jnp.transpose(cont_cotan[members].astype(jnp.float32), (0, 2, 1))))
        totals = tuple((total + grad for total, grad in zip(totals, grads[2])))
        return (totals, (outputs[0].astype(jnp.bfloat16), outputs[1].astype(jnp.bfloat16), grads[0], grads[1]))
    totals, stacked = lax.scan(one_group, zeros, jnp.arange(GROUPS, dtype=jnp.int32))
    flat = order.reshape(-1)
    cont_out = jnp.zeros((CONTS, CONT, D), jnp.bfloat16).at[flat].set(stacked[1].reshape(CONTS, CONT, D))
    cont_grad = jnp.zeros((CONTS, CONT, D), jnp.float32).at[flat].set(stacked[3].reshape(CONTS, CONT, D))
    return (jnp.transpose(stacked[0], (0, 2, 1)), jnp.transpose(cont_out, (0, 2, 1)), jnp.transpose(stacked[2], (0, 2, 1)), jnp.transpose(cont_grad, (0, 2, 1)), totals[0], totals[1], totals[2], totals[3], totals[4], totals[5], totals[6], totals[7], totals[8], totals[9], totals[10], totals[11], totals[12], totals[13], totals[14], totals[15], totals[16], totals[17], totals[18], totals[19], totals[20])
```

```python
from functools import partial
import math

import jax
import jax.numpy as jnp
import numpy as np
from jax import lax
from jax.sharding import PartitionSpec as P

EMB = 33
KER = 3
CONT = 128
GRP_DEV = 2
BLOCK = 256

epsilon = 1e-05
highest = lax.Precision.HIGHEST
f32 = jnp.float32
bf16 = jnp.bfloat16


def high_dot(left, right):
    return jnp.dot(left, right, precision=highest)


def embedding_table(length):
    steps = np.arange(length, dtype=np.float32)
    bands = (EMB - 1) // 2
    freqs = np.linspace(0.0001, bands - 1, bands, dtype=np.float32)
    angle = np.float32(2.0 * math.pi) * steps[:, None] * freqs[None, :] / np.float32(length)
    return np.concatenate(
        [steps[:, None] / np.float32(length - 1), np.cos(angle), -np.sin(angle)], axis=1
    ).astype(np.float32)


def filter_hidden(embed, embed_weight, embed_bias, inner_weight, inner_bias, sine_freq):
    first = jnp.sin(sine_freq * (high_dot(embed, embed_weight) + embed_bias))
    return jnp.sin(sine_freq * (high_dot(first, inner_weight) + inner_bias))


def block_table():
    steps = np.arange(BLOCK)
    angle = 2.0 * math.pi / BLOCK * (steps[:, None] * (steps[None, :] + 0.25))
    return np.concatenate([np.cos(angle), -np.sin(angle)], axis=1)


def spectrum(values, table):
    return jnp.dot(values.astype(bf16), table, preferred_element_type=f32)


def unspectrum(values, table):
    return lax.dot_general(
        values.astype(bf16),
        table,
        (((values.ndim - 1,), (1,)), ((), ())),
        preferred_element_type=f32,
    ) * (1.0 / BLOCK)


def split(spec):
    return (spec[..., :BLOCK], spec[..., BLOCK:])


def mul(a, b):
    return (a[0] * b[0] - a[1] * b[1], a[0] * b[1] + a[1] * b[0])


def mul_conj(a, b):
    return (a[0] * b[0] + a[1] * b[1], a[1] * b[0] - a[0] * b[1])


def add(a, b):
    return (a[0] + b[0], a[1] + b[1])


def total(items):
    result = items[0]
    for item in items[1:]:
        result = add(result, item)
    return result


def plus_i(a, b):
    return jnp.concatenate([a[0] - b[1], a[1] + b[0]], axis=-1)


def minus_i(a, b):
    return jnp.concatenate([a[0] + b[1], a[1] - b[0]], axis=-1)


def both(a):
    return jnp.concatenate(a, axis=-1)


def shift_right(values, offset, history):
    return jnp.concatenate([history, values[..., : values.shape[-1] - offset]], axis=-1)


def shift_left(values, offset):
    pad = jnp.zeros(values.shape[:-1] + (offset,), values.dtype)
    return jnp.concatenate([values[..., offset:], pad], axis=-1)


class Sizes:
    pass


def conts_of(values, sz):
    return values[..., sz.prompt :].reshape(values.shape[:-1] + (sz.per, CONT))


def conv_parts(proj, kernel, bias, sz):
    zp = proj[..., : sz.prompt]
    zc = conts_of(proj, sz)
    edge = zp[..., sz.prompt - (KER - 1) :]
    cp = bias[:, :, None] + kernel[:, 0, :, None] * zp
    cc = bias[:, :, None, None] + kernel[:, 0, :, None, None] * zc
    for offset in range(1, KER):
        zero = jnp.zeros(zp.shape[:-1] + (offset,), f32)
        cp = cp + kernel[:, offset, :, None] * shift_right(zp, offset, zero)
        hist = jnp.broadcast_to(
            edge[..., None, KER - 1 - offset :], zc.shape[:-1] + (offset,)
        )
        cc = cc + kernel[:, offset, :, None, None] * shift_right(zc, offset, hist)
    return (cp, cc)


def gated_spectra(cp, cc, table, sz):
    gp = cp[2] * cp[1]
    gc = cc[2] * cc[1]
    width = gp.shape[0]
    xp = spectrum(gp.reshape(width, sz.blocks, BLOCK), table)
    xc = spectrum(gc, table[:CONT])
    return (gp, gc, [split(xp[:, i]) for i in range(sz.blocks)], split(xc))


def lift(pair):
    return (pair[0][:, None], pair[1][:, None])


def mixer_fwd(proj, kernel, bias, skip, resp, table, sz):
    cp, cc = conv_parts(proj, kernel, bias, sz)
    gp, gc, xp, xc = gated_spectra(cp, cc, table, sz)
    n = sz.blocks
    sums = []
    for m in range(n + 1):
        sums.append(total([mul(xp[i], resp[m - i]) for i in range(n) if 0 <= m - i <= n]))
    spec = [both(sums[0])] + [plus_i(sums[m], sums[m - 1]) for m in range(1, n)]
    lp = unspectrum(jnp.stack(spec, axis=1), table).reshape(gp.shape)
    carried = plus_i(sums[n], sums[n - 1])
    own = both(mul(xc, lift(resp[0]))) + carried[:, None]
    lc = unspectrum(own, table[:CONT])
    up = lp + skip[:, None] * gp
    uc = lc + skip[:, None, None] * gc
    width = gp.shape[0]
    mixed = jnp.concatenate([up * cp[0], (uc * cc[0]).reshape(width, -1)], axis=1).astype(bf16)
    u = jnp.concatenate([up, uc.reshape(width, -1)], axis=1)
    return (mixed, u)


def mixer_bwd(grad_mixed, proj, u, kernel, bias, skip, resp, table, sz):
    cp, cc = conv_parts(proj, kernel, bias, sz)
    gp, gc, xp, xc = gated_spectra(cp, cc, table, sz)
    width = gp.shape[0]
    n = sz.blocks
    dmp, dmc = grad_mixed[:, : sz.prompt], conts_of(grad_mixed, sz)
    upp, uc = u[:, : sz.prompt], conts_of(u, sz)
    glp = dmp * cp[0]
    glc = dmc * cc[0]
    gx = spectrum(glp.reshape(width, n, BLOCK), table)
    gs = [split(gx[:, i]) for i in range(n)]
    gcs = split(spectrum(glc, table[:CONT]))
    gs.append((jnp.sum(gcs[0], axis=1), jnp.sum(gcs[1], axis=1)))
    back = []
    for i in range(n + 1):
        back.append(total([mul_conj(gs[m], resp[m - i]) for m in range(i, n + 1)]))
    spec = [minus_i(back[i], back[i + 1]) for i in range(n)]
    ggp = skip[:, None] * glp + unspectrum(jnp.stack(spec, axis=1), table).reshape(gp.shape)
    ggc = skip[:, None, None] * glc + unspectrum(both(mul_conj(gcs, lift(resp[0]))), table[:CONT])
    lag = []
    for j in range(n + 1):
        items = [mul_conj(gs[m], xp[m - j]) for m in range(j, n + 1) if m - j < n]
        lag.append(total(items))
    own = mul_conj(gcs, xc)
    lag[0] = add(lag[0], (jnp.sum(own[0], axis=1), jnp.sum(own[1], axis=1)))
    spec = [minus_i(lag[j], lag[j + 1]) for j in range(n)] + [both(lag[n])]
    resp_grad = unspectrum(jnp.stack(spec, axis=1), table).reshape(width, -1)[:, : sz.seq]
    skip_grad = jnp.sum(glp * gp, axis=1) + jnp.sum(glc * gc, axis=(1, 2))
    gcp = jnp.stack([dmp * upp, ggp * cp[2], ggp * cp[1]])
    gcc = jnp.stack([dmc * uc, ggc * cc[2], ggc * cc[1]])
    bias_grad = jnp.sum(gcp, axis=2) + jnp.sum(gcc, axis=(2, 3))
    zp = proj[..., : sz.prompt]
    zc = conts_of(proj, sz)
    edge = zp[..., sz.prompt - (KER - 1) :]
    kernel_grad = []
    for j in range(KER):
        if j == 0:
            sp, sc = zp, zc
        else:
            sp = shift_right(zp, j, jnp.zeros(zp.shape[:-1] + (j,), f32))
            hist = jnp.broadcast_to(edge[..., None, KER - 1 - j :], zc.shape[:-1] + (j,))
            sc = shift_right(zc, j, hist)
        kernel_grad.append(jnp.sum(gcp * sp, axis=2) + jnp.sum(gcc * sc, axis=(2, 3)))
    kernel_grad = jnp.stack(kernel_grad, axis=1)
    k = [kernel[:, j, :, None] for j in range(KER)]
    gzp = k[0] * gcp + k[1] * shift_left(gcp, 1) + k[2] * shift_left(gcp, 2)
    kc = [kernel[:, j, :, None, None] for j in range(KER)]
    gzc = kc[0] * gcc + kc[1] * shift_left(gcc, 1) + kc[2] * shift_left(gcc, 2)
    heads = jnp.sum(gcc[..., : KER - 1], axis=2)
    tail = jnp.concatenate(
        [k[2] * heads[..., :1], k[1] * heads[..., :1] + k[2] * heads[..., 1:2]], axis=-1
    )
    gzp = jnp.concatenate(
        [gzp[..., : sz.prompt - 2], gzp[..., sz.prompt - 2 :] + tail], axis=-1
    )
    gz = jnp.concatenate([gzp, gzc.reshape(3, width, -1)], axis=2).astype(bf16)
    return (gz, resp_grad, skip_grad, bias_grad, kernel_grad)


def normalize(values):
    count = values.shape[0]
    center = jnp.sum(values, axis=0, keepdims=True) / count
    spread = jnp.sum(values * values, axis=0, keepdims=True) / count - center * center
    scale = lax.rsqrt(spread + epsilon)
    return ((values - center) * scale, scale)


def norm_backward(grad, normal, scale, gain):
    g = grad * gain
    count = g.shape[0]
    first = jnp.sum(g, axis=0, keepdims=True) / count
    second = jnp.sum(g * normal, axis=0, keepdims=True) / count
    return scale * (g - first - normal * second)


def swap(axis, count, bit):
    def run(values):
        return lax.ppermute(values, axis, [(i, i ^ bit) for i in range(count)])

    return run


over_y = swap("tensor", 4, 2)
over_c = swap("tensor", 4, 1)


def reduce_dp(values, count, index, first=1):
    bits = [1 << b for b in range(count.bit_length() - 1)]
    held = values
    for bit in bits:
        half = held.shape[0] // 2
        high = (index & bit) != 0
        low_part, high_part = held[:half], held[half:]
        give = jnp.where(high, low_part, high_part).astype(bf16)
        keep = jnp.where(high, high_part, low_part)
        held = keep + swap("dp", count, bit)(give).astype(f32)
    held = held.astype(bf16)
    for bit in reversed(bits):
        high = (index & bit) != 0
        other = swap("dp", count, bit)(held)
        held = jnp.where(
            high,
            jnp.concatenate([other, held], axis=0),
            jnp.concatenate([held, other], axis=0),
        )
    return held.astype(f32)


def reduce_small(values, count):
    bit = 1
    while bit < count:
        values = values + swap("dp", count, bit)(values)
        bit *= 2
    return values


def shards(dp_count, *args):
    (
        prompt_tokens,
        cont_tokens,
        group_map,
        cont_lengths,
        first_gain,
        first_bias,
        in_weight,
        in_bias,
        conv_kernel,
        conv_bias,
        embed_weight,
        embed_bias,
        inner_weight,
        inner_bias,
        sine_freq,
        filter_weight,
        decay_rate,
        skip_gain,
        out_weight,
        out_bias,
        second_gain,
        second_bias,
        up_weight,
        up_bias,
        down_weight,
        down_bias,
        prompt_cotan,
        cont_cotan,
    ) = args
    width = prompt_tokens.shape[1]
    sz = Sizes()
    sz.prompt = prompt_tokens.shape[2]
    sz.seq = sz.prompt + CONT
    sz.blocks = sz.prompt // BLOCK
    conts = cont_tokens.shape[0]
    sz.per = conts // GRP_DEV
    features = 4 * width
    t = lax.axis_index("tensor")
    y = t // 2
    dp = lax.axis_index("dp")
    table = jnp.asarray(block_table(), bf16)

    local = group_map % GRP_DEV
    ids = jnp.arange(conts, dtype=jnp.int32)
    before = (ids[None, :] < ids[:, None]) & (local[None, :] == local[:, None])
    slot = local * sz.per + jnp.sum(before.astype(jnp.int32), axis=1)
    order = jnp.sum(jnp.where(slot[None, :] == ids[:, None], ids[None, :], 0), axis=1)

    def pick(prompt, cont, group):
        parts = [lax.dynamic_index_in_dim(prompt, group, 0, False)]
        for i in range(sz.per):
            member = lax.dynamic_index_in_dim(order, group * sz.per + i, 0, False)
            parts.append(lax.dynamic_index_in_dim(cont, member, 0, False))
        return jnp.concatenate(parts, axis=1)

    def blocks_of(keep, send):
        got = over_y(send)
        return [keep, over_c(keep), got, over_c(got)]

    def place(parts):
        full = jnp.zeros((features,) + parts[0].shape[1:], parts[0].dtype)
        for r, part in enumerate(parts):
            full = lax.dynamic_update_slice(full, part, (width * (t ^ r), 0))
        return full

    lengths = jnp.stack(
        [
            lax.dynamic_index_in_dim(
                cont_lengths, lax.dynamic_index_in_dim(order, y * sz.per + i, 0, False), 0, False
            )
            for i in range(sz.per)
        ]
    )
    rows_count = sz.prompt + sz.per * CONT
    positions = jnp.arange(CONT, dtype=jnp.int32)
    live = jnp.concatenate(
        [
            jnp.ones((1, sz.prompt), f32),
            (positions[None, :] < lengths[:, None]).astype(f32).reshape(1, -1),
        ],
        axis=1,
    )

    rows = place(
        blocks_of(pick(prompt_tokens, cont_tokens, y), pick(prompt_tokens, cont_tokens, 1 - y))
    ).astype(f32)
    in_w = [in_weight, over_y(in_weight)]
    channel = jnp.concatenate(
        [
            in_bias,
            conv_kernel.reshape(KER * 3, width),
            conv_bias,
            skip_gain[None],
            decay_rate[None],
            filter_weight,
        ],
        axis=0,
    )
    channels = [channel, over_y(channel)]
    vectors = jnp.stack([first_gain, first_bias, out_bias, second_gain, second_bias, down_bias], 1)
    vectors = place(blocks_of(vectors, vectors))
    first_gain, first_bias, out_bias, second_gain, second_bias, down_bias = [
        vectors[:, i : i + 1] for i in range(6)
    ]
    up_b = [up_bias, over_y(up_bias)]
    out_w = [out_weight, over_y(out_weight)]
    up_w = [up_weight, over_y(up_weight)]
    down_w = [down_weight, over_y(down_weight)]
    grad_back = place(
        blocks_of(pick(prompt_cotan, cont_cotan, y), pick(prompt_cotan, cont_cotan, 1 - y))
    )
    grad_out = grad_back.astype(f32) * live
    grad_back = grad_out.astype(bf16)

    embed = jnp.asarray(embedding_table(sz.seq))
    filter_second, filter_pull = jax.vjp(
        partial(filter_hidden, embed), embed_weight, embed_bias, inner_weight, inner_bias, sine_freq
    )
    steps = jnp.arange(sz.seq, dtype=f32) / (sz.seq - 1)
    resp, envelope = [], []
    for b in range(2):
        decay, weight = channels[b][16], channels[b][17:]
        env = jnp.exp(-decay[:, None] * steps[None, :]) + 0.05
        response = (
            lax.dot_general(weight, filter_second, (((0,), (1,)), ((), ())), precision=highest)
            * env
        )
        padded = jnp.pad(response, ((0, 0), (0, (sz.blocks + 1) * BLOCK - sz.seq)))
        spec = spectrum(padded.reshape(width, sz.blocks + 1, BLOCK), table)
        resp.append([split(spec[:, j]) for j in range(sz.blocks + 1)])
        envelope.append(env)

    normal_one, scale_one = normalize(rows)
    normed_one = (normal_one * first_gain + first_bias).astype(bf16)
    mixed, saved = [], []
    for b in range(2):
        proj = (
            jnp.einsum("kod,dr->kor", in_w[b], normed_one, preferred_element_type=f32)
            + channels[b][:3, :, None]
        )
        kernel = channels[b][3:12].reshape(3, KER, width)
        bias, skip = channels[b][12:15], channels[b][15]
        part, u = mixer_fwd(proj, kernel, bias, skip, resp[b], table, sz)
        mixed.append(part)
        saved.append((proj, u, kernel, bias, skip))
    mixed_all = mixed + [over_c(part) for part in mixed]
    out_all = out_w + [over_c(part) for part in out_w]
    branch = jnp.einsum(
        "cd,cr->dr",
        jnp.concatenate(out_all, axis=0),
        jnp.concatenate(mixed_all, axis=0),
        preferred_element_type=f32,
    )
    resid = rows + branch + out_bias
    normal_two, scale_two = normalize(resid)
    normed_two = (normal_two * second_gain + second_bias).astype(bf16)
    final, two = 0.0, 0.0
    up_grad, down_grad, up_bias_grad = [], [], []
    for b in range(2):
        hidden = (
            jnp.einsum("df,dr->fr", up_w[b], normed_two, preferred_element_type=f32)
            + up_b[b][:, None]
        )
        cdf = 0.5 * lax.erfc(-hidden * math.sqrt(0.5))
        pdf = jnp.exp(-0.5 * hidden * hidden) * (1.0 / math.sqrt(2.0 * math.pi))
        active = (hidden * cdf).astype(bf16)
        final = final + jnp.einsum("fd,fr->dr", down_w[b], active, preferred_element_type=f32)
        grad_active = jnp.einsum("fd,dr->fr", down_w[b], grad_back, preferred_element_type=f32)
        grad_hidden = (grad_active * (cdf + hidden * pdf)).astype(bf16)
        up_bias_grad.append(jnp.sum(grad_hidden, axis=1, dtype=f32))
        two = two + jnp.einsum("df,fr->dr", up_w[b], grad_hidden, preferred_element_type=f32)
        down_grad.append(
            jnp.einsum("fr,dr->fd", active, grad_back, preferred_element_type=f32)
        )
        up_grad.append(
            jnp.einsum("dr,fr->df", normed_two, grad_hidden, preferred_element_type=f32)
        )

    def mine(values, r):
        return lax.dynamic_slice_in_dim(values, width * (t ^ r), width, 0)

    passed = [over_c(mine(final, r).astype(bf16)) for r in (1, 3)]
    ends = []
    for got, r in zip(passed, (0, 2)):
        value = mine(resid, r) + mine(final, r) + got.astype(f32) + mine(down_bias, r)
        ends.append((value * live).astype(bf16))
    out_pair = [ends[0], over_y(ends[1])]

    down_bias_grad = jnp.sum(grad_back, axis=1, dtype=f32)
    two = two + 0.0
    grad_two = two + over_c(two.astype(bf16)).astype(f32)
    second_gain_grad = jnp.sum(grad_two * normal_two, axis=1)
    second_bias_grad = jnp.sum(grad_two, axis=1)
    resid_grad = grad_out + norm_backward(grad_two, normal_two, scale_two, second_gain)
    grad_branch = resid_grad.astype(bf16)
    out_bias_grad = jnp.sum(grad_branch, axis=1, dtype=f32)
    out_grad, in_grad, chan_grads, second_grads, pieces = [], [], [], 0.0, 0.0
    for b in range(2):
        proj, u, kernel, bias, skip = saved[b]
        out_grad.append(
            jnp.einsum("cr,dr->cd", mixed[b], grad_branch, preferred_element_type=f32)
        )
        grad_mixed = jnp.dot(out_w[b], grad_branch, preferred_element_type=f32)
        gz, resp_grad, skip_grad, bias_grad, kernel_grad = mixer_bwd(
            grad_mixed, proj, u, kernel, bias, skip, resp[b], table, sz
        )
        grad_raw = resp_grad * envelope[b]
        weight = channels[b][17:]
        weight_grad = lax.dot_general(
            filter_second, grad_raw, (((0,), (1,)), ((), ())), precision=highest
        )
        second_grads = second_grads + lax.dot_general(
            grad_raw, weight, (((0,), (1,)), ((), ())), precision=highest
        )
        in_bias_grad = jnp.sum(gz, axis=2, dtype=f32)
        chan_grads.append(
            jnp.concatenate(
                [
                    in_bias_grad,
                    kernel_grad.reshape(3 * KER, width),
                    bias_grad,
                    skip_grad[None],
                    weight_grad,
                ],
                axis=0,
            )
        )
        in_grad.append(
            jnp.einsum("ker,dr->ked", gz, normed_one, preferred_element_type=f32)
        )
        pieces = pieces + jnp.einsum("ked,ker->dr", in_w[b], gz, preferred_element_type=f32)
    grad_one = pieces + over_c(pieces.astype(bf16)).astype(f32)
    first_gain_grad = jnp.sum(grad_one * normal_one, axis=1)
    first_bias_grad = jnp.sum(grad_one, axis=1)
    input_grad = resid_grad + norm_backward(grad_one, normal_one, scale_one, first_gain)
    grad_pair = [mine(input_grad, 0), over_y(mine(input_grad, 2).astype(bf16)).astype(f32)]

    def join(pair):
        return pair[0] + over_y(pair[1].astype(bf16)).astype(f32)

    def reduced(pair):
        value = join(pair)
        flat = value.reshape(-1, features)
        return reduce_dp(flat, dp_count, dp).reshape(value.shape)

    down_weight_grad = reduced(down_grad)
    up_weight_grad = reduced(up_grad)
    out_weight_grad = reduced(out_grad)
    in_weight_grad = reduced(in_grad)

    vector_grads = jnp.stack(
        [
            first_gain_grad,
            first_bias_grad,
            out_bias_grad,
            second_gain_grad,
            second_bias_grad,
            down_bias_grad,
        ],
        axis=1,
    )
    vector_sum = mine(vector_grads, 0) + over_y(mine(vector_grads, 2))
    chan_sum = chan_grads[0] + over_y(chan_grads[1])
    up_bias_sum = up_bias_grad[0] + over_y(up_bias_grad[1])
    filter_grads = filter_pull(second_grads)
    filter_flat = jnp.concatenate([value.reshape(-1) for value in filter_grads])
    filter_flat = filter_flat + over_c(filter_flat)
    filter_flat = filter_flat + over_y(filter_flat)
    packed = jnp.concatenate(
        [vector_sum.reshape(-1), chan_sum.reshape(-1), up_bias_sum, filter_flat]
    )
    packed = reduce_small(packed, dp_count)
    sizes = [vector_sum.size, chan_sum.size, up_bias_sum.size]
    marks = np.cumsum(sizes)
    vector_sum = packed[: marks[0]].reshape(vector_sum.shape)
    chan_sum = packed[marks[0] : marks[1]].reshape(chan_sum.shape)
    up_bias_sum = packed[marks[1] : marks[2]]
    rest = packed[marks[2] :]
    filter_out = []
    at = 0
    for value in filter_grads:
        filter_out.append(rest[at : at + value.size].reshape(value.shape))
        at += value.size

    def unpack(pair):
        prompts = jnp.stack([value[:, : sz.prompt] for value in pair])
        prompts = jnp.stack(
            [lax.dynamic_index_in_dim(prompts, g ^ y, 0, False) for g in range(GRP_DEV)]
        )
        pool = jnp.concatenate(
            [
                jnp.transpose(value[:, sz.prompt :].reshape(width, sz.per, CONT), (1, 0, 2))
                for value in pair
            ],
            axis=0,
        )
        rel = slot ^ (sz.per * y)
        return (prompts, jnp.take(pool, rel, axis=0, mode="clip"))

    prompt_out, cont_out = unpack(out_pair)
    prompt_grad, cont_grad = unpack(grad_pair)
    return (
        prompt_out,
        cont_out,
        prompt_grad,
        cont_grad,
        vector_sum[:, 0],
        vector_sum[:, 1],
        in_weight_grad,
        chan_sum[:3],
        chan_sum[3:12].reshape(3, KER, width),
        chan_sum[12:15],
        filter_out[0],
        filter_out[1],
        filter_out[2],
        filter_out[3],
        filter_out[4],
        chan_sum[16:],
        chan_sum[15],
        out_weight_grad,
        vector_sum[:, 2],
        vector_sum[:, 3],
        vector_sum[:, 4],
        up_weight_grad,
        up_bias_sum,
        down_weight_grad,
        vector_sum[:, 5],
    )


def solution(mesh):
    placed = (
        P("dp", "tensor", None),
        P("dp", "tensor", None),
        P("dp"),
        P("dp"),
        P("tensor"),
        P("tensor"),
        P(None, "tensor", None),
        P(None, "tensor"),
        P(None, None, "tensor"),
        P(None, "tensor"),
        P(),
        P(),
        P(),
        P(),
        P(),
        P(None, "tensor"),
        P("tensor"),
        P("tensor"),
        P("tensor", None),
        P("tensor"),
        P("tensor"),
        P("tensor"),
        P(None, "tensor"),
        P("tensor"),
        P("tensor", None),
        P("tensor"),
        P("dp", "tensor", None),
        P("dp", "tensor", None),
    )
    return jax.shard_map(
        partial(shards, mesh.shape["dp"]),
        mesh=mesh,
        in_specs=placed,
        out_specs=(
            P("dp", "tensor", None),
            P("dp", "tensor", None),
            P("dp", "tensor", None),
            P("dp", "tensor", None),
            P("tensor"),
            P("tensor"),
            P(None, "tensor", None),
            P(None, "tensor"),
            P(None, None, "tensor"),
            P(None, "tensor"),
            P(),
            P(),
            P(),
            P(),
            P(),
            P(None, "tensor"),
            P("tensor"),
            P("tensor", None),
            P("tensor"),
            P("tensor"),
            P("tensor"),
            P(None, "tensor"),
            P("tensor"),
            P("tensor", None),
            P("tensor"),
        ),
        check_vma=False,
    )
```

```python
from functools import partial
import math

import jax
import jax.numpy as jnp
import numpy as np
from jax import lax
from jax.experimental import pallas as pl
from jax.experimental.pallas import tpu as pltpu
from jax.sharding import PartitionSpec as P

EMB = 33
KER = 3
CONT = 128
GRP_DEV = 2
BLOCK = 256

epsilon = 1e-05
highest = lax.Precision.HIGHEST
f32 = jnp.float32
bf16 = jnp.bfloat16


def high_dot(left, right):
    return jnp.dot(left, right, precision=highest)


def embedding_table(length):
    steps = np.arange(length, dtype=np.float32)
    bands = (EMB - 1) // 2
    freqs = np.linspace(0.0001, bands - 1, bands, dtype=np.float32)
    angle = np.float32(2.0 * math.pi) * steps[:, None] * freqs[None, :] / np.float32(length)
    return np.concatenate(
        [steps[:, None] / np.float32(length - 1), np.cos(angle), -np.sin(angle)], axis=1
    ).astype(np.float32)


def filter_hidden(embed, embed_weight, embed_bias, inner_weight, inner_bias, sine_freq):
    first = jnp.sin(sine_freq * (high_dot(embed, embed_weight) + embed_bias))
    return jnp.sin(sine_freq * (high_dot(first, inner_weight) + inner_bias))


def block_table():
    steps = np.arange(BLOCK)
    angle = 2.0 * math.pi / BLOCK * (steps[:, None] * (steps[None, :] + 0.25))
    return np.concatenate([np.cos(angle), -np.sin(angle)], axis=1)


def spectrum(values, table):
    return jnp.dot(values.astype(bf16), table, preferred_element_type=f32)


class Sizes:
    pass


LANES = 128
ROWS = 16
BIAS_IN, KERNEL, BIAS_CONV, SKIP, DECAY, FILTER = 0, 3, 12, 15, 16, 17


def cmul(a, b):
    return (a[0] * b[0] - a[1] * b[1], a[0] * b[1] + a[1] * b[0])


def cmul_conj(a, b):
    return (a[0] * b[0] + a[1] * b[1], a[1] * b[0] - a[0] * b[1])


def cadd(items):
    result = items[0]
    for item in items[1:]:
        result = (result[0] + item[0], result[1] + item[1])
    return result


def plus_i(a, b):
    return (a[0] - b[1], a[1] + b[0])


def minus_i(a, b):
    return (a[0] + b[1], a[1] - b[0])


def lane_slice(v):
    return slice(v * LANES, (v + 1) * LANES)


def column(chan, rows, at):
    return jnp.broadcast_to(chan[rows, at : at + 1], (ROWS, LANES))


def conv_stream(load, chan, rows, k, lane, prompt_tiles, tiles):
    bias = column(chan, rows, BIAS_CONV + k)
    taps = [column(chan, rows, KERNEL + KER * k + j) for j in range(KER)]
    before = [jnp.zeros((ROWS, LANES), f32)] * (KER - 1)
    last = None
    for v in range(tiles):
        value = load(k, v)
        rolled = [pltpu.roll(value, j, 1) for j in range(1, KER)]
        result = bias + taps[0] * value
        history = before if v < prompt_tiles else last
        for j in range(1, KER):
            result = result + taps[j] * jnp.where(lane < j, history[j - 1], rolled[j - 1])
        if v < prompt_tiles:
            before = rolled
            last = rolled
        yield v, value, result


def block_parts(sz):
    parts = [(slice(i * BLOCK, (i + 1) * BLOCK), BLOCK) for i in range(sz.blocks)]
    start = sz.prompt
    parts += [(slice(start + n * CONT, start + (n + 1) * CONT), CONT) for n in range(sz.per)]
    return parts


def freq_pair(ref, index, rows, tile):
    real = ref[index, rows, lane_slice(tile)]
    imag = ref[index, rows, lane_slice(tile + BLOCK // LANES)]
    return (real, imag)


def store_pair(ref, index, rows, tile, pair):
    ref[index, rows, lane_slice(tile)] = pair[0].astype(ref.dtype)
    ref[index, rows, lane_slice(tile + BLOCK // LANES)] = pair[1].astype(ref.dtype)


def mixer_fwd_kernel(
    sz, normed, weight, chan, resp, table, inverse, mixed, proj, u, z, gb, spec, prod
):
    width = chan.shape[0]
    tiles = normed.shape[1] // LANES
    prompt_tiles = sz.prompt // LANES
    parts = block_parts(sz)
    n = sz.blocks

    @pl.loop(0, normed.shape[1] // BLOCK)
    def _(i):
        cols = pl.ds(pl.multiple_of(i * BLOCK, BLOCK), BLOCK)
        got = jnp.dot(weight[...], normed[:, cols], preferred_element_type=f32)
        for k in range(3):
            z[k, :, cols] = got[k * width : (k + 1) * width]

    @pl.loop(0, width // ROWS)
    def _(c):
        rows = pl.ds(pl.multiple_of(c * ROWS, ROWS), ROWS)
        lane = lax.broadcasted_iota(jnp.int32, (ROWS, LANES), 1)
        biases = [column(chan, rows, BIAS_IN + k) for k in range(3)]

        def load(k, v):
            return z[k, rows, lane_slice(v)] + biases[k]

        streams = [conv_stream(load, chan, rows, k, lane, prompt_tiles, tiles) for k in range(3)]
        for first, second, third in zip(*streams):
            v = first[0]
            for k, item in enumerate((first, second, third)):
                proj[k, rows, lane_slice(v)] = item[1].astype(bf16)
            gated = second[2] * third[2]
            z[0, rows, lane_slice(v)] = first[2]
            z[1, rows, lane_slice(v)] = gated
            gb[rows, lane_slice(v)] = gated.astype(bf16)

    for i, (cols, length) in enumerate(parts):
        spec[i] = jnp.dot(gb[:, cols], table[:length, :], preferred_element_type=f32)

    @pl.loop(0, width // ROWS)
    def _(c):
        rows = pl.ds(pl.multiple_of(c * ROWS, ROWS), ROWS)
        for tile in range(BLOCK // LANES):
            xs = [freq_pair(spec, i, rows, tile) for i in range(n)]
            hs = [freq_pair(resp, j, rows, tile) for j in range(n + 1)]
            prior = None
            for m in range(n + 1):
                now = cadd([cmul(xs[i], hs[m - i]) for i in range(n) if 0 <= m - i <= n])
                out = now if prior is None else plus_i(now, prior)
                prior = now
                if m < n:
                    store_pair(prod, m, rows, tile, out)
            for q in range(sz.per):
                own = cmul(freq_pair(spec, n + q, rows, tile), hs[0])
                store_pair(prod, n + q, rows, tile, cadd([own, out]))

    skip = chan[:, SKIP : SKIP + 1]
    for i, (cols, length) in enumerate(parts):
        value = jnp.dot(prod[i], inverse[:, :length], preferred_element_type=f32)
        value = value + skip * z[1, :, cols]
        u[:, cols] = value.astype(bf16)
        mixed[:, cols] = (value * z[0, :, cols]).astype(bf16)


def mixer_bwd_kernel(
    sz,
    branch,
    weight,
    proj,
    u,
    chan,
    resp,
    table,
    inverse,
    gz,
    resp_grad,
    sums,
    dm,
    conv,
    gb,
    lb,
    gspec,
    xspec,
    prod,
    gg,
):
    width = chan.shape[0]
    tiles = branch.shape[1] // LANES
    prompt_tiles = sz.prompt // LANES
    parts = block_parts(sz)
    n = sz.blocks

    @pl.loop(0, branch.shape[1] // BLOCK)
    def _(i):
        cols = pl.ds(pl.multiple_of(i * BLOCK, BLOCK), BLOCK)
        dm[:, cols] = jnp.dot(weight[...], branch[:, cols], preferred_element_type=f32)

    def place_sum(rows, lane, at, value):
        total = jnp.sum(value, axis=1, keepdims=True)
        sums[rows, :] = jnp.where(lane == at, total, sums[rows, :])

    @pl.loop(0, width // ROWS)
    def _(c):
        rows = pl.ds(pl.multiple_of(c * ROWS, ROWS), ROWS)
        lane = lax.broadcasted_iota(jnp.int32, (ROWS, LANES), 1)

        def load(k, v):
            return proj[k, rows, lane_slice(v)].astype(f32)

        streams = [conv_stream(load, chan, rows, k, lane, prompt_tiles, tiles) for k in range(3)]
        skips = jnp.zeros((ROWS, LANES), f32)
        for first, second, third in zip(*streams):
            v = first[0]
            for k, item in enumerate((first, second, third)):
                conv[k, rows, lane_slice(v)] = item[2]
            gated = second[2] * third[2]
            long = dm[rows, lane_slice(v)] * first[2]
            skips = skips + long * gated
            gb[rows, lane_slice(v)] = gated.astype(bf16)
            lb[rows, lane_slice(v)] = long.astype(bf16)
        sums[rows, :] = jnp.zeros((ROWS, LANES), f32)
        place_sum(rows, lane, SKIP, skips)

    for i, (cols, length) in enumerate(parts):
        gspec[i] = jnp.dot(lb[:, cols], table[:length, :], preferred_element_type=f32)
        xspec[i] = jnp.dot(gb[:, cols], table[:length, :], preferred_element_type=f32)

    @pl.loop(0, width // ROWS)
    def _(c):
        rows = pl.ds(pl.multiple_of(c * ROWS, ROWS), ROWS)
        for tile in range(BLOCK // LANES):
            gs = [freq_pair(gspec, i, rows, tile) for i in range(n)]
            hs = [freq_pair(resp, j, rows, tile) for j in range(n + 1)]
            own, lags = [], []
            for q in range(sz.per):
                g = freq_pair(gspec, n + q, rows, tile)
                own.append(g)
                store_pair(prod, n + q, rows, tile, cmul_conj(g, hs[0]))
                lags.append(cmul_conj(g, freq_pair(xspec, n + q, rows, tile)))
            gs.append(cadd(own))
            after = cmul_conj(gs[n], hs[0])
            for i in reversed(range(n)):
                now = cadd([cmul_conj(gs[m], hs[m - i]) for m in range(i, n + 1)])
                store_pair(prod, i, rows, tile, minus_i(now, after))
                after = now
            xs = [freq_pair(xspec, i, rows, tile) for i in range(n)]
            after = None
            for j in reversed(range(n + 1)):
                items = [cmul_conj(gs[m], xs[m - j]) for m in range(j, n + 1) if m - j < n]
                now = cadd(items + (lags if j == 0 else []))
                out = now if after is None else minus_i(now, after)
                store_pair(prod, n + sz.per + j, rows, tile, out)
                after = now

    skip = chan[:, SKIP : SKIP + 1]
    for i, (cols, length) in enumerate(parts):
        value = jnp.dot(prod[i], inverse[:, :length], preferred_element_type=f32)
        gg[:, cols] = value + skip * (dm[:, cols] * conv[0, :, cols])
    for j in range(n + 1):
        resp_grad[:, j * BLOCK : (j + 1) * BLOCK] = jnp.dot(
            prod[n + sz.per + j], inverse[...], preferred_element_type=f32
        )

    @pl.loop(0, width // ROWS)
    def _(c):
        rows = pl.ds(pl.multiple_of(c * ROWS, ROWS), ROWS)
        lane = lax.broadcasted_iota(jnp.int32, (ROWS, LANES), 1)
        zero = jnp.zeros((ROWS, LANES), f32)
        for k in range(3):
            taps = [column(chan, rows, KERNEL + KER * k + j) for j in range(KER)]
            total_bias, total_out = zero, zero
            total_taps = [zero] * KER
            heads = zero
            after = None
            for v in list(range(prompt_tiles, tiles)) + list(reversed(range(prompt_tiles))):
                cols = lane_slice(v)
                if k == 0:
                    grad = dm[rows, cols] * u[rows, cols].astype(f32)
                else:
                    grad = gg[rows, cols] * conv[3 - k, rows, cols]
                rolled = [pltpu.roll(grad, LANES - j, 1) for j in range(1, KER)]
                if v >= prompt_tiles:
                    heads = heads + grad
                    following = [zero] * (KER - 1)
                else:
                    if after is None:
                        after = [pltpu.roll(heads, LANES - j, 1) for j in range(1, KER)]
                    following = after
                    after = rolled
                shifted = [grad] + [
                    jnp.where(lane < LANES - j, rolled[j - 1], following[j - 1])
                    for j in range(1, KER)
                ]
                value = proj[k, rows, cols].astype(f32)
                out = taps[0] * grad
                for j in range(1, KER):
                    out = out + taps[j] * shifted[j]
                low = out.astype(bf16)
                gz[k, rows, cols] = low
                total_bias = total_bias + grad
                total_out = total_out + low.astype(f32)
                total_taps = [t + value * s for t, s in zip(total_taps, shifted)]
            place_sum(rows, lane, BIAS_IN + k, total_out)
            place_sum(rows, lane, BIAS_CONV + k, total_bias)
            for j in range(KER):
                place_sum(rows, lane, KERNEL + KER * k + j, total_taps[j])


VMEM_SPEC = pl.BlockSpec(memory_space=pltpu.VMEM)


def call(kernel, ins, outs, scratch, flops, name, limit):
    nbytes = sum(math.prod(v.shape) * v.dtype.itemsize for v in list(ins) + list(outs))
    return pl.pallas_call(
        kernel,
        out_shape=tuple(outs),
        in_specs=[VMEM_SPEC] * len(ins),
        out_specs=tuple([VMEM_SPEC] * len(outs)),
        scratch_shapes=scratch,
        compiler_params=pltpu.CompilerParams(vmem_limit_bytes=limit << 20),
        cost_estimate=pl.CostEstimate(flops=flops, bytes_accessed=nbytes, transcendentals=0),
        name=name,
    )(*ins)


def mixer_fwd(normed, weight, chan, resp, table, inverse, sz):
    width = chan.shape[0]
    cols = normed.shape[1]
    parts = sz.blocks + sz.per
    outs = [
        jax.ShapeDtypeStruct((width, cols), bf16),
        jax.ShapeDtypeStruct((3, width, cols), bf16),
        jax.ShapeDtypeStruct((width, cols), bf16),
    ]
    scratch = [
        pltpu.VMEM((3, width, cols), f32),
        pltpu.VMEM((width, cols), bf16),
        pltpu.VMEM((parts, width, 2 * BLOCK), f32),
        pltpu.VMEM((parts, width, 2 * BLOCK), bf16),
    ]
    return call(
        partial(mixer_fwd_kernel, sz),
        (normed, weight, chan, resp, table, inverse),
        outs,
        scratch,
        8 * width * cols * normed.shape[0],
        "mixer_fwd",
        32,
    )


def mixer_bwd(branch, weight, proj, u, chan, resp, table, inverse, sz):
    width = chan.shape[0]
    cols = branch.shape[1]
    parts = sz.blocks + sz.per
    outs = [
        jax.ShapeDtypeStruct((3, width, cols), bf16),
        jax.ShapeDtypeStruct((width, (sz.blocks + 1) * BLOCK), f32),
        jax.ShapeDtypeStruct((width, LANES), f32),
    ]
    scratch = [
        pltpu.VMEM((width, cols), f32),
        pltpu.VMEM((3, width, cols), f32),
        pltpu.VMEM((width, cols), bf16),
        pltpu.VMEM((width, cols), bf16),
        pltpu.VMEM((parts, width, 2 * BLOCK), f32),
        pltpu.VMEM((parts, width, 2 * BLOCK), f32),
        pltpu.VMEM((parts + sz.blocks + 1, width, 2 * BLOCK), bf16),
        pltpu.VMEM((width, cols), f32),
    ]
    return call(
        partial(mixer_bwd_kernel, sz),
        (branch, weight, proj, u, chan, resp, table, inverse),
        outs,
        scratch,
        12 * width * cols * branch.shape[0],
        "mixer_bwd",
        40,
    )


def normalize(values):
    count = values.shape[0]
    center = jnp.sum(values, axis=0, keepdims=True) / count
    spread = jnp.sum(values * values, axis=0, keepdims=True) / count - center * center
    scale = lax.rsqrt(spread + epsilon)
    return ((values - center) * scale, scale)


def norm_backward(grad, normal, scale, gain):
    g = grad * gain
    count = g.shape[0]
    first = jnp.sum(g, axis=0, keepdims=True) / count
    second = jnp.sum(g * normal, axis=0, keepdims=True) / count
    return scale * (g - first - normal * second)


def gelu_parts(hidden):
    size = jnp.abs(hidden)
    bell = jnp.exp(-0.5 * hidden * hidden)
    part = 1.0 / (1.0 + (0.3275911 * math.sqrt(0.5)) * size)
    poly = 1.061405429
    for value in (-1.453152027, 1.421413741, -0.284496736, 0.254829592):
        poly = poly * part + value
    tail = 0.5 * poly * part * bell
    cdf = jnp.where(hidden < 0, tail, 1.0 - tail)
    slope = cdf + hidden * (bell * (1.0 / math.sqrt(2.0 * math.pi)))
    return lax.optimization_barrier(((hidden * cdf).astype(bf16), slope.astype(bf16)))


def swap(axis, count, bit):
    def run(values):
        return lax.ppermute(values, axis, [(i, i ^ bit) for i in range(count)])

    return run


over_y = swap("tensor", 4, 2)
over_c = swap("tensor", 4, 1)


def reduce_dp(values, count, index, first=1):
    bits = [1 << b for b in range(count.bit_length() - 1)]
    held = values
    for bit in bits:
        half = held.shape[0] // 2
        high = (index & bit) != 0
        low_part, high_part = held[:half], held[half:]
        give = jnp.where(high, low_part, high_part).astype(bf16)
        keep = jnp.where(high, high_part, low_part)
        held = keep + swap("dp", count, bit)(give).astype(f32)
    held = held.astype(bf16)
    for bit in reversed(bits):
        high = (index & bit) != 0
        other = swap("dp", count, bit)(held)
        held = jnp.where(
            high,
            jnp.concatenate([other, held], axis=0),
            jnp.concatenate([held, other], axis=0),
        )
    return held.astype(f32)


def reduce_small(values, count):
    bit = 1
    while bit < count:
        values = values + swap("dp", count, bit)(values)
        bit *= 2
    return values


def shards(dp_count, *args):
    (
        prompt_tokens,
        cont_tokens,
        group_map,
        cont_lengths,
        first_gain,
        first_bias,
        in_weight,
        in_bias,
        conv_kernel,
        conv_bias,
        embed_weight,
        embed_bias,
        inner_weight,
        inner_bias,
        sine_freq,
        filter_weight,
        decay_rate,
        skip_gain,
        out_weight,
        out_bias,
        second_gain,
        second_bias,
        up_weight,
        up_bias,
        down_weight,
        down_bias,
        prompt_cotan,
        cont_cotan,
    ) = args
    width = prompt_tokens.shape[1]
    sz = Sizes()
    sz.prompt = prompt_tokens.shape[2]
    sz.seq = sz.prompt + CONT
    sz.blocks = sz.prompt // BLOCK
    conts = cont_tokens.shape[0]
    sz.per = conts // GRP_DEV
    features = 4 * width
    t = lax.axis_index("tensor")
    y = t // 2
    dp = lax.axis_index("dp")
    table = jnp.asarray(block_table(), bf16)
    inverse = jnp.asarray(block_table().T / BLOCK, bf16)

    local = group_map % GRP_DEV
    ids = jnp.arange(conts, dtype=jnp.int32)
    before = (ids[None, :] < ids[:, None]) & (local[None, :] == local[:, None])
    slot = local * sz.per + jnp.sum(before.astype(jnp.int32), axis=1)
    order = jnp.sum(jnp.where(slot[None, :] == ids[:, None], ids[None, :], 0), axis=1)

    def pick(prompt, cont, group):
        parts = [lax.dynamic_index_in_dim(prompt, group, 0, False)]
        for i in range(sz.per):
            member = lax.dynamic_index_in_dim(order, group * sz.per + i, 0, False)
            parts.append(lax.dynamic_index_in_dim(cont, member, 0, False))
        return jnp.concatenate(parts, axis=1)

    def blocks_of(keep, send):
        got = over_y(send)
        return [keep, over_c(keep), got, over_c(got)]

    def place(parts):
        full = jnp.zeros((features,) + parts[0].shape[1:], parts[0].dtype)
        for r, part in enumerate(parts):
            full = lax.dynamic_update_slice(full, part, (width * (t ^ r), 0))
        return full

    lengths = jnp.stack(
        [
            lax.dynamic_index_in_dim(
                cont_lengths, lax.dynamic_index_in_dim(order, y * sz.per + i, 0, False), 0, False
            )
            for i in range(sz.per)
        ]
    )
    rows_count = sz.prompt + sz.per * CONT
    positions = jnp.arange(CONT, dtype=jnp.int32)
    live = jnp.concatenate(
        [
            jnp.ones((1, sz.prompt), f32),
            (positions[None, :] < lengths[:, None]).astype(f32).reshape(1, -1),
        ],
        axis=1,
    )

    rows = place(
        blocks_of(pick(prompt_tokens, cont_tokens, y), pick(prompt_tokens, cont_tokens, 1 - y))
    ).astype(f32)
    in_w = [in_weight, over_y(in_weight)]
    channel = jnp.concatenate(
        [
            in_bias,
            conv_kernel.reshape(KER * 3, width),
            conv_bias,
            skip_gain[None],
            decay_rate[None],
            filter_weight,
        ],
        axis=0,
    )
    channels = [channel, over_y(channel)]
    vectors = jnp.stack([first_gain, first_bias, out_bias, second_gain, second_bias, down_bias], 1)
    vectors = place(blocks_of(vectors, vectors))
    first_gain, first_bias, out_bias, second_gain, second_bias, down_bias = [
        vectors[:, i : i + 1] for i in range(6)
    ]
    up_b = [up_bias, over_y(up_bias)]
    out_w = [out_weight, over_y(out_weight)]
    up_w = [up_weight, over_y(up_weight)]
    down_w = [down_weight, over_y(down_weight)]
    grad_back = place(
        blocks_of(pick(prompt_cotan, cont_cotan, y), pick(prompt_cotan, cont_cotan, 1 - y))
    )
    grad_out = grad_back.astype(f32) * live
    grad_back = grad_out.astype(bf16)

    embed = jnp.asarray(embedding_table(sz.seq))
    filter_second, filter_pull = jax.vjp(
        partial(filter_hidden, embed), embed_weight, embed_bias, inner_weight, inner_bias, sine_freq
    )
    steps = jnp.arange(sz.seq, dtype=f32) / (sz.seq - 1)
    resp, envelope = [], []
    for b in range(2):
        decay, weight = channels[b][16], channels[b][17:]
        env = jnp.exp(-decay[:, None] * steps[None, :]) + 0.05
        response = (
            lax.dot_general(weight, filter_second, (((0,), (1,)), ((), ())), precision=highest)
            * env
        )
        padded = jnp.pad(response, ((0, 0), (0, (sz.blocks + 1) * BLOCK - sz.seq)))
        resp.append(
            jnp.stack(
                [
                    spectrum(padded[:, j * BLOCK : (j + 1) * BLOCK], table)
                    for j in range(sz.blocks + 1)
                ]
            )
        )
        envelope.append(env)

    normal_one, scale_one = normalize(rows)
    normed_one = (normal_one * first_gain + first_bias).astype(bf16)
    chans = [jnp.pad(value.T, ((0, 0), (0, LANES - value.shape[0]))) for value in channels]
    mixed, saved = [], []
    for b in range(2):
        part, proj, u = mixer_fwd(
            normed_one, in_w[b].reshape(3 * width, -1), chans[b], resp[b], table, inverse, sz
        )
        mixed.append(part)
        saved.append((proj, u))
    mixed_all = mixed + [over_c(part) for part in mixed]
    out_all = out_w + [over_c(part) for part in out_w]
    branch = jnp.einsum(
        "cd,cr->dr",
        jnp.concatenate(out_all, axis=0),
        jnp.concatenate(mixed_all, axis=0),
        preferred_element_type=f32,
    )
    resid = rows + branch + out_bias
    normal_two, scale_two = normalize(resid)
    normed_two = (normal_two * second_gain + second_bias).astype(bf16)
    final, two = 0.0, 0.0
    up_grad, down_grad, up_bias_grad = [], [], []
    for b in range(2):
        hidden = (
            jnp.einsum("df,dr->fr", up_w[b], normed_two, preferred_element_type=f32)
            + up_b[b][:, None]
        )
        active, slope = gelu_parts(hidden)
        final = final + jnp.einsum("fd,fr->dr", down_w[b], active, preferred_element_type=f32)
        grad_active = jnp.einsum("fd,dr->fr", down_w[b], grad_back, preferred_element_type=f32)
        grad_hidden = (grad_active * slope).astype(bf16)
        up_bias_grad.append(jnp.sum(grad_hidden, axis=1, dtype=f32))
        two = two + jnp.einsum("df,fr->dr", up_w[b], grad_hidden, preferred_element_type=f32)
        down_grad.append(
            jnp.einsum("fr,dr->fd", active, grad_back, preferred_element_type=f32)
        )
        up_grad.append(
            jnp.einsum("dr,fr->df", normed_two, grad_hidden, preferred_element_type=f32)
        )

    def mine(values, r):
        return lax.dynamic_slice_in_dim(values, width * (t ^ r), width, 0)

    passed = [over_c(mine(final, r).astype(bf16)) for r in (1, 3)]
    ends = []
    for got, r in zip(passed, (0, 2)):
        value = mine(resid, r) + mine(final, r) + got.astype(f32) + mine(down_bias, r)
        ends.append((value * live).astype(bf16))
    out_pair = [ends[0], over_y(ends[1])]

    down_bias_grad = jnp.sum(grad_back, axis=1, dtype=f32)
    two = two + 0.0
    grad_two = two + over_c(two.astype(bf16)).astype(f32)
    second_gain_grad = jnp.sum(grad_two * normal_two, axis=1)
    second_bias_grad = jnp.sum(grad_two, axis=1)
    resid_grad = grad_out + norm_backward(grad_two, normal_two, scale_two, second_gain)
    grad_branch = resid_grad.astype(bf16)
    out_bias_grad = jnp.sum(grad_branch, axis=1, dtype=f32)
    out_grad, in_grad, chan_grads, second_grads, pieces = [], [], [], 0.0, 0.0
    for b in range(2):
        proj, u = saved[b]
        out_grad.append(
            jnp.einsum("cr,dr->cd", mixed[b], grad_branch, preferred_element_type=f32)
        )
        gz, resp_grad, sums = mixer_bwd(
            grad_branch, out_w[b], proj, u, chans[b], resp[b], table, inverse, sz
        )
        resp_grad = resp_grad[:, : sz.seq]
        grad_raw = resp_grad * envelope[b]
        weight = channels[b][17:]
        weight_grad = lax.dot_general(
            filter_second, grad_raw, (((0,), (1,)), ((), ())), precision=highest
        )
        second_grads = second_grads + lax.dot_general(
            grad_raw, weight, (((0,), (1,)), ((), ())), precision=highest
        )
        chan_grads.append(jnp.concatenate([sums.T[:DECAY], weight_grad], axis=0))
        in_grad.append(
            jnp.einsum("ker,dr->ked", gz, normed_one, preferred_element_type=f32)
        )
        pieces = pieces + jnp.einsum("ked,ker->dr", in_w[b], gz, preferred_element_type=f32)
    grad_one = pieces + over_c(pieces.astype(bf16)).astype(f32)
    first_gain_grad = jnp.sum(grad_one * normal_one, axis=1)
    first_bias_grad = jnp.sum(grad_one, axis=1)
    input_grad = resid_grad + norm_backward(grad_one, normal_one, scale_one, first_gain)
    grad_pair = [mine(input_grad, 0), over_y(mine(input_grad, 2).astype(bf16)).astype(f32)]

    def join(pair):
        return pair[0] + over_y(pair[1].astype(bf16)).astype(f32)

    def reduced(pair):
        value = join(pair)
        flat = value.reshape(-1, features)
        return reduce_dp(flat, dp_count, dp).reshape(value.shape)

    down_weight_grad = reduced(down_grad)
    up_weight_grad = reduced(up_grad)
    out_weight_grad = reduced(out_grad)
    in_weight_grad = reduced(in_grad)

    vector_grads = jnp.stack(
        [
            first_gain_grad,
            first_bias_grad,
            out_bias_grad,
            second_gain_grad,
            second_bias_grad,
            down_bias_grad,
        ],
        axis=1,
    )
    vector_sum = mine(vector_grads, 0) + over_y(mine(vector_grads, 2))
    chan_sum = chan_grads[0] + over_y(chan_grads[1])
    up_bias_sum = up_bias_grad[0] + over_y(up_bias_grad[1])
    filter_grads = filter_pull(second_grads)
    filter_flat = jnp.concatenate([value.reshape(-1) for value in filter_grads])
    filter_flat = filter_flat + over_c(filter_flat)
    filter_flat = filter_flat + over_y(filter_flat)
    packed = jnp.concatenate(
        [vector_sum.reshape(-1), chan_sum.reshape(-1), up_bias_sum, filter_flat]
    )
    packed = reduce_small(packed, dp_count)
    sizes = [vector_sum.size, chan_sum.size, up_bias_sum.size]
    marks = np.cumsum(sizes)
    vector_sum = packed[: marks[0]].reshape(vector_sum.shape)
    chan_sum = packed[marks[0] : marks[1]].reshape(chan_sum.shape)
    up_bias_sum = packed[marks[1] : marks[2]]
    rest = packed[marks[2] :]
    filter_out = []
    at = 0
    for value in filter_grads:
        filter_out.append(rest[at : at + value.size].reshape(value.shape))
        at += value.size

    def unpack(pair):
        prompts = jnp.stack([value[:, : sz.prompt] for value in pair])
        prompts = jnp.stack(
            [lax.dynamic_index_in_dim(prompts, g ^ y, 0, False) for g in range(GRP_DEV)]
        )
        pool = jnp.concatenate(
            [
                jnp.transpose(value[:, sz.prompt :].reshape(width, sz.per, CONT), (1, 0, 2))
                for value in pair
            ],
            axis=0,
        )
        rel = slot ^ (sz.per * y)
        return (prompts, jnp.take(pool, rel, axis=0, mode="clip"))

    prompt_out, cont_out = unpack(out_pair)
    prompt_grad, cont_grad = unpack(grad_pair)
    return (
        prompt_out,
        cont_out,
        prompt_grad,
        cont_grad,
        vector_sum[:, 0],
        vector_sum[:, 1],
        in_weight_grad,
        chan_sum[:3],
        chan_sum[3:12].reshape(3, KER, width),
        chan_sum[12:15],
        filter_out[0],
        filter_out[1],
        filter_out[2],
        filter_out[3],
        filter_out[4],
        chan_sum[16:],
        chan_sum[15],
        out_weight_grad,
        vector_sum[:, 2],
        vector_sum[:, 3],
        vector_sum[:, 4],
        up_weight_grad,
        up_bias_sum,
        down_weight_grad,
        vector_sum[:, 5],
    )


def solution(mesh):
    placed = (
        P("dp", "tensor", None),
        P("dp", "tensor", None),
        P("dp"),
        P("dp"),
        P("tensor"),
        P("tensor"),
        P(None, "tensor", None),
        P(None, "tensor"),
        P(None, None, "tensor"),
        P(None, "tensor"),
        P(),
        P(),
        P(),
        P(),
        P(),
        P(None, "tensor"),
        P("tensor"),
        P("tensor"),
        P("tensor", None),
        P("tensor"),
        P("tensor"),
        P("tensor"),
        P(None, "tensor"),
        P("tensor"),
        P("tensor", None),
        P("tensor"),
        P("dp", "tensor", None),
        P("dp", "tensor", None),
    )
    return jax.shard_map(
        partial(shards, mesh.shape["dp"]),
        mesh=mesh,
        in_specs=placed,
        out_specs=(
            P("dp", "tensor", None),
            P("dp", "tensor", None),
            P("dp", "tensor", None),
            P("dp", "tensor", None),
            P("tensor"),
            P("tensor"),
            P(None, "tensor", None),
            P(None, "tensor"),
            P(None, None, "tensor"),
            P(None, "tensor"),
            P(),
            P(),
            P(),
            P(),
            P(),
            P(None, "tensor"),
            P("tensor"),
            P("tensor", None),
            P("tensor"),
            P("tensor"),
            P("tensor"),
            P(None, "tensor"),
            P("tensor"),
            P("tensor", None),
            P("tensor"),
        ),
        check_vma=False,
    )
```

```python
from functools import partial
import math

import jax
import jax.numpy as jnp
import numpy as np
from jax import lax
from jax.experimental import pallas as pl
from jax.experimental.pallas import tpu as pltpu
from jax.sharding import PartitionSpec as P

EMB = 33
KER = 3
CONT = 128
GRP_DEV = 2
BLOCK = 256

epsilon = 1e-05
highest = lax.Precision.HIGHEST
f32 = jnp.float32
bf16 = jnp.bfloat16


def high_dot(left, right):
    return jnp.dot(left, right, precision=highest)


def embedding_table(length):
    steps = np.arange(length, dtype=np.float32)
    bands = (EMB - 1) // 2
    freqs = np.linspace(0.0001, bands - 1, bands, dtype=np.float32)
    angle = np.float32(2.0 * math.pi) * steps[:, None] * freqs[None, :] / np.float32(length)
    return np.concatenate(
        [steps[:, None] / np.float32(length - 1), np.cos(angle), -np.sin(angle)], axis=1
    ).astype(np.float32)


def filter_hidden(embed, embed_weight, embed_bias, inner_weight, inner_bias, sine_freq):
    first = jnp.sin(sine_freq * (high_dot(embed, embed_weight) + embed_bias))
    return jnp.sin(sine_freq * (high_dot(first, inner_weight) + inner_bias))


def block_table():
    steps = np.arange(BLOCK)
    angle = 2.0 * math.pi / BLOCK * (steps[:, None] * (steps[None, :] + 0.25))
    return np.concatenate([np.cos(angle), -np.sin(angle)], axis=1)


def spectrum(values, table):
    return jnp.dot(values.astype(bf16), table, preferred_element_type=f32)


class Sizes:
    pass


LANES = 128
ROWS = 16
BIAS_IN, KERNEL, BIAS_CONV, SKIP, DECAY, FILTER = 0, 3, 12, 15, 16, 17


def cmul(a, b):
    return (a[0] * b[0] - a[1] * b[1], a[0] * b[1] + a[1] * b[0])


def cmul_conj(a, b):
    return (a[0] * b[0] + a[1] * b[1], a[1] * b[0] - a[0] * b[1])


def cadd(items):
    result = items[0]
    for item in items[1:]:
        result = (result[0] + item[0], result[1] + item[1])
    return result


def plus_i(a, b):
    return (a[0] - b[1], a[1] + b[0])


def minus_i(a, b):
    return (a[0] + b[1], a[1] - b[0])


def lane_slice(v):
    return slice(v * LANES, (v + 1) * LANES)


def column(chan, rows, at):
    return jnp.broadcast_to(chan[rows, at : at + 1], (ROWS, LANES))


def conv_stream(load, chan, rows, k, lane, prompt_tiles, tiles):
    bias = column(chan, rows, BIAS_CONV + k)
    taps = [column(chan, rows, KERNEL + KER * k + j) for j in range(KER)]
    before = [jnp.zeros((ROWS, LANES), f32)] * (KER - 1)
    last = None
    for v in range(tiles):
        value = load(k, v)
        rolled = [pltpu.roll(value, j, 1) for j in range(1, KER)]
        result = bias + taps[0] * value
        history = before if v < prompt_tiles else last
        for j in range(1, KER):
            result = result + taps[j] * jnp.where(lane < j, history[j - 1], rolled[j - 1])
        if v < prompt_tiles:
            before = rolled
            last = rolled
        yield v, value, result


def block_parts(sz):
    parts = [(slice(i * BLOCK, (i + 1) * BLOCK), BLOCK) for i in range(sz.blocks)]
    start = sz.prompt
    parts += [(slice(start + n * CONT, start + (n + 1) * CONT), CONT) for n in range(sz.per)]
    return parts


def freq_pair(ref, index, rows, tile):
    real = ref[index, rows, lane_slice(tile)]
    imag = ref[index, rows, lane_slice(tile + BLOCK // LANES)]
    return (real, imag)


def store_pair(ref, index, rows, tile, pair):
    ref[index, rows, lane_slice(tile)] = pair[0].astype(ref.dtype)
    ref[index, rows, lane_slice(tile + BLOCK // LANES)] = pair[1].astype(ref.dtype)


def mixer_fwd_kernel(
    sz, normed, weight, chan, resp, table, inverse, mixed, proj, u, z, gb, spec, prod
):
    width = chan.shape[0]
    tiles = normed.shape[1] // LANES
    prompt_tiles = sz.prompt // LANES
    parts = block_parts(sz)
    n = sz.blocks

    @pl.loop(0, normed.shape[1] // BLOCK)
    def _(i):
        cols = pl.ds(pl.multiple_of(i * BLOCK, BLOCK), BLOCK)
        got = jnp.dot(weight[: 3 * width, :], normed[:, cols], preferred_element_type=f32)
        for k in range(3):
            z[k, :, cols] = got[k * width : (k + 1) * width]

    @pl.loop(0, width // ROWS)
    def _(c):
        rows = pl.ds(pl.multiple_of(c * ROWS, ROWS), ROWS)
        lane = lax.broadcasted_iota(jnp.int32, (ROWS, LANES), 1)
        biases = [column(chan, rows, BIAS_IN + k) for k in range(3)]

        def load(k, v):
            return z[k, rows, lane_slice(v)] + biases[k]

        streams = [conv_stream(load, chan, rows, k, lane, prompt_tiles, tiles) for k in range(3)]
        for first, second, third in zip(*streams):
            v = first[0]
            for k, item in enumerate((first, second, third)):
                proj[k, rows, lane_slice(v)] = item[1].astype(bf16)
            gated = second[2] * third[2]
            z[0, rows, lane_slice(v)] = first[2]
            z[1, rows, lane_slice(v)] = gated
            gb[rows, lane_slice(v)] = gated.astype(bf16)

    for i, (cols, length) in enumerate(parts):
        spec[i] = jnp.dot(gb[:, cols], table[:length, :], preferred_element_type=f32)

    @pl.loop(0, width // ROWS)
    def _(c):
        rows = pl.ds(pl.multiple_of(c * ROWS, ROWS), ROWS)
        for tile in range(BLOCK // LANES):
            xs = [freq_pair(spec, i, rows, tile) for i in range(n)]
            hs = [freq_pair(resp, j, rows, tile) for j in range(n + 1)]
            prior = None
            for m in range(n + 1):
                now = cadd([cmul(xs[i], hs[m - i]) for i in range(n) if 0 <= m - i <= n])
                out = now if prior is None else plus_i(now, prior)
                prior = now
                if m < n:
                    store_pair(prod, m, rows, tile, out)
            for q in range(sz.per):
                own = cmul(freq_pair(spec, n + q, rows, tile), hs[0])
                store_pair(prod, n + q, rows, tile, cadd([own, out]))

    skip = chan[:, SKIP : SKIP + 1]
    for i, (cols, length) in enumerate(parts):
        value = jnp.dot(prod[i], inverse[:, :length], preferred_element_type=f32)
        value = value + skip * z[1, :, cols]
        u[:, cols] = value.astype(bf16)
        mixed[:, cols] = (value * z[0, :, cols]).astype(bf16)


def mixer_bwd_kernel(
    sz,
    branch,
    weight,
    proj,
    u,
    chan,
    resp,
    table,
    inverse,
    gz,
    resp_grad,
    sums,
    dm,
    conv,
    gb,
    lb,
    gspec,
    xspec,
    prod,
    gg,
):
    width = chan.shape[0]
    tiles = branch.shape[1] // LANES
    prompt_tiles = sz.prompt // LANES
    parts = block_parts(sz)
    n = sz.blocks

    @pl.loop(0, branch.shape[1] // BLOCK)
    def _(i):
        cols = pl.ds(pl.multiple_of(i * BLOCK, BLOCK), BLOCK)
        dm[:, cols] = jnp.dot(
            weight[3 * width :, :], branch[:, cols], preferred_element_type=f32
        )

    def place_sum(rows, lane, at, value):
        total = jnp.sum(value, axis=1, keepdims=True)
        sums[rows, :] = jnp.where(lane == at, total, sums[rows, :])

    @pl.loop(0, width // ROWS)
    def _(c):
        rows = pl.ds(pl.multiple_of(c * ROWS, ROWS), ROWS)
        lane = lax.broadcasted_iota(jnp.int32, (ROWS, LANES), 1)

        def load(k, v):
            return proj[k, rows, lane_slice(v)].astype(f32)

        streams = [conv_stream(load, chan, rows, k, lane, prompt_tiles, tiles) for k in range(3)]
        skips = jnp.zeros((ROWS, LANES), f32)
        for first, second, third in zip(*streams):
            v = first[0]
            for k, item in enumerate((first, second, third)):
                conv[k, rows, lane_slice(v)] = item[2]
            gated = second[2] * third[2]
            long = dm[rows, lane_slice(v)] * first[2]
            skips = skips + long * gated
            gb[rows, lane_slice(v)] = gated.astype(bf16)
            lb[rows, lane_slice(v)] = long.astype(bf16)
        sums[rows, :] = jnp.zeros((ROWS, LANES), f32)
        place_sum(rows, lane, SKIP, skips)

    for i, (cols, length) in enumerate(parts):
        gspec[i] = jnp.dot(lb[:, cols], table[:length, :], preferred_element_type=f32)
        xspec[i] = jnp.dot(gb[:, cols], table[:length, :], preferred_element_type=f32)

    @pl.loop(0, width // ROWS)
    def _(c):
        rows = pl.ds(pl.multiple_of(c * ROWS, ROWS), ROWS)
        for tile in range(BLOCK // LANES):
            gs = [freq_pair(gspec, i, rows, tile) for i in range(n)]
            hs = [freq_pair(resp, j, rows, tile) for j in range(n + 1)]
            own, lags = [], []
            for q in range(sz.per):
                g = freq_pair(gspec, n + q, rows, tile)
                own.append(g)
                store_pair(prod, n + q, rows, tile, cmul_conj(g, hs[0]))
                lags.append(cmul_conj(g, freq_pair(xspec, n + q, rows, tile)))
            gs.append(cadd(own))
            after = cmul_conj(gs[n], hs[0])
            for i in reversed(range(n)):
                now = cadd([cmul_conj(gs[m], hs[m - i]) for m in range(i, n + 1)])
                store_pair(prod, i, rows, tile, minus_i(now, after))
                after = now
            xs = [freq_pair(xspec, i, rows, tile) for i in range(n)]
            after = None
            for j in reversed(range(n + 1)):
                items = [cmul_conj(gs[m], xs[m - j]) for m in range(j, n + 1) if m - j < n]
                now = cadd(items + (lags if j == 0 else []))
                out = now if after is None else minus_i(now, after)
                store_pair(prod, n + sz.per + j, rows, tile, out)
                after = now

    skip = chan[:, SKIP : SKIP + 1]
    for i, (cols, length) in enumerate(parts):
        value = jnp.dot(prod[i], inverse[:, :length], preferred_element_type=f32)
        gg[:, cols] = value + skip * (dm[:, cols] * conv[0, :, cols])
    for j in range(n + 1):
        resp_grad[:, j * BLOCK : (j + 1) * BLOCK] = jnp.dot(
            prod[n + sz.per + j], inverse[...], preferred_element_type=f32
        )

    @pl.loop(0, width // ROWS)
    def _(c):
        rows = pl.ds(pl.multiple_of(c * ROWS, ROWS), ROWS)
        lane = lax.broadcasted_iota(jnp.int32, (ROWS, LANES), 1)
        zero = jnp.zeros((ROWS, LANES), f32)
        for k in range(3):
            taps = [column(chan, rows, KERNEL + KER * k + j) for j in range(KER)]
            total_bias, total_out = zero, zero
            total_taps = [zero] * KER
            heads = zero
            after = None
            for v in list(range(prompt_tiles, tiles)) + list(reversed(range(prompt_tiles))):
                cols = lane_slice(v)
                if k == 0:
                    grad = dm[rows, cols] * u[rows, cols].astype(f32)
                else:
                    grad = gg[rows, cols] * conv[3 - k, rows, cols]
                rolled = [pltpu.roll(grad, LANES - j, 1) for j in range(1, KER)]
                if v >= prompt_tiles:
                    heads = heads + grad
                    following = [zero] * (KER - 1)
                else:
                    if after is None:
                        after = [pltpu.roll(heads, LANES - j, 1) for j in range(1, KER)]
                    following = after
                    after = rolled
                shifted = [grad] + [
                    jnp.where(lane < LANES - j, rolled[j - 1], following[j - 1])
                    for j in range(1, KER)
                ]
                value = proj[k, rows, cols].astype(f32)
                out = taps[0] * grad
                for j in range(1, KER):
                    out = out + taps[j] * shifted[j]
                low = out.astype(bf16)
                gz[k, rows, cols] = low
                total_bias = total_bias + grad
                total_out = total_out + low.astype(f32)
                total_taps = [t + value * s for t, s in zip(total_taps, shifted)]
            place_sum(rows, lane, BIAS_IN + k, total_out)
            place_sum(rows, lane, BIAS_CONV + k, total_bias)
            for j in range(KER):
                place_sum(rows, lane, KERNEL + KER * k + j, total_taps[j])


VMEM_SPEC = pl.BlockSpec(memory_space=pltpu.VMEM)


SMEM_SPEC = pl.BlockSpec(memory_space=pltpu.SMEM)


def call(kernel, ins, outs, scratch, flops, name, limit, scalars=0):
    nbytes = sum(math.prod(v.shape) * v.dtype.itemsize for v in list(ins) + list(outs))
    return pl.pallas_call(
        kernel,
        out_shape=tuple(outs),
        in_specs=[SMEM_SPEC] * scalars + [VMEM_SPEC] * (len(ins) - scalars),
        out_specs=tuple([VMEM_SPEC] * len(outs)),
        scratch_shapes=scratch,
        compiler_params=pltpu.CompilerParams(vmem_limit_bytes=limit << 20),
        cost_estimate=pl.CostEstimate(flops=flops, bytes_accessed=nbytes, transcendentals=0),
        name=name,
    )(*ins)


def mixer_fwd(normed, weight, chan, resp, table, inverse, sz):
    width = chan.shape[0]
    cols = normed.shape[1]
    parts = sz.blocks + sz.per
    outs = [
        jax.ShapeDtypeStruct((width, cols), bf16),
        jax.ShapeDtypeStruct((3, width, cols), bf16),
        jax.ShapeDtypeStruct((width, cols), bf16),
    ]
    scratch = [
        pltpu.VMEM((3, width, cols), f32),
        pltpu.VMEM((width, cols), bf16),
        pltpu.VMEM((parts, width, 2 * BLOCK), f32),
        pltpu.VMEM((parts, width, 2 * BLOCK), bf16),
    ]
    return call(
        partial(mixer_fwd_kernel, sz),
        (normed, weight, chan, resp, table, inverse),
        outs,
        scratch,
        8 * width * cols * normed.shape[0],
        "mixer_fwd",
        32,
    )


def mixer_bwd(branch, weight, proj, u, chan, resp, table, inverse, sz):
    width = chan.shape[0]
    cols = branch.shape[1]
    parts = sz.blocks + sz.per
    outs = [
        jax.ShapeDtypeStruct((3, width, cols), bf16),
        jax.ShapeDtypeStruct((width, (sz.blocks + 1) * BLOCK), f32),
        jax.ShapeDtypeStruct((width, LANES), f32),
    ]
    scratch = [
        pltpu.VMEM((width, cols), f32),
        pltpu.VMEM((3, width, cols), f32),
        pltpu.VMEM((width, cols), bf16),
        pltpu.VMEM((width, cols), bf16),
        pltpu.VMEM((parts, width, 2 * BLOCK), f32),
        pltpu.VMEM((parts, width, 2 * BLOCK), f32),
        pltpu.VMEM((parts + sz.blocks + 1, width, 2 * BLOCK), bf16),
        pltpu.VMEM((width, cols), f32),
    ]
    return call(
        partial(mixer_bwd_kernel, sz),
        (branch, weight, proj, u, chan, resp, table, inverse),
        outs,
        scratch,
        12 * width * cols * branch.shape[0],
        "mixer_bwd",
        40,
    )


def each_cont(sz, group_map, run):
    y = lax.axis_index("tensor") // 2
    used = [jnp.int32(0), jnp.int32(0)]
    for c in range(sz.per * GRP_DEV):
        local = lax.rem(group_map[c], GRP_DEV)
        rank = jnp.minimum(jnp.where(local == 0, used[0], used[1]), sz.per - 1)
        used = [used[g] + (local == g).astype(jnp.int32) for g in range(GRP_DEV)]
        cols = pl.ds(pl.multiple_of(sz.prompt + rank * CONT, CONT), CONT)
        run(c, local == y, cols)
    return y


def pick_kernel(sz, group_map, lengths, prompt, cont, keep, send, live):
    live[...] = jnp.ones(live.shape, f32)

    def run(c, own, cols):
        @pl.when(own)
        def _():
            keep[:, cols] = cont[c]
            place = lax.broadcasted_iota(jnp.int32, (8, CONT), 1)
            live[:, cols] = jnp.where(place < lengths[c], 1.0, 0.0)

        @pl.when(jnp.logical_not(own))
        def _():
            send[:, cols] = cont[c]

    y = each_cont(sz, group_map, run)
    keep[:, : sz.prompt] = prompt[y]
    send[:, : sz.prompt] = prompt[1 - y]


def pick(group_map, lengths, prompt, cont, sz):
    shape = (prompt.shape[1], sz.prompt + sz.per * CONT)
    outs = [jax.ShapeDtypeStruct(shape, bf16)] * 2
    outs.append(jax.ShapeDtypeStruct((8, shape[1]), f32))
    ins = (group_map, lengths, prompt, cont)
    return call(partial(pick_kernel, sz), ins, outs, [], 0, "pick", 16, 2)


def unpack_kernel(sz, group_map, own, other, prompts, conts):
    kind = prompts.dtype

    def run(c, here, cols):
        @pl.when(here)
        def _():
            conts[c] = own[:, cols].astype(kind)

        @pl.when(jnp.logical_not(here))
        def _():
            conts[c] = other[:, cols].astype(kind)

    y = each_cont(sz, group_map, run)
    prompts[y] = own[:, : sz.prompt].astype(kind)
    prompts[1 - y] = other[:, : sz.prompt].astype(kind)


def unpack(group_map, own, other, sz):
    width = own.shape[0]
    outs = [
        jax.ShapeDtypeStruct((GRP_DEV, width, sz.prompt), own.dtype),
        jax.ShapeDtypeStruct((GRP_DEV * sz.per, width, CONT), own.dtype),
    ]
    ins = (group_map, own, other)
    return call(partial(unpack_kernel, sz), ins, outs, [], 0, "unpack", 24, 1)


def feature_rows(width, r):
    place = lax.axis_index("tensor") ^ r
    return pl.ds(pl.multiple_of(place * width, 64), width)


def norm_one_kernel(width, first, second, third, fourth, vectors, rows, normed, stats):
    parts = (first, second, third, fourth)
    count = len(parts) * width
    total, square = 0.0, 0.0
    for part in parts:
        value = part[...].astype(f32)
        total = total + jnp.sum(value, axis=0, keepdims=True)
        square = square + jnp.sum(value * value, axis=0, keepdims=True)
    center = total / count
    scale = lax.rsqrt(square / count - center * center + epsilon)
    for r, part in enumerate(parts):
        at = feature_rows(width, r)
        value = (part[...].astype(f32) - center) * scale
        rows[at, :] = part[...]
        normed[at, :] = (value * vectors[at, 0:1] + vectors[at, 1:2]).astype(bf16)
    stats[...] = jnp.concatenate(
        [jnp.broadcast_to(v, (8, v.shape[1])) for v in (center, scale)], axis=0
    )


def grad_kernel(width, first, second, third, fourth, live, grad):
    for r, part in enumerate((first, second, third, fourth)):
        value = part[...].astype(f32) * live[0:1, :]
        grad[feature_rows(width, r), :] = value.astype(bf16)


def by_columns(kernel, ins, outs, name):
    count = outs[0].shape[1]

    def spec(v):
        if v.shape[1] == count:
            return pl.BlockSpec((v.shape[0], BLOCK), lambda i: (0, i))
        return pl.BlockSpec(v.shape, lambda i: (0, 0))

    nbytes = sum(math.prod(v.shape) * v.dtype.itemsize for v in list(ins) + list(outs))
    return pl.pallas_call(
        kernel,
        grid=(count // BLOCK,),
        out_shape=tuple(outs),
        in_specs=[spec(v) for v in ins],
        out_specs=tuple(spec(v) for v in outs),
        compiler_params=pltpu.CompilerParams(vmem_limit_bytes=24 << 20),
        cost_estimate=pl.CostEstimate(flops=0, bytes_accessed=nbytes, transcendentals=0),
        name=name,
    )(*ins)


def normalize(values):
    count = values.shape[0]
    center = jnp.sum(values, axis=0, keepdims=True) / count
    spread = jnp.sum(values * values, axis=0, keepdims=True) / count - center * center
    scale = lax.rsqrt(spread + epsilon)
    return ((values - center) * scale, scale)


def norm_backward(grad, normal, scale, gain):
    g = grad * gain
    count = g.shape[0]
    first = jnp.sum(g, axis=0, keepdims=True) / count
    second = jnp.sum(g * normal, axis=0, keepdims=True) / count
    return scale * (g - first - normal * second)


def gelu_parts(hidden):
    size = jnp.abs(hidden)
    bell = jnp.exp(-0.5 * hidden * hidden)
    part = 1.0 / (1.0 + (0.3275911 * math.sqrt(0.5)) * size)
    poly = 1.061405429
    for value in (-1.453152027, 1.421413741, -0.284496736, 0.254829592):
        poly = poly * part + value
    tail = 0.5 * poly * part * bell
    cdf = jnp.where(hidden < 0, tail, 1.0 - tail)
    slope = cdf + hidden * (bell * (1.0 / math.sqrt(2.0 * math.pi)))
    return lax.optimization_barrier(((hidden * cdf).astype(bf16), slope.astype(bf16)))


def after(value, *others):
    return lax.optimization_barrier((value,) + others)[0]


def swap(axis, count, bit):
    def run(values):
        return lax.ppermute(values, axis, [(i, i ^ bit) for i in range(count)])

    return run


over_y = swap("tensor", 4, 2)
over_c = swap("tensor", 4, 1)


def reduce_dp(values, count, index, holds):
    bits = [1 << b for b in range(count.bit_length() - 1)]
    holds = list(holds)

    def arrived(value):
        return after(value, holds.pop(0)) if holds else value

    held = values
    for bit in bits:
        half = held.shape[0] // 2
        high = (index & bit) != 0
        low_part, high_part = held[:half], held[half:]
        give = jnp.where(high, low_part, high_part).astype(bf16)
        keep = jnp.where(high, high_part, low_part)
        held = keep + arrived(swap("dp", count, bit)(give)).astype(f32)
    held = held.astype(bf16)
    for bit in reversed(bits):
        high = (index & bit) != 0
        other = swap("dp", count, bit)(held)
        held = jnp.where(
            high,
            jnp.concatenate([other, held], axis=0),
            jnp.concatenate([held, other], axis=0),
        )
    return held.astype(f32)


def reduce_small(values, count):
    bit = 1
    while bit < count:
        values = values + swap("dp", count, bit)(values)
        bit *= 2
    return values


def shards(dp_count, *args):
    (
        prompt_tokens,
        cont_tokens,
        group_map,
        cont_lengths,
        first_gain,
        first_bias,
        in_weight,
        in_bias,
        conv_kernel,
        conv_bias,
        embed_weight,
        embed_bias,
        inner_weight,
        inner_bias,
        sine_freq,
        filter_weight,
        decay_rate,
        skip_gain,
        out_weight,
        out_bias,
        second_gain,
        second_bias,
        up_weight,
        up_bias,
        down_weight,
        down_bias,
        prompt_cotan,
        cont_cotan,
    ) = args
    width = prompt_tokens.shape[1]
    sz = Sizes()
    sz.prompt = prompt_tokens.shape[2]
    sz.seq = sz.prompt + CONT
    sz.blocks = sz.prompt // BLOCK
    conts = cont_tokens.shape[0]
    sz.per = conts // GRP_DEV
    features = 4 * width
    t = lax.axis_index("tensor")
    y = t // 2
    dp = lax.axis_index("dp")
    table = jnp.asarray(block_table(), bf16)
    inverse = jnp.asarray(block_table().T / BLOCK, bf16)

    def place(parts):
        full = jnp.zeros((features,) + parts[0].shape[1:], parts[0].dtype)
        for r, part in enumerate(parts):
            full = lax.dynamic_update_slice(full, part, (width * (t ^ r), 0))
        return full

    over_x = swap("dp", dp_count, 1)
    x = dp % 2
    vectors = jnp.stack([first_gain, first_bias, out_bias, second_gain, second_bias, down_bias], 1)
    there = over_y(vectors)
    vectors = place([vectors, over_c(vectors), there, over_c(there)])
    channel = jnp.concatenate(
        [
            in_bias,
            conv_kernel.reshape(KER * 3, width),
            conv_bias,
            skip_gain[None],
            decay_rate[None],
            filter_weight,
        ],
        axis=0,
    )
    channels = [channel, over_y(channel)]
    first_gain, first_bias, out_bias, second_gain, second_bias, down_bias = [
        vectors[:, i : i + 1] for i in range(6)
    ]
    up_b = [up_bias, over_y(up_bias)]

    def fetch(weight, *others):
        half = weight.shape[0] // 2
        part = lax.dynamic_slice_in_dim(weight, x * half, half, 0)
        got = over_y(after(part, *others))
        other = over_x(got)
        full = jnp.where(
            x != 0,
            jnp.concatenate([other, got], axis=0),
            jnp.concatenate([got, other], axis=0),
        )
        return full, got

    keep, send, live = pick(group_map, cont_lengths, prompt_tokens, cont_tokens, sz)
    got = over_y(send)
    near = over_c(keep)
    token_blocks = [keep, near, got, over_c(got)]
    mix_own = jnp.concatenate([in_weight.reshape(3 * width, features), out_weight], axis=0)
    mix_other, mix_half = fetch(mix_own, near)
    mix_w = [mix_own, mix_other]
    keep_grad, send_grad, _ = pick(group_map, cont_lengths, prompt_cotan, cont_cotan, sz)
    got_grad = over_y(after(send_grad, got))
    grad_blocks = [keep_grad, over_c(after(keep_grad, got)), got_grad, over_c(got_grad)]
    up_other, up_half = fetch(up_weight, mix_half)
    down_other, _ = fetch(down_weight, got_grad)
    up_w = [up_weight, up_other]
    down_w = [down_weight, down_other]
    out_w = [weight[3 * width :] for weight in mix_w]
    rows, normed_one, stats = by_columns(
        partial(norm_one_kernel, width),
        (*token_blocks, vectors),
        [
            jax.ShapeDtypeStruct((features, keep.shape[1]), bf16),
            jax.ShapeDtypeStruct((features, keep.shape[1]), bf16),
            jax.ShapeDtypeStruct((16, keep.shape[1]), f32),
        ],
        "norm_one",
    )
    (grad_back,) = by_columns(
        partial(grad_kernel, width),
        (*grad_blocks, live),
        [jax.ShapeDtypeStruct((features, keep.shape[1]), bf16)],
        "place_grad",
    )
    live = live[0:1]

    embed = jnp.asarray(embedding_table(sz.seq))
    filter_second, filter_pull = jax.vjp(
        partial(filter_hidden, embed), embed_weight, embed_bias, inner_weight, inner_bias, sine_freq
    )
    steps = jnp.arange(sz.seq, dtype=f32) / (sz.seq - 1)
    resp, envelope = [], []
    for b in range(2):
        decay, weight = channels[b][16], channels[b][17:]
        env = jnp.exp(-decay[:, None] * steps[None, :]) + 0.05
        response = (
            lax.dot_general(weight, filter_second, (((0,), (1,)), ((), ())), precision=highest)
            * env
        )
        padded = jnp.pad(response, ((0, 0), (0, (sz.blocks + 1) * BLOCK - sz.seq)))
        resp.append(
            jnp.stack(
                [
                    spectrum(padded[:, j * BLOCK : (j + 1) * BLOCK], table)
                    for j in range(sz.blocks + 1)
                ]
            )
        )
        envelope.append(env)

    chans = [jnp.pad(value.T, ((0, 0), (0, LANES - value.shape[0]))) for value in channels]
    mixed, saved = [], []
    for b in range(2):
        part, proj, u = mixer_fwd(
            normed_one, mix_w[b], chans[b], resp[b], table, inverse, sz
        )
        mixed.append(part)
        saved.append((proj, u))
    mixed_all = mixed + [over_c(part) for part in mixed]
    out_near = over_c(jnp.concatenate(out_w, axis=0))
    branch = jnp.einsum(
        "cd,cr->dr",
        jnp.concatenate([*out_w, out_near], axis=0),
        jnp.concatenate(mixed_all, axis=0),
        preferred_element_type=f32,
    )
    resid = rows.astype(f32) + branch + out_bias
    normal_two, scale_two = normalize(resid)
    normed_two = (normal_two * second_gain + second_bias).astype(bf16)
    final, two = 0.0, 0.0
    up_grad, down_grad, up_bias_grad = [], [], []
    for b in range(2):
        hidden = (
            jnp.einsum("df,dr->fr", up_w[b], normed_two, preferred_element_type=f32)
            + up_b[b][:, None]
        )
        active, slope = gelu_parts(hidden)
        final = final + jnp.einsum("fd,fr->dr", down_w[b], active, preferred_element_type=f32)
        grad_active = jnp.einsum("fd,dr->fr", down_w[b], grad_back, preferred_element_type=f32)
        grad_hidden = (grad_active * slope).astype(bf16)
        up_bias_grad.append(jnp.sum(grad_hidden, axis=1, dtype=f32))
        two = two + jnp.einsum("df,fr->dr", up_w[b], grad_hidden, preferred_element_type=f32)
        down_grad.append(
            jnp.einsum("fr,dr->fd", active, grad_back, preferred_element_type=f32)
        )
        up_grad.append(
            jnp.einsum("dr,fr->df", normed_two, grad_hidden, preferred_element_type=f32)
        )

    def mine(values, r):
        return lax.dynamic_slice_in_dim(values, width * (t ^ r), width, 0)

    passed = [over_c(mine(final, r).astype(bf16)) for r in (1, 3)]
    ends = []
    for got, r in zip(passed, (0, 2)):
        value = mine(resid, r) + mine(final, r) + got.astype(f32) + mine(down_bias, r)
        ends.append((value * live).astype(bf16))

    down_bias_grad = jnp.sum(grad_back, axis=1, dtype=f32)
    grad_two = two + over_c(two.astype(bf16)).astype(f32)
    second_gain_grad = jnp.sum(grad_two * normal_two, axis=1)
    second_bias_grad = jnp.sum(grad_two, axis=1)
    resid_grad = grad_back.astype(f32) + norm_backward(grad_two, normal_two, scale_two, second_gain)
    grad_branch = resid_grad.astype(bf16)
    out_bias_grad = jnp.sum(grad_branch, axis=1, dtype=f32)
    mix_grad, chan_grads, gates, second_grads, pieces = [], [], [], 0.0, 0.0
    for b in (1, 0):
        proj, u = saved[b]
        out_grad = jnp.einsum("cr,dr->cd", mixed[b], grad_branch, preferred_element_type=f32)
        gz, resp_grad, sums = mixer_bwd(
            grad_branch, mix_w[b], proj, u, chans[b], resp[b], table, inverse, sz
        )
        gz = gz.reshape(3 * width, -1)
        gates.append(gz)
        resp_grad = resp_grad[:, : sz.seq]
        grad_raw = resp_grad * envelope[b]
        weight = channels[b][17:]
        weight_grad = lax.dot_general(
            filter_second, grad_raw, (((0,), (1,)), ((), ())), precision=highest
        )
        second_grads = second_grads + lax.dot_general(
            grad_raw, weight, (((0,), (1,)), ((), ())), precision=highest
        )
        chan_grads.append(jnp.concatenate([sums.T[:DECAY], weight_grad], axis=0))
        in_grad = jnp.einsum("er,dr->ed", gz, normed_one, preferred_element_type=f32)
        mix_grad.append(jnp.concatenate([in_grad, out_grad], axis=0))
        if b == 1:
            mix_got = over_y(mix_grad[0].astype(bf16))
            out_pair = [ends[0], over_y(after(ends[1], mix_grad[0]))]
        pieces = pieces + jnp.einsum(
            "ed,er->dr", mix_w[b][: 3 * width], gz, preferred_element_type=f32
        )
    chan_grads = chan_grads[::-1]
    grad_one = pieces + over_c(pieces.astype(bf16)).astype(f32)
    scale_one = stats[8:9]
    normal_one = (rows.astype(f32) - stats[0:1]) * scale_one
    first_gain_grad = jnp.sum(grad_one * normal_one, axis=1)
    first_bias_grad = jnp.sum(grad_one, axis=1)
    input_grad = resid_grad + norm_backward(grad_one, normal_one, scale_one, first_gain)
    grad_pair = [mine(input_grad, 0), over_y(mine(input_grad, 2).astype(bf16))]

    down_got = after(over_y(down_grad[1].astype(bf16)), grad_branch)
    up_got = after(over_y(up_grad[1].astype(bf16)), gates[0])
    down_weight_grad = reduce_dp(
        down_grad[0] + down_got.astype(f32), dp_count, dp, (gates[0], gates[1])
    )
    up_weight_grad = reduce_dp(up_grad[0] + up_got.astype(f32), dp_count, dp, (gates[1],))
    mix_sum = reduce_dp(mix_grad[1] + mix_got.astype(f32), dp_count, dp, ())
    in_weight_grad = mix_sum[: 3 * width].reshape(3, width, features)
    out_weight_grad = mix_sum[3 * width :]

    vector_grads = jnp.stack(
        [
            first_gain_grad,
            first_bias_grad,
            out_bias_grad,
            second_gain_grad,
            second_bias_grad,
            down_bias_grad,
        ],
        axis=1,
    )
    vector_sum = mine(vector_grads, 0) + over_y(mine(vector_grads, 2))
    chan_sum = chan_grads[0] + over_y(chan_grads[1])
    up_bias_sum = up_bias_grad[0] + over_y(up_bias_grad[1])
    filter_grads = filter_pull(second_grads)
    filter_flat = jnp.concatenate([value.reshape(-1) for value in filter_grads])
    filter_flat = filter_flat + over_c(filter_flat)
    filter_flat = filter_flat + over_y(filter_flat)
    packed = jnp.concatenate(
        [vector_sum.reshape(-1), chan_sum.reshape(-1), up_bias_sum, filter_flat]
    )
    packed = reduce_small(packed, dp_count)
    sizes = [vector_sum.size, chan_sum.size, up_bias_sum.size]
    marks = np.cumsum(sizes)
    vector_sum = packed[: marks[0]].reshape(vector_sum.shape)
    chan_sum = packed[marks[0] : marks[1]].reshape(chan_sum.shape)
    up_bias_sum = packed[marks[1] : marks[2]]
    rest = packed[marks[2] :]
    filter_out = []
    at = 0
    for value in filter_grads:
        filter_out.append(rest[at : at + value.size].reshape(value.shape))
        at += value.size

    prompt_out, cont_out = unpack(group_map, *out_pair, sz)
    prompt_grad, cont_grad = unpack(group_map, *grad_pair, sz)
    return (
        prompt_out,
        cont_out,
        prompt_grad,
        cont_grad,
        vector_sum[:, 0],
        vector_sum[:, 1],
        in_weight_grad,
        chan_sum[:3],
        chan_sum[3:12].reshape(3, KER, width),
        chan_sum[12:15],
        filter_out[0],
        filter_out[1],
        filter_out[2],
        filter_out[3],
        filter_out[4],
        chan_sum[16:],
        chan_sum[15],
        out_weight_grad,
        vector_sum[:, 2],
        vector_sum[:, 3],
        vector_sum[:, 4],
        up_weight_grad,
        up_bias_sum,
        down_weight_grad,
        vector_sum[:, 5],
    )


def solution(mesh):
    placed = (
        P("dp", "tensor", None),
        P("dp", "tensor", None),
        P("dp"),
        P("dp"),
        P("tensor"),
        P("tensor"),
        P(None, "tensor", None),
        P(None, "tensor"),
        P(None, None, "tensor"),
        P(None, "tensor"),
        P(),
        P(),
        P(),
        P(),
        P(),
        P(None, "tensor"),
        P("tensor"),
        P("tensor"),
        P("tensor", None),
        P("tensor"),
        P("tensor"),
        P("tensor"),
        P(None, "tensor"),
        P("tensor"),
        P("tensor", None),
        P("tensor"),
        P("dp", "tensor", None),
        P("dp", "tensor", None),
    )
    return jax.shard_map(
        partial(shards, mesh.shape["dp"]),
        mesh=mesh,
        in_specs=placed,
        out_specs=(
            P("dp", "tensor", None),
            P("dp", "tensor", None),
            P("dp", "tensor", None),
            P("dp", "tensor", None),
            P("tensor"),
            P("tensor"),
            P(None, "tensor", None),
            P(None, "tensor"),
            P(None, None, "tensor"),
            P(None, "tensor"),
            P(),
            P(),
            P(),
            P(),
            P(),
            P(None, "tensor"),
            P("tensor"),
            P("tensor", None),
            P("tensor"),
            P("tensor"),
            P("tensor"),
            P(None, "tensor"),
            P("tensor"),
            P("tensor", None),
            P("tensor"),
        ),
        check_vma=False,
    )
```

```python
from functools import partial
import math

import jax
import jax.numpy as jnp
import numpy as np
from jax import lax
from jax.experimental import pallas as pl
from jax.experimental.pallas import tpu as pltpu
from jax.sharding import PartitionSpec as P

EMB = 33
KER = 3
CONT = 128
GRP_DEV = 2
BLOCK = 256

epsilon = 1e-05
highest = lax.Precision.HIGHEST
f32 = jnp.float32
bf16 = jnp.bfloat16


def high_dot(left, right):
    return jnp.dot(left, right, precision=highest)


def embedding_table(length):
    steps = np.arange(length, dtype=np.float32)
    bands = (EMB - 1) // 2
    freqs = np.linspace(0.0001, bands - 1, bands, dtype=np.float32)
    angle = np.float32(2.0 * math.pi) * steps[:, None] * freqs[None, :] / np.float32(length)
    return np.concatenate(
        [steps[:, None] / np.float32(length - 1), np.cos(angle), -np.sin(angle)], axis=1
    ).astype(np.float32)


def filter_hidden(embed, embed_weight, embed_bias, inner_weight, inner_bias, sine_freq):
    first = jnp.sin(sine_freq * (high_dot(embed, embed_weight) + embed_bias))
    return jnp.sin(sine_freq * (high_dot(first, inner_weight) + inner_bias))


def block_table():
    steps = np.arange(BLOCK)
    angle = 2.0 * math.pi / BLOCK * (steps[:, None] * (steps[None, :] + 0.25))
    return np.concatenate([np.cos(angle), -np.sin(angle)], axis=1)


def spectrum(values, table):
    return jnp.dot(values.astype(bf16), table, preferred_element_type=f32)


class Sizes:
    pass


LANES = 128
ROWS = 16
BIAS_IN, KERNEL, BIAS_CONV, SKIP, DECAY, FILTER = 0, 3, 12, 15, 16, 17


def cmul(a, b):
    return (a[0] * b[0] - a[1] * b[1], a[0] * b[1] + a[1] * b[0])


def cmul_conj(a, b):
    return (a[0] * b[0] + a[1] * b[1], a[1] * b[0] - a[0] * b[1])


def cadd(items):
    result = items[0]
    for item in items[1:]:
        result = (result[0] + item[0], result[1] + item[1])
    return result


def plus_i(a, b):
    return (a[0] - b[1], a[1] + b[0])


def minus_i(a, b):
    return (a[0] + b[1], a[1] - b[0])


def lane_slice(v):
    return slice(v * LANES, (v + 1) * LANES)


def column(chan, rows, at):
    return jnp.broadcast_to(chan[rows, at : at + 1], (ROWS, LANES))


def conv_stream(load, chan, rows, k, lane, prompt_tiles, tiles):
    bias = column(chan, rows, BIAS_CONV + k)
    taps = [column(chan, rows, KERNEL + KER * k + j) for j in range(KER)]
    before = [jnp.zeros((ROWS, LANES), f32)] * (KER - 1)
    last = None
    for v in range(tiles):
        value = load(k, v)
        rolled = [pltpu.roll(value, j, 1) for j in range(1, KER)]
        result = bias + taps[0] * value
        history = before if v < prompt_tiles else last
        for j in range(1, KER):
            result = result + taps[j] * jnp.where(lane < j, history[j - 1], rolled[j - 1])
        if v < prompt_tiles:
            before = rolled
            last = rolled
        yield v, value, result


def block_parts(sz):
    parts = [(slice(i * BLOCK, (i + 1) * BLOCK), BLOCK) for i in range(sz.blocks)]
    start = sz.prompt
    parts += [(slice(start + n * CONT, start + (n + 1) * CONT), CONT) for n in range(sz.per)]
    return parts


def freq_pair(ref, index, rows, tile):
    real = ref[index, rows, lane_slice(tile)]
    imag = ref[index, rows, lane_slice(tile + BLOCK // LANES)]
    return (real, imag)


def store_pair(ref, index, rows, tile, pair):
    ref[index, rows, lane_slice(tile)] = pair[0].astype(ref.dtype)
    ref[index, rows, lane_slice(tile + BLOCK // LANES)] = pair[1].astype(ref.dtype)


def mixer_fwd_kernel(
    sz, normed, weight, chan, resp, table, inverse, mixed, proj, u, z, gb, spec, prod
):
    width = chan.shape[0]
    tiles = normed.shape[1] // LANES
    prompt_tiles = sz.prompt // LANES
    parts = block_parts(sz)
    n = sz.blocks

    @pl.loop(0, normed.shape[1] // BLOCK)
    def _(i):
        cols = pl.ds(pl.multiple_of(i * BLOCK, BLOCK), BLOCK)
        got = jnp.dot(weight[: 3 * width, :], normed[:, cols], preferred_element_type=f32)
        for k in range(3):
            z[k, :, cols] = got[k * width : (k + 1) * width]

    @pl.loop(0, width // ROWS)
    def _(c):
        rows = pl.ds(pl.multiple_of(c * ROWS, ROWS), ROWS)
        lane = lax.broadcasted_iota(jnp.int32, (ROWS, LANES), 1)
        biases = [column(chan, rows, BIAS_IN + k) for k in range(3)]

        def load(k, v):
            return z[k, rows, lane_slice(v)] + biases[k]

        streams = [conv_stream(load, chan, rows, k, lane, prompt_tiles, tiles) for k in range(3)]
        for first, second, third in zip(*streams):
            v = first[0]
            for k, item in enumerate((first, second, third)):
                proj[k, rows, lane_slice(v)] = item[1].astype(bf16)
            gated = second[2] * third[2]
            z[0, rows, lane_slice(v)] = first[2]
            z[1, rows, lane_slice(v)] = gated
            gb[rows, lane_slice(v)] = gated.astype(bf16)

    for i, (cols, length) in enumerate(parts):
        spec[i] = jnp.dot(gb[:, cols], table[:length, :], preferred_element_type=f32)

    @pl.loop(0, width // ROWS)
    def _(c):
        rows = pl.ds(pl.multiple_of(c * ROWS, ROWS), ROWS)
        for tile in range(BLOCK // LANES):
            xs = [freq_pair(spec, i, rows, tile) for i in range(n)]
            hs = [freq_pair(resp, j, rows, tile) for j in range(n + 1)]
            prior = None
            for m in range(n + 1):
                now = cadd([cmul(xs[i], hs[m - i]) for i in range(n) if 0 <= m - i <= n])
                out = now if prior is None else plus_i(now, prior)
                prior = now
                if m < n:
                    store_pair(prod, m, rows, tile, out)
            for q in range(sz.per):
                own = cmul(freq_pair(spec, n + q, rows, tile), hs[0])
                store_pair(prod, n + q, rows, tile, cadd([own, out]))

    skip = chan[:, SKIP : SKIP + 1]
    for i, (cols, length) in enumerate(parts):
        value = jnp.dot(prod[i], inverse[:, :length], preferred_element_type=f32)
        value = value + skip * z[1, :, cols]
        u[:, cols] = value.astype(bf16)
        mixed[:, cols] = (value * z[0, :, cols]).astype(bf16)


def mixer_bwd_kernel(
    sz,
    branch,
    weight,
    proj,
    u,
    chan,
    resp,
    table,
    inverse,
    gz,
    resp_grad,
    sums,
    dm,
    conv,
    gb,
    lb,
    gspec,
    xspec,
    prod,
    gg,
):
    width = chan.shape[0]
    tiles = branch.shape[1] // LANES
    prompt_tiles = sz.prompt // LANES
    parts = block_parts(sz)
    n = sz.blocks

    @pl.loop(0, branch.shape[1] // BLOCK)
    def _(i):
        cols = pl.ds(pl.multiple_of(i * BLOCK, BLOCK), BLOCK)
        dm[:, cols] = jnp.dot(
            weight[3 * width :, :], branch[:, cols], preferred_element_type=f32
        )

    def place_sum(rows, lane, at, value):
        total = jnp.sum(value, axis=1, keepdims=True)
        sums[rows, :] = jnp.where(lane == at, total, sums[rows, :])

    @pl.loop(0, width // ROWS)
    def _(c):
        rows = pl.ds(pl.multiple_of(c * ROWS, ROWS), ROWS)
        lane = lax.broadcasted_iota(jnp.int32, (ROWS, LANES), 1)

        def load(k, v):
            return proj[k, rows, lane_slice(v)].astype(f32)

        streams = [conv_stream(load, chan, rows, k, lane, prompt_tiles, tiles) for k in range(3)]
        skips = jnp.zeros((ROWS, LANES), f32)
        for first, second, third in zip(*streams):
            v = first[0]
            for k, item in enumerate((first, second, third)):
                conv[k, rows, lane_slice(v)] = item[2]
            gated = second[2] * third[2]
            long = dm[rows, lane_slice(v)] * first[2]
            skips = skips + long * gated
            gb[rows, lane_slice(v)] = gated.astype(bf16)
            lb[rows, lane_slice(v)] = long.astype(bf16)
        sums[rows, :] = jnp.zeros((ROWS, LANES), f32)
        place_sum(rows, lane, SKIP, skips)

    for i, (cols, length) in enumerate(parts):
        gspec[i] = jnp.dot(lb[:, cols], table[:length, :], preferred_element_type=f32)
        xspec[i] = jnp.dot(gb[:, cols], table[:length, :], preferred_element_type=f32)

    @pl.loop(0, width // ROWS)
    def _(c):
        rows = pl.ds(pl.multiple_of(c * ROWS, ROWS), ROWS)
        for tile in range(BLOCK // LANES):
            gs = [freq_pair(gspec, i, rows, tile) for i in range(n)]
            hs = [freq_pair(resp, j, rows, tile) for j in range(n + 1)]
            own, lags = [], []
            for q in range(sz.per):
                g = freq_pair(gspec, n + q, rows, tile)
                own.append(g)
                store_pair(prod, n + q, rows, tile, cmul_conj(g, hs[0]))
                lags.append(cmul_conj(g, freq_pair(xspec, n + q, rows, tile)))
            gs.append(cadd(own))
            after = cmul_conj(gs[n], hs[0])
            for i in reversed(range(n)):
                now = cadd([cmul_conj(gs[m], hs[m - i]) for m in range(i, n + 1)])
                store_pair(prod, i, rows, tile, minus_i(now, after))
                after = now
            xs = [freq_pair(xspec, i, rows, tile) for i in range(n)]
            after = None
            for j in reversed(range(n + 1)):
                items = [cmul_conj(gs[m], xs[m - j]) for m in range(j, n + 1) if m - j < n]
                now = cadd(items + (lags if j == 0 else []))
                out = now if after is None else minus_i(now, after)
                store_pair(prod, n + sz.per + j, rows, tile, out)
                after = now

    skip = chan[:, SKIP : SKIP + 1]
    for i, (cols, length) in enumerate(parts):
        value = jnp.dot(prod[i], inverse[:, :length], preferred_element_type=f32)
        gg[:, cols] = value + skip * (dm[:, cols] * conv[0, :, cols])
    for j in range(n + 1):
        resp_grad[:, j * BLOCK : (j + 1) * BLOCK] = jnp.dot(
            prod[n + sz.per + j], inverse[...], preferred_element_type=f32
        )

    @pl.loop(0, width // ROWS)
    def _(c):
        rows = pl.ds(pl.multiple_of(c * ROWS, ROWS), ROWS)
        lane = lax.broadcasted_iota(jnp.int32, (ROWS, LANES), 1)
        zero = jnp.zeros((ROWS, LANES), f32)
        for k in range(3):
            taps = [column(chan, rows, KERNEL + KER * k + j) for j in range(KER)]
            total_bias, total_out = zero, zero
            total_taps = [zero] * KER
            heads = zero
            after = None
            for v in list(range(prompt_tiles, tiles)) + list(reversed(range(prompt_tiles))):
                cols = lane_slice(v)
                if k == 0:
                    grad = dm[rows, cols] * u[rows, cols].astype(f32)
                else:
                    grad = gg[rows, cols] * conv[3 - k, rows, cols]
                rolled = [pltpu.roll(grad, LANES - j, 1) for j in range(1, KER)]
                if v >= prompt_tiles:
                    heads = heads + grad
                    following = [zero] * (KER - 1)
                else:
                    if after is None:
                        after = [pltpu.roll(heads, LANES - j, 1) for j in range(1, KER)]
                    following = after
                    after = rolled
                shifted = [grad] + [
                    jnp.where(lane < LANES - j, rolled[j - 1], following[j - 1])
                    for j in range(1, KER)
                ]
                value = proj[k, rows, cols].astype(f32)
                out = taps[0] * grad
                for j in range(1, KER):
                    out = out + taps[j] * shifted[j]
                low = out.astype(bf16)
                gz[k, rows, cols] = low
                total_bias = total_bias + grad
                total_out = total_out + low.astype(f32)
                total_taps = [t + value * s for t, s in zip(total_taps, shifted)]
            place_sum(rows, lane, BIAS_IN + k, total_out)
            place_sum(rows, lane, BIAS_CONV + k, total_bias)
            for j in range(KER):
                place_sum(rows, lane, KERNEL + KER * k + j, total_taps[j])


VMEM_SPEC = pl.BlockSpec(memory_space=pltpu.VMEM)


SMEM_SPEC = pl.BlockSpec(memory_space=pltpu.SMEM)

def cost(ins, outs, flops=0):
    nbytes = sum(math.prod(v.shape) * v.dtype.itemsize for v in list(ins) + list(outs))
    return pl.CostEstimate(flops=flops, bytes_accessed=nbytes, transcendentals=0)


def call(kernel, ins, outs, scratch, name, limit, scalars=0, flops=0):
    return pl.pallas_call(
        kernel,
        out_shape=tuple(outs),
        in_specs=[SMEM_SPEC] * scalars + [VMEM_SPEC] * (len(ins) - scalars),
        out_specs=tuple([VMEM_SPEC] * len(outs)),
        scratch_shapes=scratch,
        compiler_params=pltpu.CompilerParams(vmem_limit_bytes=limit << 20),
        cost_estimate=cost(ins, outs, flops),
        name=name,
    )(*ins)


def mixer_fwd(normed, weight, chan, resp, table, inverse, sz):
    width = chan.shape[0]
    cols = normed.shape[1]
    parts = sz.blocks + sz.per
    outs = [
        jax.ShapeDtypeStruct((width, cols), bf16),
        jax.ShapeDtypeStruct((3, width, cols), bf16),
        jax.ShapeDtypeStruct((width, cols), bf16),
    ]
    scratch = [
        pltpu.VMEM((3, width, cols), f32),
        pltpu.VMEM((width, cols), bf16),
        pltpu.VMEM((parts, width, 2 * BLOCK), f32),
        pltpu.VMEM((parts, width, 2 * BLOCK), bf16),
    ]
    return call(
        partial(mixer_fwd_kernel, sz),
        (normed, weight, chan, resp, table, inverse),
        outs,
        scratch,
        "mixer_fwd",
        32,
        flops=8 * width * cols * normed.shape[0],
    )


def mixer_bwd(branch, weight, proj, u, chan, resp, table, inverse, sz):
    width = chan.shape[0]
    cols = branch.shape[1]
    parts = sz.blocks + sz.per
    outs = [
        jax.ShapeDtypeStruct((3, width, cols), bf16),
        jax.ShapeDtypeStruct((width, (sz.blocks + 1) * BLOCK), f32),
        jax.ShapeDtypeStruct((width, LANES), f32),
    ]
    scratch = [
        pltpu.VMEM((width, cols), f32),
        pltpu.VMEM((3, width, cols), f32),
        pltpu.VMEM((width, cols), bf16),
        pltpu.VMEM((width, cols), bf16),
        pltpu.VMEM((parts, width, 2 * BLOCK), f32),
        pltpu.VMEM((parts, width, 2 * BLOCK), f32),
        pltpu.VMEM((parts + sz.blocks + 1, width, 2 * BLOCK), bf16),
        pltpu.VMEM((width, cols), f32),
    ]
    return call(
        partial(mixer_bwd_kernel, sz),
        (branch, weight, proj, u, chan, resp, table, inverse),
        outs,
        scratch,
        "mixer_bwd",
        40,
        flops=12 * width * cols * branch.shape[0],
    )


def each_cont(sz, group_map, run):
    y = lax.axis_index("tensor") // 2
    used = [jnp.int32(0), jnp.int32(0)]
    for c in range(sz.per * GRP_DEV):
        local = lax.rem(group_map[c], GRP_DEV)
        rank = jnp.minimum(jnp.where(local == 0, used[0], used[1]), sz.per - 1)
        used = [used[g] + (local == g).astype(jnp.int32) for g in range(GRP_DEV)]
        cols = pl.ds(pl.multiple_of(sz.prompt + rank * CONT, CONT), CONT)
        run(c, local == y, cols)
    return y


def pick_kernel(sz, group_map, lengths, prompt, cont, keep, send, live):
    live[...] = jnp.ones(live.shape, f32)

    def run(c, own, cols):
        @pl.when(own)
        def _():
            keep[:, cols] = cont[c]
            place = lax.broadcasted_iota(jnp.int32, (8, CONT), 1)
            live[:, cols] = jnp.where(place < lengths[c], 1.0, 0.0)

        @pl.when(jnp.logical_not(own))
        def _():
            send[:, cols] = cont[c]

    y = each_cont(sz, group_map, run)
    keep[:, : sz.prompt] = prompt[y]
    send[:, : sz.prompt] = prompt[1 - y]


def pick(group_map, lengths, prompt, cont, sz):
    shape = (prompt.shape[1], sz.prompt + sz.per * CONT)
    outs = [jax.ShapeDtypeStruct(shape, bf16)] * 2
    outs.append(jax.ShapeDtypeStruct((8, shape[1]), f32))
    ins = (group_map, lengths, prompt, cont)
    return call(partial(pick_kernel, sz), ins, outs, [], "pick", 16, 2)


def unpack_kernel(sz, group_map, own, other, prompts, conts):
    kind = prompts.dtype

    def run(c, here, cols):
        @pl.when(here)
        def _():
            conts[c] = own[:, cols].astype(kind)

        @pl.when(jnp.logical_not(here))
        def _():
            conts[c] = other[:, cols].astype(kind)

    y = each_cont(sz, group_map, run)
    prompts[y] = own[:, : sz.prompt].astype(kind)
    prompts[1 - y] = other[:, : sz.prompt].astype(kind)


def unpack(group_map, own, other, sz):
    width = own.shape[0]
    outs = [
        jax.ShapeDtypeStruct((GRP_DEV, width, sz.prompt), own.dtype),
        jax.ShapeDtypeStruct((GRP_DEV * sz.per, width, CONT), own.dtype),
    ]
    ins = (group_map, own, other)
    return call(partial(unpack_kernel, sz), ins, outs, [], "unpack", 24, 1)


def feature_rows(width, r):
    place = lax.axis_index("tensor") ^ r
    return pl.ds(pl.multiple_of(place * width, 64), width)


def norm_one_kernel(width, first, second, third, fourth, vectors, rows, normed, mid, factor):
    parts = (first, second, third, fourth)
    count = len(parts) * width
    total, square = 0.0, 0.0
    for part in parts:
        value = part[...].astype(f32)
        total = total + jnp.sum(value, axis=0, keepdims=True)
        square = square + jnp.sum(value * value, axis=0, keepdims=True)
    center = total / count
    scale = lax.rsqrt(square / count - center * center + epsilon)
    for r, part in enumerate(parts):
        at = feature_rows(width, r)
        value = (part[...].astype(f32) - center) * scale
        rows[at, :] = part[...]
        normed[at, :] = (value * vectors[at, 0:1] + vectors[at, 1:2]).astype(bf16)
    mid[...] = center
    factor[...] = scale


def lane_sum(values):
    return values[:, :LANES] + values[:, LANES:]


def add_sums(sums, width, parts):
    @pl.when(pl.program_id(0) == 0)
    def _():
        sums[...] = jnp.zeros(sums.shape, f32)

    for i, part in enumerate(parts):
        for b in range(2):
            at = slice((2 * i + b) * width, (2 * i + b + 1) * width)
            sums[at, :] = sums[at, :] + lane_sum(part[feature_rows(width, 2 * b), :])


def norm_backward(grad, normal, scale, gain):
    g = grad * gain
    count = g.shape[0]
    first = jnp.sum(g, axis=0, keepdims=True) / count
    second = jnp.sum(g * normal, axis=0, keepdims=True) / count
    return scale * (g - first - normal * second)


def back_two_kernel(
    width, grad, got, resid, mid, factor, base, vectors, low, own, other, sums, work
):
    value = grad[...] + got[...].astype(f32)
    normal = (resid[...] - mid[...]) * factor[...]
    start = base[...].astype(f32)
    result = start + norm_backward(value, normal, factor[...], vectors[:, 3:4])
    rounded = result.astype(bf16)
    low[...] = rounded
    for i, part in enumerate((value * normal, value, rounded.astype(f32), start, result)):
        work[i] = part
    own[...] = work[4, feature_rows(width, 0), :]
    other[...] = work[4, feature_rows(width, 2), :]
    add_sums(sums, width, [work.at[i] for i in range(4)])


def back_one_kernel(
    width, grad, got, rows, mid, factor, near, far, vectors, own, other, sums, work
):
    value = grad[...] + got[...].astype(f32)
    normal = (rows[...].astype(f32) - mid[...]) * factor[...]
    result = norm_backward(value, normal, factor[...], vectors[:, 0:1])
    for i, part in enumerate((value * normal, value, result)):
        work[i] = part
    own[...] = near[...] + work[2, feature_rows(width, 0), :]
    other[...] = (far[...] + work[2, feature_rows(width, 2), :]).astype(bf16)
    add_sums(sums, width, [work.at[i] for i in range(2)])


def grad_kernel(width, first, second, third, fourth, live, grad):
    for r, part in enumerate((first, second, third, fourth)):
        value = part[...].astype(f32) * live[0:1, :]
        grad[feature_rows(width, r), :] = value.astype(bf16)


def by_columns(kernel, ins, outs, name, scratch=()):
    count = outs[0].shape[1]

    def spec(v):
        if v.shape[1] == count:
            return pl.BlockSpec((v.shape[0], BLOCK), lambda i: (0, i))
        return pl.BlockSpec(v.shape, lambda i: (0, 0))

    return pl.pallas_call(
        kernel,
        grid=(count // BLOCK,),
        out_shape=tuple(outs),
        in_specs=[spec(v) for v in ins],
        out_specs=tuple(spec(v) for v in outs),
        scratch_shapes=list(scratch),
        compiler_params=pltpu.CompilerParams(vmem_limit_bytes=32 << 20),
        cost_estimate=cost(ins, outs),
        name=name,
    )(*ins)


def normalize(values):
    count = values.shape[0]
    center = jnp.sum(values, axis=0, keepdims=True) / count
    spread = jnp.sum(values * values, axis=0, keepdims=True) / count - center * center
    scale = lax.rsqrt(spread + epsilon)
    return ((values - center) * scale, center, scale)


def gelu_parts(hidden):
    size = jnp.abs(hidden)
    bell = jnp.exp(-0.5 * hidden * hidden)
    part = 1.0 / (1.0 + (0.3275911 * math.sqrt(0.5)) * size)
    poly = 1.061405429
    for value in (-1.453152027, 1.421413741, -0.284496736, 0.254829592):
        poly = poly * part + value
    tail = 0.5 * poly * part * bell
    cdf = jnp.where(hidden < 0, tail, 1.0 - tail)
    slope = cdf + hidden * (bell * (1.0 / math.sqrt(2.0 * math.pi)))
    return lax.optimization_barrier(((hidden * cdf).astype(bf16), slope.astype(bf16)))


def together(*values):
    return lax.optimization_barrier(values)


def swap(axis, count, bit):
    def run(values):
        return lax.ppermute(values, axis, [(i, i ^ bit) for i in range(count)])

    return run


over_y = swap("tensor", 4, 2)
over_c = swap("tensor", 4, 1)


def halves(values, high):
    half = values.shape[0] // 2
    low_part, high_part = values[:half], values[half:]
    give = jnp.where(high, low_part, high_part).astype(bf16)
    return (give, jnp.where(high, high_part, low_part))


def gathered(held, other, high):
    return jnp.where(
        high,
        jnp.concatenate([other, held], axis=0),
        jnp.concatenate([held, other], axis=0),
    )


def reduce_far(values, count, index):
    bits = [1 << b for b in range(2, count.bit_length() - 1)]
    held = values
    for bit in bits:
        give, keep = halves(held, (index & bit) != 0)
        held = keep + swap("dp", count, bit)(give).astype(f32)
    held = held.astype(bf16)
    for bit in reversed(bits):
        held = gathered(held, swap("dp", count, bit)(held), (index & bit) != 0)
    return held


def reduce_small(values, count):
    bit = 1
    while bit < count:
        values = values + swap("dp", count, bit)(values)
        bit *= 2
    return values


def shards(dp_count, *args):
    (
        prompt_tokens,
        cont_tokens,
        group_map,
        cont_lengths,
        first_gain,
        first_bias,
        in_weight,
        in_bias,
        conv_kernel,
        conv_bias,
        embed_weight,
        embed_bias,
        inner_weight,
        inner_bias,
        sine_freq,
        filter_weight,
        decay_rate,
        skip_gain,
        out_weight,
        out_bias,
        second_gain,
        second_bias,
        up_weight,
        up_bias,
        down_weight,
        down_bias,
        prompt_cotan,
        cont_cotan,
    ) = args
    width = prompt_tokens.shape[1]
    sz = Sizes()
    sz.prompt = prompt_tokens.shape[2]
    sz.seq = sz.prompt + CONT
    sz.blocks = sz.prompt // BLOCK
    conts = cont_tokens.shape[0]
    sz.per = conts // GRP_DEV
    features = 4 * width
    t = lax.axis_index("tensor")
    y = t // 2
    dp = lax.axis_index("dp")
    table = jnp.asarray(block_table(), bf16)
    inverse = jnp.asarray(block_table().T / BLOCK, bf16)

    over_x = swap("dp", dp_count, 1)
    over_z = swap("dp", dp_count, 2)
    x = dp % 2
    high_x, high_z = x != 0, (dp & 2) != 0
    vectors = jnp.stack([first_gain, first_bias, out_bias, second_gain, second_bias, down_bias], 1)
    vectors_other = over_y(vectors)
    keep, send, live = pick(group_map, cont_lengths, prompt_tokens, cont_tokens, sz)
    got = over_y(send)
    near = over_c(keep)
    vectors = jnp.stack([vectors, vectors_other])
    vectors_near = over_c(vectors)
    odd = t % 2 != 0
    pairs = jnp.where(
        odd, jnp.stack([vectors_near, vectors], 1), jnp.stack([vectors, vectors_near], 1)
    )
    pairs = jnp.where(y != 0, jnp.stack([pairs[1], pairs[0]]), pairs)
    vectors = pairs.reshape(features, -1)
    first_gain, first_bias, out_bias, second_gain, second_bias, down_bias = [
        vectors[:, i : i + 1] for i in range(6)
    ]
    in_bias, conv_kernel, conv_bias, filter_weight, near = together(
        in_bias, conv_kernel, conv_bias, filter_weight, near
    )
    up_rows = up_bias.shape[0] // width
    channel = jnp.concatenate(
        [
            in_bias,
            conv_kernel.reshape(KER * 3, width),
            conv_bias,
            skip_gain[None],
            decay_rate[None],
            filter_weight,
            up_bias.reshape(up_rows, width),
        ],
        axis=0,
    )
    channels = [channel, over_y(channel)]
    up_b = [up_bias, channels[1][-up_rows:].reshape(-1)]
    channels = [value[:-up_rows] for value in channels]

    def half_of(weight):
        half = weight.shape[0] // 2
        return lax.dynamic_slice_in_dim(weight, x * half, half, 0)

    def whole_of(got, other):
        return jnp.where(
            x != 0,
            jnp.concatenate([other, got], axis=0),
            jnp.concatenate([got, other], axis=0),
        )

    mix_own = jnp.concatenate([in_weight.reshape(3 * width, features), out_weight], axis=0)
    mix_part, near = together(half_of(mix_own), near)
    mix_half = over_y(mix_part)
    keep_grad, send_grad, _ = pick(group_map, cont_lengths, prompt_cotan, cont_cotan, sz)
    embed_weight, near = together(embed_weight, near)

    embed = jnp.asarray(embedding_table(sz.seq))
    filter_second, filter_pull = jax.vjp(
        partial(filter_hidden, embed), embed_weight, embed_bias, inner_weight, inner_bias, sine_freq
    )
    steps = jnp.arange(sz.seq, dtype=f32) / (sz.seq - 1)
    resp, envelope = [], []
    for b in range(2):
        decay, weight = channels[b][16], channels[b][17:]
        env = jnp.exp(-decay[:, None] * steps[None, :]) + 0.05
        response = (
            lax.dot_general(weight, filter_second, (((0,), (1,)), ((), ())), precision=highest)
            * env
        )
        padded = jnp.pad(response, ((0, 0), (0, (sz.blocks + 1) * BLOCK - sz.seq)))
        resp.append(
            jnp.stack(
                [
                    spectrum(padded[:, j * BLOCK : (j + 1) * BLOCK], table)
                    for j in range(sz.blocks + 1)
                ]
            )
        )
        envelope.append(env)
    got, mix_half, resp[0] = together(got, mix_half, resp[0])
    got_near = over_c(got)
    up_part, down_part, send_grad, got = together(
        half_of(up_weight), half_of(down_weight), send_grad, got
    )
    got_grad = over_y(send_grad)
    token_blocks = [keep, near, got, got_near]
    rows, normed_one, center_one, scale_one = by_columns(
        partial(norm_one_kernel, width),
        (*token_blocks, vectors),
        [
            jax.ShapeDtypeStruct((features, keep.shape[1]), bf16),
            jax.ShapeDtypeStruct((features, keep.shape[1]), bf16),
            jax.ShapeDtypeStruct((1, keep.shape[1]), f32),
            jax.ShapeDtypeStruct((1, keep.shape[1]), f32),
        ],
        "norm_one",
    )
    mix_rest = over_x(mix_half)
    up_half = over_y(up_part)
    mix_w = [mix_own]
    down_half = over_y(down_part)

    chans = [jnp.pad(value.T, ((0, 0), (0, LANES - value.shape[0]))) for value in channels]
    mixed, saved = [], []
    for b in range(2):
        part, proj, u = mixer_fwd(
            normed_one, mix_w[b], chans[b], resp[b], table, inverse, sz
        )
        if b == 0:
            mix_rest, part = together(mix_rest, part)
            mix_w.append(whole_of(mix_half, mix_rest))
        mixed.append(part)
        saved.append((proj, u))
    out_w = [weight[3 * width :] for weight in mix_w]
    up_half, got_grad, mixed[1] = together(up_half, got_grad, mixed[1])
    up_w = [up_weight, whole_of(up_half, over_x(up_half))]
    grad_blocks = [keep_grad, over_c(keep_grad), got_grad, over_c(got_grad)]
    (grad_back,) = by_columns(
        partial(grad_kernel, width),
        (*grad_blocks, live),
        [jax.ShapeDtypeStruct((features, keep.shape[1]), bf16)],
        "place_grad",
    )
    live = live[0:1]
    mixed_near = [over_c(part) for part in mixed]
    mixed_all = mixed + mixed_near
    out_near = over_c(jnp.concatenate(out_w, axis=0))
    branch = jnp.einsum(
        "cd,cr->dr",
        jnp.concatenate([*out_w, out_near], axis=0),
        jnp.concatenate(mixed_all, axis=0),
        preferred_element_type=f32,
    )
    resid = rows.astype(f32) + branch + out_bias
    normal_two, center_two, scale_two = normalize(resid)
    normed_two = (normal_two * second_gain + second_bias).astype(bf16)
    two, actives = 0.0, []
    up_grad, down_grad, up_bias_grad = [], [], []
    for b in range(2):
        hidden = (
            jnp.einsum("df,dr->fr", up_w[b], normed_two, preferred_element_type=f32)
            + up_b[b][:, None]
        )
        active, slope = gelu_parts(hidden)
        if b == 0:
            down_half, active = together(down_half, active)
            down_w = [down_weight, whole_of(down_half, over_x(down_half))]
        actives.append(active)
        grad_active = jnp.einsum("fd,dr->fr", down_w[b], grad_back, preferred_element_type=f32)
        grad_hidden = (grad_active * slope).astype(bf16)
        up_bias_grad.append(jnp.sum(grad_hidden, axis=1, dtype=f32))
        two = two + jnp.einsum("df,fr->dr", up_w[b], grad_hidden, preferred_element_type=f32)
        down_grad.append(
            jnp.einsum("fr,dr->fd", active, grad_back, preferred_element_type=f32)
        )
        up_grad.append(
            jnp.einsum("dr,fr->df", normed_two, grad_hidden, preferred_element_type=f32)
        )

    def mine(values, r):
        return lax.dynamic_slice_in_dim(values, width * (t ^ r), width, 0)

    block = jax.ShapeDtypeStruct((width, keep.shape[1]), f32)
    grad_branch, near_grad, far_grad, sums_two = by_columns(
        partial(back_two_kernel, width),
        (two, over_c(two.astype(bf16)), resid, center_two, scale_two, grad_back, vectors),
        [
            jax.ShapeDtypeStruct((features, keep.shape[1]), bf16),
            block,
            block,
            jax.ShapeDtypeStruct((8 * width, LANES), f32),
        ],
        "norm_two_back",
        [pltpu.VMEM((5, features, BLOCK), f32)],
    )
    up_gives, up_keeps = zip(*[halves(value, high_z) for value in up_grad])
    up_got = over_z(jnp.concatenate(up_gives, axis=0))
    down_got = over_y(down_grad[1].astype(bf16))

    def out_grad(b):
        return jnp.einsum("cr,dr->cd", mixed[b], grad_branch, preferred_element_type=f32)

    def in_grad(gz):
        return jnp.einsum("er,dr->ed", gz, normed_one, preferred_element_type=f32)

    def mixer_back(b, branch):
        proj, u = saved[b]
        gz, response, sums = mixer_bwd(
            branch, mix_w[b], proj, u, chans[b], resp[b], table, inverse, sz
        )
        return (gz.reshape(3 * width, -1), response, sums)

    def back_in(b, gz):
        return jnp.einsum("ed,er->dr", mix_w[b][: 3 * width], gz, preferred_element_type=f32)

    out_give, branch_now = together(out_grad(1).astype(bf16), grad_branch)
    out_got = over_y(out_give)
    gz_1, response_1, sums_1 = mixer_back(1, branch_now)
    down_got, up_got, out_got, gz_1 = together(down_got, up_got, out_got, gz_1)
    down_give, down_keep = halves(down_grad[0] + down_got.astype(f32), high_x)
    in_give, down_give, branch_now = together(in_grad(gz_1).astype(bf16), down_give, grad_branch)
    down_got, in_got = over_x(down_give), over_y(in_give)
    gz_0, response_0, sums_0 = mixer_back(0, branch_now)
    down_got, in_got, gz_0 = together(down_got, in_got, gz_0)
    up_held = jnp.concatenate(up_keeps, axis=0) + up_got.astype(f32)
    half = up_held.shape[0] // 2
    down_give, down_keep = halves(down_keep + down_got.astype(f32), high_z)
    mix_sum = jnp.concatenate([in_grad(gz_0), out_grad(0)], axis=0) + jnp.concatenate(
        [in_got, out_got], axis=0
    ).astype(f32)
    mix_give, mix_keep = halves(mix_sum, high_z)
    up_give, down_give, mix_give, gz_0 = together(
        up_held[half:].astype(bf16), down_give, mix_give, gz_0
    )
    up_got, down_got, mix_got = over_y(up_give), over_z(down_give), over_z(mix_give)
    pieces = back_in(1, gz_1) + back_in(0, gz_0)
    chan_grads, responses = [sums_1, sums_0], [response_1, response_0]
    pieces_near = over_c(pieces.astype(bf16))
    up_got, down_got, mix_got, pieces_near = together(up_got, down_got, mix_got, pieces_near)
    up_give, up_keep = halves(up_held[:half] + up_got.astype(f32), high_x)
    mix_give, mix_keep = halves(mix_keep + mix_got.astype(f32), high_x)
    up_give, mix_give, pieces_near = together(up_give, mix_give, pieces_near)
    mix_got, up_got = over_x(mix_give), over_x(up_give)
    down_far = reduce_far(down_keep + down_got.astype(f32), dp_count, dp)
    own_grad, other_grad, sums_one = by_columns(
        partial(back_one_kernel, width),
        (
            pieces,
            pieces_near,
            rows,
            center_one,
            scale_one,
            near_grad,
            far_grad,
            vectors,
        ),
        [
            block,
            jax.ShapeDtypeStruct((width, keep.shape[1]), bf16),
            jax.ShapeDtypeStruct((4 * width, LANES), f32),
        ],
        "norm_one_back",
        [pltpu.VMEM((3, features, BLOCK), f32)],
    )
    grad_pair = [own_grad, over_y(other_grad)]

    responses[0], responses[1], actives[0], sums_one = together(*responses, actives[0], sums_one)
    final = sum(
        jnp.einsum("fd,fr->dr", down_w[b], actives[b], preferred_element_type=f32)
        for b in range(2)
    )
    passed = [over_c(mine(final, r).astype(bf16)) for r in (1, 3)]
    ends = []
    for value, r in zip(passed, (0, 2)):
        value = mine(resid, r) + mine(final, r) + value.astype(f32) + mine(down_bias, r)
        ends.append((value * live).astype(bf16))

    out_pair = [ends[0], over_y(ends[1])]

    second_grads = 0.0
    for i, b in enumerate((1, 0)):
        grad_raw = responses[i][:, : sz.seq] * envelope[b]
        weight = channels[b][17:]
        weight_grad = lax.dot_general(
            filter_second, grad_raw, (((0,), (1,)), ((), ())), precision=highest
        )
        second_grads = second_grads + lax.dot_general(
            grad_raw, weight, (((0,), (1,)), ((), ())), precision=highest
        )
        chan_grads[i] = jnp.concatenate([chan_grads[i].T[:DECAY], weight_grad], axis=0)
    chan_grads = chan_grads[::-1]
    up_got, mix_got, second_grads = together(up_got, mix_got, second_grads)
    mix_far = reduce_far(mix_keep + mix_got.astype(f32), dp_count, dp)
    up_far = reduce_far(up_keep + up_got.astype(f32), dp_count, dp)
    down_far = gathered(down_far, over_z(down_far), high_z)
    down_weight_grad = gathered(down_far, over_x(down_far), high_x).astype(f32)
    mix_far = gathered(mix_far, over_x(mix_far), high_x)
    mix_far = gathered(mix_far, over_z(mix_far), high_z).astype(f32)
    up_far = gathered(up_far, over_x(up_far), high_x)
    up_weight_grad = gathered(up_far, over_z(up_far), high_z).astype(f32)
    in_weight_grad = mix_far[: 3 * width].reshape(3, width, features)
    out_weight_grad = mix_far[3 * width :]

    sums_two = jnp.sum(sums_two, axis=1).reshape(4, 2, width)
    sums_one = jnp.sum(sums_one, axis=1).reshape(2, 2, width)
    filter_grads = filter_pull(second_grads)
    filter_flat = jnp.concatenate([value.reshape(-1) for value in filter_grads])
    filter_size = filter_flat.shape[0]
    filter_flat = jnp.pad(filter_flat, (0, -filter_size % width)).reshape(-1, width)
    filter_flat = filter_flat + over_c(filter_flat)
    packs = [
        jnp.concatenate(
            [chan_grads[b], up_bias_grad[b].reshape(up_rows, width), sums_two[:, b], sums_one[:, b], filter_flat],
            axis=0,
        )
        for b in range(2)
    ]
    packed = reduce_small(packs[0] + over_y(packs[1]), dp_count)
    marks = np.cumsum([chan_grads[0].shape[0], up_rows, 6])
    chan_sum = packed[: marks[0]]
    up_bias_sum = packed[marks[0] : marks[1]].reshape(-1)
    vector_sum = packed[marks[1] : marks[2]]
    rest = packed[marks[2] :].reshape(-1)
    filter_out = []
    at = 0
    for value in filter_grads:
        filter_out.append(rest[at : at + value.size].reshape(value.shape))
        at += value.size

    prompt_out, cont_out = unpack(group_map, *out_pair, sz)
    prompt_grad, cont_grad = unpack(group_map, *grad_pair, sz)
    return (
        prompt_out,
        cont_out,
        prompt_grad,
        cont_grad,
        vector_sum[4],
        vector_sum[5],
        in_weight_grad,
        chan_sum[:3],
        chan_sum[3:12].reshape(3, KER, width),
        chan_sum[12:15],
        filter_out[0],
        filter_out[1],
        filter_out[2],
        filter_out[3],
        filter_out[4],
        chan_sum[16:],
        chan_sum[15],
        out_weight_grad,
        vector_sum[2],
        vector_sum[0],
        vector_sum[1],
        up_weight_grad,
        up_bias_sum,
        down_weight_grad,
        vector_sum[3],
    )


def solution(mesh):
    placed = (
        P("dp", "tensor", None),
        P("dp", "tensor", None),
        P("dp"),
        P("dp"),
        P("tensor"),
        P("tensor"),
        P(None, "tensor", None),
        P(None, "tensor"),
        P(None, None, "tensor"),
        P(None, "tensor"),
        P(),
        P(),
        P(),
        P(),
        P(),
        P(None, "tensor"),
        P("tensor"),
        P("tensor"),
        P("tensor", None),
        P("tensor"),
        P("tensor"),
        P("tensor"),
        P(None, "tensor"),
        P("tensor"),
        P("tensor", None),
        P("tensor"),
        P("dp", "tensor", None),
        P("dp", "tensor", None),
    )
    return jax.shard_map(
        partial(shards, mesh.shape["dp"]),
        mesh=mesh,
        in_specs=placed,
        out_specs=(
            P("dp", "tensor", None),
            P("dp", "tensor", None),
            P("dp", "tensor", None),
            P("dp", "tensor", None),
            P("tensor"),
            P("tensor"),
            P(None, "tensor", None),
            P(None, "tensor"),
            P(None, None, "tensor"),
            P(None, "tensor"),
            P(),
            P(),
            P(),
            P(),
            P(),
            P(None, "tensor"),
            P("tensor"),
            P("tensor", None),
            P("tensor"),
            P("tensor"),
            P("tensor"),
            P(None, "tensor"),
            P("tensor"),
            P("tensor", None),
            P("tensor"),
        ),
        check_vma=False,
    )
```

```python
from functools import partial
import math

import jax
import jax.numpy as jnp
import numpy as np
from jax import lax
from jax.experimental import pallas as pl
from jax.experimental.pallas import tpu as pltpu
from jax.sharding import PartitionSpec as P

EMB = 33
KER = 3
CONT = 128
GRP_DEV = 2
BLOCK = 256

epsilon = 1e-05
highest = lax.Precision.HIGHEST
f32 = jnp.float32
bf16 = jnp.bfloat16


def high_dot(left, right):
    return jnp.dot(left, right, precision=highest)


def embedding_table(length):
    steps = np.arange(length, dtype=np.float32)
    bands = (EMB - 1) // 2
    freqs = np.linspace(0.0001, bands - 1, bands, dtype=np.float32)
    angle = np.float32(2.0 * math.pi) * steps[:, None] * freqs[None, :] / np.float32(length)
    return np.concatenate(
        [steps[:, None] / np.float32(length - 1), np.cos(angle), -np.sin(angle)], axis=1
    ).astype(np.float32)


def filter_hidden(embed, embed_weight, embed_bias, inner_weight, inner_bias, sine_freq):
    first = jnp.sin(sine_freq * (high_dot(embed, embed_weight) + embed_bias))
    return jnp.sin(sine_freq * (high_dot(first, inner_weight) + inner_bias))


def block_table():
    steps = np.arange(BLOCK)
    angle = 2.0 * math.pi / BLOCK * (steps[:, None] * (steps[None, :] + 0.25))
    return np.concatenate([np.cos(angle), -np.sin(angle)], axis=1)


def spectrum(values, table):
    return jnp.dot(values.astype(bf16), table, preferred_element_type=f32)


class Sizes:
    pass


LANES = 128
ROWS = 16
BIAS_IN, KERNEL, BIAS_CONV, SKIP, DECAY, FILTER = 0, 3, 12, 15, 16, 17


def cmul(a, b):
    return (a[0] * b[0] - a[1] * b[1], a[0] * b[1] + a[1] * b[0])


def cmul_conj(a, b):
    return (a[0] * b[0] + a[1] * b[1], a[1] * b[0] - a[0] * b[1])


def cadd(items):
    result = items[0]
    for item in items[1:]:
        result = (result[0] + item[0], result[1] + item[1])
    return result


def plus_i(a, b):
    return (a[0] - b[1], a[1] + b[0])


def minus_i(a, b):
    return (a[0] + b[1], a[1] - b[0])


def lane_slice(v):
    return slice(v * LANES, (v + 1) * LANES)


def column(chan, rows, at):
    return jnp.broadcast_to(chan[rows, at : at + 1], (ROWS, LANES))


def conv_stream(load, chan, rows, k, lane, prompt_tiles, tiles):
    bias = column(chan, rows, BIAS_CONV + k)
    taps = [column(chan, rows, KERNEL + KER * k + j) for j in range(KER)]
    before = [jnp.zeros((ROWS, LANES), f32)] * (KER - 1)
    last = None
    for v in range(tiles):
        value = load(k, v)
        rolled = [pltpu.roll(value, j, 1) for j in range(1, KER)]
        result = bias + taps[0] * value
        history = before if v < prompt_tiles else last
        for j in range(1, KER):
            result = result + taps[j] * jnp.where(lane < j, history[j - 1], rolled[j - 1])
        if v < prompt_tiles:
            before = rolled
            last = rolled
        yield v, value, result


def block_parts(sz):
    parts = [(slice(i * BLOCK, (i + 1) * BLOCK), BLOCK) for i in range(sz.blocks)]
    start = sz.prompt
    parts += [(slice(start + n * CONT, start + (n + 1) * CONT), CONT) for n in range(sz.per)]
    return parts


def freq_pair(ref, index, rows, tile):
    real = ref[index, rows, lane_slice(tile)]
    imag = ref[index, rows, lane_slice(tile + BLOCK // LANES)]
    return (real, imag)


def store_pair(ref, index, rows, tile, pair):
    ref[index, rows, lane_slice(tile)] = pair[0].astype(ref.dtype)
    ref[index, rows, lane_slice(tile + BLOCK // LANES)] = pair[1].astype(ref.dtype)


def mixer_fwd_kernel(
    sz, normed, weight, chan, resp, table, inverse, mixed, proj, u, z, gb, spec, prod
):
    width = chan.shape[0]
    tiles = normed.shape[1] // LANES
    prompt_tiles = sz.prompt // LANES
    parts = block_parts(sz)
    n = sz.blocks

    @pl.loop(0, normed.shape[1] // BLOCK)
    def _(i):
        cols = pl.ds(pl.multiple_of(i * BLOCK, BLOCK), BLOCK)
        got = jnp.dot(weight[: 3 * width, :], normed[:, cols], preferred_element_type=f32)
        for k in range(3):
            z[k, :, cols] = got[k * width : (k + 1) * width]

    @pl.loop(0, width // ROWS)
    def _(c):
        rows = pl.ds(pl.multiple_of(c * ROWS, ROWS), ROWS)
        lane = lax.broadcasted_iota(jnp.int32, (ROWS, LANES), 1)
        biases = [column(chan, rows, BIAS_IN + k) for k in range(3)]

        def load(k, v):
            return z[k, rows, lane_slice(v)] + biases[k]

        streams = [conv_stream(load, chan, rows, k, lane, prompt_tiles, tiles) for k in range(3)]
        for first, second, third in zip(*streams):
            v = first[0]
            for k, item in enumerate((first, second, third)):
                proj[k, rows, lane_slice(v)] = item[1].astype(bf16)
            gated = second[2] * third[2]
            z[0, rows, lane_slice(v)] = first[2]
            z[1, rows, lane_slice(v)] = gated
            gb[rows, lane_slice(v)] = gated.astype(bf16)

    for i, (cols, length) in enumerate(parts):
        spec[i] = jnp.dot(gb[:, cols], table[:length, :], preferred_element_type=f32)

    @pl.loop(0, width // ROWS)
    def _(c):
        rows = pl.ds(pl.multiple_of(c * ROWS, ROWS), ROWS)
        for tile in range(BLOCK // LANES):
            xs = [freq_pair(spec, i, rows, tile) for i in range(n)]
            hs = [freq_pair(resp, j, rows, tile) for j in range(n + 1)]
            prior = None
            for m in range(n + 1):
                now = cadd([cmul(xs[i], hs[m - i]) for i in range(n) if 0 <= m - i <= n])
                out = now if prior is None else plus_i(now, prior)
                prior = now
                if m < n:
                    store_pair(prod, m, rows, tile, out)
            for q in range(sz.per):
                own = cmul(freq_pair(spec, n + q, rows, tile), hs[0])
                store_pair(prod, n + q, rows, tile, cadd([own, out]))

    skip = chan[:, SKIP : SKIP + 1]
    for i, (cols, length) in enumerate(parts):
        value = jnp.dot(prod[i], inverse[:, :length], preferred_element_type=f32)
        value = value + skip * z[1, :, cols]
        u[:, cols] = value.astype(bf16)
        mixed[:, cols] = (value * z[0, :, cols]).astype(bf16)


def mixer_bwd_kernel(
    sz,
    branch,
    weight,
    proj,
    u,
    chan,
    resp,
    table,
    inverse,
    gz,
    resp_grad,
    sums,
    dm,
    conv,
    gb,
    lb,
    gspec,
    xspec,
    prod,
    gg,
):
    width = chan.shape[0]
    tiles = branch.shape[1] // LANES
    prompt_tiles = sz.prompt // LANES
    parts = block_parts(sz)
    n = sz.blocks

    @pl.loop(0, branch.shape[1] // BLOCK)
    def _(i):
        cols = pl.ds(pl.multiple_of(i * BLOCK, BLOCK), BLOCK)
        dm[:, cols] = jnp.dot(
            weight[3 * width :, :], branch[:, cols], preferred_element_type=f32
        )

    def place_sum(rows, lane, at, value):
        total = jnp.sum(value, axis=1, keepdims=True)
        sums[rows, :] = jnp.where(lane == at, total, sums[rows, :])

    @pl.loop(0, width // ROWS)
    def _(c):
        rows = pl.ds(pl.multiple_of(c * ROWS, ROWS), ROWS)
        lane = lax.broadcasted_iota(jnp.int32, (ROWS, LANES), 1)

        def load(k, v):
            return proj[k, rows, lane_slice(v)].astype(f32)

        streams = [conv_stream(load, chan, rows, k, lane, prompt_tiles, tiles) for k in range(3)]
        skips = jnp.zeros((ROWS, LANES), f32)
        for first, second, third in zip(*streams):
            v = first[0]
            for k, item in enumerate((first, second, third)):
                conv[k, rows, lane_slice(v)] = item[2]
            gated = second[2] * third[2]
            long = dm[rows, lane_slice(v)] * first[2]
            skips = skips + long * gated
            gb[rows, lane_slice(v)] = gated.astype(bf16)
            lb[rows, lane_slice(v)] = long.astype(bf16)
        sums[rows, :] = jnp.zeros((ROWS, LANES), f32)
        place_sum(rows, lane, SKIP, skips)

    for i, (cols, length) in enumerate(parts):
        gspec[i] = jnp.dot(lb[:, cols], table[:length, :], preferred_element_type=f32)
        xspec[i] = jnp.dot(gb[:, cols], table[:length, :], preferred_element_type=f32)

    @pl.loop(0, width // ROWS)
    def _(c):
        rows = pl.ds(pl.multiple_of(c * ROWS, ROWS), ROWS)
        for tile in range(BLOCK // LANES):
            gs = [freq_pair(gspec, i, rows, tile) for i in range(n)]
            hs = [freq_pair(resp, j, rows, tile) for j in range(n + 1)]
            own, lags = [], []
            for q in range(sz.per):
                g = freq_pair(gspec, n + q, rows, tile)
                own.append(g)
                store_pair(prod, n + q, rows, tile, cmul_conj(g, hs[0]))
                lags.append(cmul_conj(g, freq_pair(xspec, n + q, rows, tile)))
            gs.append(cadd(own))
            after = cmul_conj(gs[n], hs[0])
            for i in reversed(range(n)):
                now = cadd([cmul_conj(gs[m], hs[m - i]) for m in range(i, n + 1)])
                store_pair(prod, i, rows, tile, minus_i(now, after))
                after = now
            xs = [freq_pair(xspec, i, rows, tile) for i in range(n)]
            after = None
            for j in reversed(range(n + 1)):
                items = [cmul_conj(gs[m], xs[m - j]) for m in range(j, n + 1) if m - j < n]
                now = cadd(items + (lags if j == 0 else []))
                out = now if after is None else minus_i(now, after)
                store_pair(prod, n + sz.per + j, rows, tile, out)
                after = now

    skip = chan[:, SKIP : SKIP + 1]
    for i, (cols, length) in enumerate(parts):
        value = jnp.dot(prod[i], inverse[:, :length], preferred_element_type=f32)
        gg[:, cols] = value + skip * (dm[:, cols] * conv[0, :, cols])
    for j in range(n + 1):
        resp_grad[:, j * BLOCK : (j + 1) * BLOCK] = jnp.dot(
            prod[n + sz.per + j], inverse[...], preferred_element_type=f32
        )

    @pl.loop(0, width // ROWS)
    def _(c):
        rows = pl.ds(pl.multiple_of(c * ROWS, ROWS), ROWS)
        lane = lax.broadcasted_iota(jnp.int32, (ROWS, LANES), 1)
        zero = jnp.zeros((ROWS, LANES), f32)
        for k in range(3):
            taps = [column(chan, rows, KERNEL + KER * k + j) for j in range(KER)]
            total_bias, total_out = zero, zero
            total_taps = [zero] * KER
            heads = zero
            after = None
            for v in list(range(prompt_tiles, tiles)) + list(reversed(range(prompt_tiles))):
                cols = lane_slice(v)
                if k == 0:
                    grad = dm[rows, cols] * u[rows, cols].astype(f32)
                else:
                    grad = gg[rows, cols] * conv[3 - k, rows, cols]
                rolled = [pltpu.roll(grad, LANES - j, 1) for j in range(1, KER)]
                if v >= prompt_tiles:
                    heads = heads + grad
                    following = [zero] * (KER - 1)
                else:
                    if after is None:
                        after = [pltpu.roll(heads, LANES - j, 1) for j in range(1, KER)]
                    following = after
                    after = rolled
                shifted = [grad] + [
                    jnp.where(lane < LANES - j, rolled[j - 1], following[j - 1])
                    for j in range(1, KER)
                ]
                value = proj[k, rows, cols].astype(f32)
                out = taps[0] * grad
                for j in range(1, KER):
                    out = out + taps[j] * shifted[j]
                low = out.astype(bf16)
                gz[k, rows, cols] = low
                total_bias = total_bias + grad
                total_out = total_out + low.astype(f32)
                total_taps = [t + value * s for t, s in zip(total_taps, shifted)]
            place_sum(rows, lane, BIAS_IN + k, total_out)
            place_sum(rows, lane, BIAS_CONV + k, total_bias)
            for j in range(KER):
                place_sum(rows, lane, KERNEL + KER * k + j, total_taps[j])


VMEM_SPEC = pl.BlockSpec(memory_space=pltpu.VMEM)


SMEM_SPEC = pl.BlockSpec(memory_space=pltpu.SMEM)

def cost(ins, outs, flops=0):
    nbytes = sum(math.prod(v.shape) * v.dtype.itemsize for v in list(ins) + list(outs))
    return pl.CostEstimate(flops=flops, bytes_accessed=nbytes, transcendentals=0)


def call(kernel, ins, outs, scratch, name, limit, scalars=0, flops=0):
    return pl.pallas_call(
        kernel,
        out_shape=tuple(outs),
        in_specs=[SMEM_SPEC] * scalars + [VMEM_SPEC] * (len(ins) - scalars),
        out_specs=tuple([VMEM_SPEC] * len(outs)),
        scratch_shapes=scratch,
        compiler_params=pltpu.CompilerParams(vmem_limit_bytes=limit << 20),
        cost_estimate=cost(ins, outs, flops),
        name=name,
    )(*ins)


def mixer_fwd(normed, weight, chan, resp, table, inverse, sz):
    width = chan.shape[0]
    cols = normed.shape[1]
    parts = sz.blocks + sz.per
    outs = [
        jax.ShapeDtypeStruct((width, cols), bf16),
        jax.ShapeDtypeStruct((3, width, cols), bf16),
        jax.ShapeDtypeStruct((width, cols), bf16),
    ]
    scratch = [
        pltpu.VMEM((3, width, cols), f32),
        pltpu.VMEM((width, cols), bf16),
        pltpu.VMEM((parts, width, 2 * BLOCK), f32),
        pltpu.VMEM((parts, width, 2 * BLOCK), bf16),
    ]
    return call(
        partial(mixer_fwd_kernel, sz),
        (normed, weight, chan, resp, table, inverse),
        outs,
        scratch,
        "mixer_fwd",
        32,
        flops=8 * width * cols * normed.shape[0],
    )


def mixer_bwd(branch, weight, proj, u, chan, resp, table, inverse, sz):
    width = chan.shape[0]
    cols = branch.shape[1]
    parts = sz.blocks + sz.per
    outs = [
        jax.ShapeDtypeStruct((3, width, cols), bf16),
        jax.ShapeDtypeStruct((width, (sz.blocks + 1) * BLOCK), f32),
        jax.ShapeDtypeStruct((width, LANES), f32),
    ]
    scratch = [
        pltpu.VMEM((width, cols), f32),
        pltpu.VMEM((3, width, cols), f32),
        pltpu.VMEM((width, cols), bf16),
        pltpu.VMEM((width, cols), bf16),
        pltpu.VMEM((parts, width, 2 * BLOCK), f32),
        pltpu.VMEM((parts, width, 2 * BLOCK), f32),
        pltpu.VMEM((parts + sz.blocks + 1, width, 2 * BLOCK), bf16),
        pltpu.VMEM((width, cols), f32),
    ]
    return call(
        partial(mixer_bwd_kernel, sz),
        (branch, weight, proj, u, chan, resp, table, inverse),
        outs,
        scratch,
        "mixer_bwd",
        40,
        flops=12 * width * cols * branch.shape[0],
    )


def each_cont(sz, group_map, run):
    y = lax.axis_index("tensor") // 2
    used = [jnp.int32(0), jnp.int32(0)]
    for c in range(sz.per * GRP_DEV):
        local = lax.rem(group_map[c], GRP_DEV)
        rank = jnp.minimum(jnp.where(local == 0, used[0], used[1]), sz.per - 1)
        used = [used[g] + (local == g).astype(jnp.int32) for g in range(GRP_DEV)]
        cols = pl.ds(pl.multiple_of(sz.prompt + rank * CONT, CONT), CONT)
        run(c, local == y, cols)
    return y


def pick_kernel(sz, group_map, lengths, prompt, cont, keep, send, live):
    live[...] = jnp.ones(live.shape, f32)

    def run(c, own, cols):
        @pl.when(own)
        def _():
            keep[:, cols] = cont[c]
            place = lax.broadcasted_iota(jnp.int32, (8, CONT), 1)
            live[:, cols] = jnp.where(place < lengths[c], 1.0, 0.0)

        @pl.when(jnp.logical_not(own))
        def _():
            send[:, cols] = cont[c]

    y = each_cont(sz, group_map, run)
    keep[:, : sz.prompt] = prompt[y]
    send[:, : sz.prompt] = prompt[1 - y]


def pick(group_map, lengths, prompt, cont, sz):
    shape = (prompt.shape[1], sz.prompt + sz.per * CONT)
    outs = [jax.ShapeDtypeStruct(shape, bf16)] * 2
    outs.append(jax.ShapeDtypeStruct((8, shape[1]), f32))
    ins = (group_map, lengths, prompt, cont)
    return call(partial(pick_kernel, sz), ins, outs, [], "pick", 16, 2)


def unpack_kernel(sz, group_map, own, other, prompts, conts):
    kind = prompts.dtype

    def run(c, here, cols):
        @pl.when(here)
        def _():
            conts[c] = own[:, cols].astype(kind)

        @pl.when(jnp.logical_not(here))
        def _():
            conts[c] = other[:, cols].astype(kind)

    y = each_cont(sz, group_map, run)
    prompts[y] = own[:, : sz.prompt].astype(kind)
    prompts[1 - y] = other[:, : sz.prompt].astype(kind)


def unpack(group_map, own, other, sz):
    width = own.shape[0]
    outs = [
        jax.ShapeDtypeStruct((GRP_DEV, width, sz.prompt), own.dtype),
        jax.ShapeDtypeStruct((GRP_DEV * sz.per, width, CONT), own.dtype),
    ]
    ins = (group_map, own, other)
    return call(partial(unpack_kernel, sz), ins, outs, [], "unpack", 24, 1)


def feature_rows(width, r):
    place = lax.axis_index("tensor") ^ r
    return pl.ds(pl.multiple_of(place * width, 64), width)


def norm_one_kernel(width, first, second, third, fourth, vectors, rows, normed, mid, factor):
    parts = (first, second, third, fourth)
    count = len(parts) * width
    total, square = 0.0, 0.0
    for part in parts:
        value = part[...].astype(f32)
        total = total + jnp.sum(value, axis=0, keepdims=True)
        square = square + jnp.sum(value * value, axis=0, keepdims=True)
    center = total / count
    scale = lax.rsqrt(square / count - center * center + epsilon)
    for r, part in enumerate(parts):
        at = feature_rows(width, r)
        value = (part[...].astype(f32) - center) * scale
        rows[at, :] = part[...]
        normed[at, :] = (value * vectors[at, 0:1] + vectors[at, 1:2]).astype(bf16)
    mid[...] = center
    factor[...] = scale


def lane_sum(values):
    return values[:, :LANES] + values[:, LANES:]


def add_sums(sums, width, parts):
    @pl.when(pl.program_id(0) == 0)
    def _():
        sums[...] = jnp.zeros(sums.shape, f32)

    for i, part in enumerate(parts):
        for b in range(2):
            at = slice((2 * i + b) * width, (2 * i + b + 1) * width)
            sums[at, :] = sums[at, :] + lane_sum(part[feature_rows(width, 2 * b), :])


def norm_backward(grad, normal, scale, gain):
    g = grad * gain
    count = g.shape[0]
    first = jnp.sum(g, axis=0, keepdims=True) / count
    second = jnp.sum(g * normal, axis=0, keepdims=True) / count
    return scale * (g - first - normal * second)


def back_two_kernel(
    width, grad, got, resid, mid, factor, base, vectors, low, own, other, sums, work
):
    value = grad[...] + got[...].astype(f32)
    normal = (resid[...] - mid[...]) * factor[...]
    start = base[...].astype(f32)
    result = start + norm_backward(value, normal, factor[...], vectors[:, 3:4])
    rounded = result.astype(bf16)
    low[...] = rounded
    for i, part in enumerate((value * normal, value, rounded.astype(f32), start, result)):
        work[i] = part
    own[...] = work[4, feature_rows(width, 0), :]
    other[...] = work[4, feature_rows(width, 2), :]
    add_sums(sums, width, [work.at[i] for i in range(4)])


def back_one_kernel(
    width, grad, got, rows, mid, factor, near, far, vectors, own, other, sums, work
):
    value = grad[...] + got[...].astype(f32)
    normal = (rows[...].astype(f32) - mid[...]) * factor[...]
    result = norm_backward(value, normal, factor[...], vectors[:, 0:1])
    for i, part in enumerate((value * normal, value, result)):
        work[i] = part
    own[...] = near[...] + work[2, feature_rows(width, 0), :]
    other[...] = (far[...] + work[2, feature_rows(width, 2), :]).astype(bf16)
    add_sums(sums, width, [work.at[i] for i in range(2)])


def grad_kernel(width, first, second, third, fourth, live, grad):
    for r, part in enumerate((first, second, third, fourth)):
        value = part[...].astype(f32) * live[0:1, :]
        grad[feature_rows(width, r), :] = value.astype(bf16)


def by_columns(kernel, ins, outs, name, scratch=()):
    count = outs[0].shape[1]

    def spec(v):
        if v.shape[1] == count:
            return pl.BlockSpec((v.shape[0], BLOCK), lambda i: (0, i))
        return pl.BlockSpec(v.shape, lambda i: (0, 0))

    return pl.pallas_call(
        kernel,
        grid=(count // BLOCK,),
        out_shape=tuple(outs),
        in_specs=[spec(v) for v in ins],
        out_specs=tuple(spec(v) for v in outs),
        scratch_shapes=list(scratch),
        compiler_params=pltpu.CompilerParams(vmem_limit_bytes=32 << 20),
        cost_estimate=cost(ins, outs),
        name=name,
    )(*ins)


def normalize(values):
    count = values.shape[0]
    center = jnp.sum(values, axis=0, keepdims=True) / count
    spread = jnp.sum(values * values, axis=0, keepdims=True) / count - center * center
    scale = lax.rsqrt(spread + epsilon)
    return ((values - center) * scale, center, scale)


def gelu_parts(hidden):
    size = jnp.abs(hidden)
    bell = jnp.exp(-0.5 * hidden * hidden)
    part = 1.0 / (1.0 + (0.3275911 * math.sqrt(0.5)) * size)
    poly = 1.061405429
    for value in (-1.453152027, 1.421413741, -0.284496736, 0.254829592):
        poly = poly * part + value
    tail = 0.5 * poly * part * bell
    cdf = jnp.where(hidden < 0, tail, 1.0 - tail)
    slope = cdf + hidden * (bell * (1.0 / math.sqrt(2.0 * math.pi)))
    return lax.optimization_barrier(((hidden * cdf).astype(bf16), slope.astype(bf16)))


def together(*values):
    return lax.optimization_barrier(values)


def swap(axis, count, bit):
    def run(values):
        return lax.ppermute(values, axis, [(i, i ^ bit) for i in range(count)])

    return run


over_y = swap("tensor", 4, 2)
over_c = swap("tensor", 4, 1)


def halves(values, high):
    half = values.shape[0] // 2
    low_part, high_part = values[:half], values[half:]
    give = jnp.where(high, low_part, high_part).astype(bf16)
    return (give, jnp.where(high, high_part, low_part))


def gathered(held, other, high):
    return jnp.where(
        high,
        jnp.concatenate([other, held], axis=0),
        jnp.concatenate([held, other], axis=0),
    )


def reduce_far(values, count, index, work=None, ins=()):
    bits = [1 << b for b in range(2, count.bit_length() - 1)]
    held, outs = values, None
    for bit in bits:
        give, keep = halves(held, (index & bit) != 0)
        if work is not None and outs is None:
            give, *ins = together(give, *ins)
            outs = work(*ins)
            got, *outs = together(swap("dp", count, bit)(give), *outs)
        else:
            got = swap("dp", count, bit)(give)
        held = keep + got.astype(f32)
    held = held.astype(bf16)
    for bit in reversed(bits):
        held = gathered(held, swap("dp", count, bit)(held), (index & bit) != 0)
    return (held, outs)


def reduce_small(values, count):
    bit = 1
    while bit < count:
        values = values + swap("dp", count, bit)(values)
        bit *= 2
    return values


def shards(dp_count, *args):
    (
        prompt_tokens,
        cont_tokens,
        group_map,
        cont_lengths,
        first_gain,
        first_bias,
        in_weight,
        in_bias,
        conv_kernel,
        conv_bias,
        embed_weight,
        embed_bias,
        inner_weight,
        inner_bias,
        sine_freq,
        filter_weight,
        decay_rate,
        skip_gain,
        out_weight,
        out_bias,
        second_gain,
        second_bias,
        up_weight,
        up_bias,
        down_weight,
        down_bias,
        prompt_cotan,
        cont_cotan,
    ) = args
    width = prompt_tokens.shape[1]
    sz = Sizes()
    sz.prompt = prompt_tokens.shape[2]
    sz.seq = sz.prompt + CONT
    sz.blocks = sz.prompt // BLOCK
    conts = cont_tokens.shape[0]
    sz.per = conts // GRP_DEV
    features = 4 * width
    t = lax.axis_index("tensor")
    y = t // 2
    dp = lax.axis_index("dp")
    table = jnp.asarray(block_table(), bf16)
    inverse = jnp.asarray(block_table().T / BLOCK, bf16)

    over_x = swap("dp", dp_count, 1)
    over_z = swap("dp", dp_count, 2)
    x = dp % 2
    high_x, high_z = x != 0, (dp & 2) != 0
    vectors = jnp.stack([first_gain, first_bias, out_bias, second_gain, second_bias, down_bias], 1)
    vectors_other = over_y(vectors)
    keep, send, live = pick(group_map, cont_lengths, prompt_tokens, cont_tokens, sz)
    got = over_y(send)
    near = over_c(keep)
    vectors = jnp.stack([vectors, vectors_other])
    vectors_near = over_c(vectors)
    odd = t % 2 != 0
    pairs = jnp.where(
        odd, jnp.stack([vectors_near, vectors], 1), jnp.stack([vectors, vectors_near], 1)
    )
    pairs = jnp.where(y != 0, jnp.stack([pairs[1], pairs[0]]), pairs)
    vectors = pairs.reshape(features, -1)
    first_gain, first_bias, out_bias, second_gain, second_bias, down_bias = [
        vectors[:, i : i + 1] for i in range(6)
    ]
    in_bias, conv_kernel, conv_bias, filter_weight, near = together(
        in_bias, conv_kernel, conv_bias, filter_weight, near
    )
    up_rows = up_bias.shape[0] // width
    channel = jnp.concatenate(
        [
            in_bias,
            conv_kernel.reshape(KER * 3, width),
            conv_bias,
            skip_gain[None],
            decay_rate[None],
            filter_weight,
            up_bias.reshape(up_rows, width),
        ],
        axis=0,
    )
    channels = [channel, over_y(channel)]
    up_b = [up_bias, channels[1][-up_rows:].reshape(-1)]
    channels = [value[:-up_rows] for value in channels]

    def half_of(weight):
        half = weight.shape[0] // 2
        return lax.dynamic_slice_in_dim(weight, x * half, half, 0)

    def whole_of(got, other):
        return jnp.where(
            x != 0,
            jnp.concatenate([other, got], axis=0),
            jnp.concatenate([got, other], axis=0),
        )

    mix_own = jnp.concatenate([in_weight.reshape(3 * width, features), out_weight], axis=0)
    mix_part, near = together(half_of(mix_own), near)
    mix_half = over_y(mix_part)
    keep_grad, send_grad, _ = pick(group_map, cont_lengths, prompt_cotan, cont_cotan, sz)
    embed_weight, near = together(embed_weight, near)

    embed = jnp.asarray(embedding_table(sz.seq))
    filter_second, filter_pull = jax.vjp(
        partial(filter_hidden, embed), embed_weight, embed_bias, inner_weight, inner_bias, sine_freq
    )
    steps = jnp.arange(sz.seq, dtype=f32) / (sz.seq - 1)
    resp, envelope = [], []
    for b in range(2):
        decay, weight = channels[b][16], channels[b][17:]
        env = jnp.exp(-decay[:, None] * steps[None, :]) + 0.05
        response = (
            lax.dot_general(weight, filter_second, (((0,), (1,)), ((), ())), precision=highest)
            * env
        )
        padded = jnp.pad(response, ((0, 0), (0, (sz.blocks + 1) * BLOCK - sz.seq)))
        resp.append(
            jnp.stack(
                [
                    spectrum(padded[:, j * BLOCK : (j + 1) * BLOCK], table)
                    for j in range(sz.blocks + 1)
                ]
            )
        )
        envelope.append(env)
    got, mix_half, resp[0] = together(got, mix_half, resp[0])
    got_near = over_c(got)
    up_part, down_part, send_grad, got = together(
        half_of(up_weight), half_of(down_weight), send_grad, got
    )
    got_grad = over_y(send_grad)
    token_blocks = [keep, near, got, got_near]
    rows, normed_one, center_one, scale_one = by_columns(
        partial(norm_one_kernel, width),
        (*token_blocks, vectors),
        [
            jax.ShapeDtypeStruct((features, keep.shape[1]), bf16),
            jax.ShapeDtypeStruct((features, keep.shape[1]), bf16),
            jax.ShapeDtypeStruct((1, keep.shape[1]), f32),
            jax.ShapeDtypeStruct((1, keep.shape[1]), f32),
        ],
        "norm_one",
    )
    mix_rest = over_x(mix_half)
    up_half = over_y(up_part)
    mix_w = [mix_own]
    down_half = over_y(down_part)

    chans = [jnp.pad(value.T, ((0, 0), (0, LANES - value.shape[0]))) for value in channels]
    mixed, saved = [], []
    for b in range(2):
        part, proj, u = mixer_fwd(
            normed_one, mix_w[b], chans[b], resp[b], table, inverse, sz
        )
        if b == 0:
            mix_rest, part = together(mix_rest, part)
            mix_w.append(whole_of(mix_half, mix_rest))
        mixed.append(part)
        saved.append((proj, u))
    out_w = [weight[3 * width :] for weight in mix_w]
    up_half, got_grad, mixed[1] = together(up_half, got_grad, mixed[1])
    up_w = [up_weight, whole_of(up_half, over_x(up_half))]
    grad_blocks = [keep_grad, over_c(keep_grad), got_grad, over_c(got_grad)]
    (grad_back,) = by_columns(
        partial(grad_kernel, width),
        (*grad_blocks, live),
        [jax.ShapeDtypeStruct((features, keep.shape[1]), bf16)],
        "place_grad",
    )
    live = live[0:1]
    mixed_near = [over_c(part) for part in mixed]
    mixed_all = mixed + mixed_near
    out_near = over_c(jnp.concatenate(out_w, axis=0))
    branch = jnp.einsum(
        "cd,cr->dr",
        jnp.concatenate([*out_w, out_near], axis=0),
        jnp.concatenate(mixed_all, axis=0),
        preferred_element_type=f32,
    )
    resid = rows.astype(f32) + branch + out_bias
    normal_two, center_two, scale_two = normalize(resid)
    normed_two = (normal_two * second_gain + second_bias).astype(bf16)
    two, actives = 0.0, []
    up_grad, down_grad, up_bias_grad = [], [], []
    for b in range(2):
        hidden = (
            jnp.einsum("df,dr->fr", up_w[b], normed_two, preferred_element_type=f32)
            + up_b[b][:, None]
        )
        active, slope = gelu_parts(hidden)
        if b == 0:
            down_half, active = together(down_half, active)
            down_w = [down_weight, whole_of(down_half, over_x(down_half))]
        actives.append(active)
        grad_active = jnp.einsum("fd,dr->fr", down_w[b], grad_back, preferred_element_type=f32)
        grad_hidden = (grad_active * slope).astype(bf16)
        up_bias_grad.append(jnp.sum(grad_hidden, axis=1, dtype=f32))
        two = two + jnp.einsum("df,fr->dr", up_w[b], grad_hidden, preferred_element_type=f32)
        down_grad.append(
            jnp.einsum("fr,dr->fd", active, grad_back, preferred_element_type=f32)
        )
        up_grad.append(
            jnp.einsum("dr,fr->df", normed_two, grad_hidden, preferred_element_type=f32)
        )

    block = jax.ShapeDtypeStruct((width, keep.shape[1]), f32)
    grad_branch, near_grad, far_grad, sums_two = by_columns(
        partial(back_two_kernel, width),
        (two, over_c(two.astype(bf16)), resid, center_two, scale_two, grad_back, vectors),
        [
            jax.ShapeDtypeStruct((features, keep.shape[1]), bf16),
            block,
            block,
            jax.ShapeDtypeStruct((8 * width, LANES), f32),
        ],
        "norm_two_back",
        [pltpu.VMEM((5, features, BLOCK), f32)],
    )
    up_gives, up_keeps = zip(*[halves(value, high_z) for value in up_grad])
    up_got = over_z(jnp.concatenate(up_gives, axis=0))
    down_got = over_y(down_grad[1].astype(bf16))

    def out_grad(b):
        return jnp.einsum("cr,dr->cd", mixed[b], grad_branch, preferred_element_type=f32)

    def in_grad(gz):
        return jnp.einsum("er,dr->ed", gz, normed_one, preferred_element_type=f32)

    def mixer_back(b, branch):
        proj, u = saved[b]
        gz, response, sums = mixer_bwd(
            branch, mix_w[b], proj, u, chans[b], resp[b], table, inverse, sz
        )
        return (gz.reshape(3 * width, -1), response, sums)

    def back_in(b, gz):
        return jnp.einsum("ed,er->dr", mix_w[b][: 3 * width], gz, preferred_element_type=f32)

    out_give, branch_now = together(out_grad(1).astype(bf16), grad_branch)
    out_got = over_y(out_give)
    gz_1, response_1, sums_1 = mixer_back(1, branch_now)
    down_got, up_got, out_got, gz_1 = together(down_got, up_got, out_got, gz_1)
    down_give, down_keep = halves(down_grad[0] + down_got.astype(f32), high_x)
    in_give, down_give, branch_now = together(in_grad(gz_1).astype(bf16), down_give, grad_branch)
    down_got, in_got = over_x(down_give), over_y(in_give)
    gz_0, response_0, sums_0 = mixer_back(0, branch_now)
    down_got, in_got, gz_0 = together(down_got, in_got, gz_0)
    up_held = jnp.concatenate(up_keeps, axis=0) + up_got.astype(f32)
    half = up_held.shape[0] // 2
    down_give, down_keep = halves(down_keep + down_got.astype(f32), high_z)
    mix_sum = jnp.concatenate([in_grad(gz_0), out_grad(0)], axis=0) + jnp.concatenate(
        [in_got, out_got], axis=0
    ).astype(f32)
    mix_give, mix_keep = halves(mix_sum, high_x)
    up_give, down_give, mix_give, gz_0 = together(
        up_held[half:].astype(bf16), down_give, mix_give, gz_0
    )
    up_got, down_got, mix_got = over_y(up_give), over_z(down_give), over_x(mix_give)
    pieces = back_in(1, gz_1) + back_in(0, gz_0)
    chan_grads, responses = [sums_1, sums_0], [response_1, response_0]
    pieces_near = over_c(pieces.astype(bf16))
    own_grad, other_grad, sums_one = by_columns(
        partial(back_one_kernel, width),
        (
            pieces,
            pieces_near,
            rows,
            center_one,
            scale_one,
            near_grad,
            far_grad,
            vectors,
        ),
        [
            block,
            jax.ShapeDtypeStruct((width, keep.shape[1]), bf16),
            jax.ShapeDtypeStruct((4 * width, LANES), f32),
        ],
        "norm_one_back",
        [pltpu.VMEM((3, features, BLOCK), f32)],
    )
    grad_pair = [own_grad, over_y(other_grad)]

    up_got, down_got, mix_got, sums_one = together(up_got, down_got, mix_got, sums_one)
    up_give, up_keep = halves(up_held[:half] + up_got.astype(f32), high_x)
    mix_give, mix_keep = halves(mix_keep + mix_got.astype(f32), high_z)
    up_give, mix_give, responses[0], responses[1] = together(up_give, mix_give, *responses)
    up_got, mix_got = over_x(up_give), over_z(mix_give)
    down_far, _ = reduce_far(down_keep + down_got.astype(f32), dp_count, dp)

    second_grads = 0.0
    for i, b in enumerate((1, 0)):
        grad_raw = responses[i][:, : sz.seq] * envelope[b]
        weight = channels[b][17:]
        weight_grad = lax.dot_general(
            filter_second, grad_raw, (((0,), (1,)), ((), ())), precision=highest
        )
        second_grads = second_grads + lax.dot_general(
            grad_raw, weight, (((0,), (1,)), ((), ())), precision=highest
        )
        chan_grads[i] = jnp.concatenate([chan_grads[i].T[:DECAY], weight_grad], axis=0)
    chan_grads = chan_grads[::-1]
    up_got, mix_got, down_far, second_grads = together(up_got, mix_got, down_far, second_grads)
    far_held = jnp.concatenate(
        [mix_keep + mix_got.astype(f32), up_keep + up_got.astype(f32)], axis=1
    )

    def beside(second, active):
        final = jnp.einsum("fd,fr->dr", down_w[0], active, preferred_element_type=f32)
        final = final + jnp.einsum(
            "fd,fr->dr", down_w[1], actives[1], preferred_element_type=f32
        )
        rows = [v if v.ndim == 2 else v[None] for v in filter_pull(second)]
        return (final, jnp.concatenate(rows, axis=0))

    far, (final, filter_rows) = reduce_far(
        far_held, dp_count, dp, beside, (second_grads, actives[0])
    )
    def mine(values, r):
        return lax.dynamic_slice_in_dim(values, width * (t ^ r), width, 0)

    passed = [over_c(mine(final, r).astype(bf16)) for r in (1, 3)]
    ends = []
    for value, r in zip(passed, (0, 2)):
        value = mine(resid, r) + mine(final, r) + value.astype(f32) + mine(down_bias, r)
        ends.append((value * live).astype(bf16))
    out_pair = [ends[0], over_y(ends[1])]
    mix_far, up_far = far[:, :features], far[:, features:]
    down_far = gathered(down_far, over_z(down_far), high_z)
    down_weight_grad = gathered(down_far, over_x(down_far), high_x).astype(f32)
    mix_far = gathered(mix_far, over_z(mix_far), high_z)
    mix_far = gathered(mix_far, over_x(mix_far), high_x).astype(f32)
    up_far = gathered(up_far, over_x(up_far), high_x)
    up_weight_grad = gathered(up_far, over_z(up_far), high_z).astype(f32)
    in_weight_grad = mix_far[: 3 * width].reshape(3, width, features)
    out_weight_grad = mix_far[3 * width :]

    sums_two = jnp.sum(sums_two, axis=1).reshape(4, 2, width)
    sums_one = jnp.sum(sums_one, axis=1).reshape(2, 2, width)
    filter_rows = filter_rows + over_c(filter_rows)
    filter_rows = jnp.pad(filter_rows, ((0, 0), (0, width - filter_rows.shape[1])))
    packs = [
        jnp.concatenate(
            [chan_grads[b], up_bias_grad[b].reshape(up_rows, width), sums_two[:, b], sums_one[:, b], filter_rows],
            axis=0,
        )
        for b in range(2)
    ]
    packed = reduce_small(packs[0] + over_y(packs[1]), dp_count)
    marks = np.cumsum([chan_grads[0].shape[0], up_rows, 6])
    chan_sum = packed[: marks[0]]
    up_bias_sum = packed[marks[0] : marks[1]].reshape(-1)
    vector_sum = packed[marks[1] : marks[2]]
    filter_out = []
    at = marks[2]
    for value in (embed_weight, embed_bias, inner_weight, inner_bias, sine_freq):
        count = value.size // value.shape[-1]
        filter_out.append(packed[at : at + count, : value.shape[-1]].reshape(value.shape))
        at += count

    prompt_out, cont_out = unpack(group_map, *out_pair, sz)
    prompt_grad, cont_grad = unpack(group_map, *grad_pair, sz)
    return (
        prompt_out,
        cont_out,
        prompt_grad,
        cont_grad,
        vector_sum[4],
        vector_sum[5],
        in_weight_grad,
        chan_sum[:3],
        chan_sum[3:12].reshape(3, KER, width),
        chan_sum[12:15],
        filter_out[0],
        filter_out[1],
        filter_out[2],
        filter_out[3],
        filter_out[4],
        chan_sum[16:],
        chan_sum[15],
        out_weight_grad,
        vector_sum[2],
        vector_sum[0],
        vector_sum[1],
        up_weight_grad,
        up_bias_sum,
        down_weight_grad,
        vector_sum[3],
    )


def solution(mesh):
    placed = (
        P("dp", "tensor", None),
        P("dp", "tensor", None),
        P("dp"),
        P("dp"),
        P("tensor"),
        P("tensor"),
        P(None, "tensor", None),
        P(None, "tensor"),
        P(None, None, "tensor"),
        P(None, "tensor"),
        P(),
        P(),
        P(),
        P(),
        P(),
        P(None, "tensor"),
        P("tensor"),
        P("tensor"),
        P("tensor", None),
        P("tensor"),
        P("tensor"),
        P("tensor"),
        P(None, "tensor"),
        P("tensor"),
        P("tensor", None),
        P("tensor"),
        P("dp", "tensor", None),
        P("dp", "tensor", None),
    )
    return jax.shard_map(
        partial(shards, mesh.shape["dp"]),
        mesh=mesh,
        in_specs=placed,
        out_specs=(
            P("dp", "tensor", None),
            P("dp", "tensor", None),
            P("dp", "tensor", None),
            P("dp", "tensor", None),
            P("tensor"),
            P("tensor"),
            P(None, "tensor", None),
            P(None, "tensor"),
            P(None, None, "tensor"),
            P(None, "tensor"),
            P(),
            P(),
            P(),
            P(),
            P(),
            P(None, "tensor"),
            P("tensor"),
            P("tensor", None),
            P("tensor"),
            P("tensor"),
            P("tensor"),
            P(None, "tensor"),
            P("tensor"),
            P("tensor", None),
            P("tensor"),
        ),
        check_vma=False,
    )
```

```python
from functools import partial
import math

import jax
import jax.numpy as jnp
import numpy as np
from jax import lax
from jax.experimental import pallas as pl
from jax.experimental.pallas import tpu as pltpu
from jax.sharding import PartitionSpec as P

EMB = 33
KER = 3
CONT = 128
GRP_DEV = 2
BLOCK = 256

epsilon = 1e-05
highest = lax.Precision.HIGHEST
f32 = jnp.float32
bf16 = jnp.bfloat16


def high_dot(left, right):
    return jnp.dot(left, right, precision=highest)


def embedding_table(length):
    steps = np.arange(length, dtype=np.float32)
    bands = (EMB - 1) // 2
    freqs = np.linspace(0.0001, bands - 1, bands, dtype=np.float32)
    angle = np.float32(2.0 * math.pi) * steps[:, None] * freqs[None, :] / np.float32(length)
    return np.concatenate(
        [steps[:, None] / np.float32(length - 1), np.cos(angle), -np.sin(angle)], axis=1
    ).astype(np.float32)


def filter_hidden(embed, embed_weight, embed_bias, inner_weight, inner_bias, sine_freq):
    first = jnp.sin(sine_freq * (high_dot(embed, embed_weight) + embed_bias))
    return jnp.sin(sine_freq * (high_dot(first, inner_weight) + inner_bias))


def block_table():
    steps = np.arange(BLOCK)
    angle = 2.0 * math.pi / BLOCK * (steps[:, None] * (steps[None, :] + 0.25))
    return np.concatenate([np.cos(angle), -np.sin(angle)], axis=1)


def spectrum(values, table):
    return jnp.dot(values.astype(bf16), table, preferred_element_type=f32)


class Sizes:
    pass


LANES = 128
ROWS = 16
BIAS_IN, KERNEL, BIAS_CONV, SKIP, DECAY, FILTER = 0, 3, 12, 15, 16, 17


def cmul(a, b):
    return (a[0] * b[0] - a[1] * b[1], a[0] * b[1] + a[1] * b[0])


def cmul_conj(a, b):
    return (a[0] * b[0] + a[1] * b[1], a[1] * b[0] - a[0] * b[1])


def cadd(items):
    result = items[0]
    for item in items[1:]:
        result = (result[0] + item[0], result[1] + item[1])
    return result


def plus_i(a, b):
    return (a[0] - b[1], a[1] + b[0])


def minus_i(a, b):
    return (a[0] + b[1], a[1] - b[0])


def lane_slice(v):
    return slice(v * LANES, (v + 1) * LANES)


def column(chan, rows, at):
    return jnp.broadcast_to(chan[rows, at : at + 1], (ROWS, LANES))


def conv_stream(load, chan, rows, k, lane, prompt_tiles, tiles):
    bias = column(chan, rows, BIAS_CONV + k)
    taps = [column(chan, rows, KERNEL + KER * k + j) for j in range(KER)]
    before = [jnp.zeros((ROWS, LANES), f32)] * (KER - 1)
    last = None
    for v in range(tiles):
        value = load(k, v)
        rolled = [pltpu.roll(value, j, 1) for j in range(1, KER)]
        result = bias + taps[0] * value
        history = before if v < prompt_tiles else last
        for j in range(1, KER):
            result = result + taps[j] * jnp.where(lane < j, history[j - 1], rolled[j - 1])
        if v < prompt_tiles:
            before = rolled
            last = rolled
        yield v, value, result


def block_parts(sz):
    parts = [(slice(i * BLOCK, (i + 1) * BLOCK), BLOCK) for i in range(sz.blocks)]
    start = sz.prompt
    parts += [(slice(start + n * CONT, start + (n + 1) * CONT), CONT) for n in range(sz.per)]
    return parts


def freq_pair(ref, index, rows, tile):
    real = ref[index, rows, lane_slice(tile)]
    imag = ref[index, rows, lane_slice(tile + BLOCK // LANES)]
    return (real, imag)


def store_pair(ref, index, rows, tile, pair):
    ref[index, rows, lane_slice(tile)] = pair[0].astype(ref.dtype)
    ref[index, rows, lane_slice(tile + BLOCK // LANES)] = pair[1].astype(ref.dtype)


def mixer_fwd_kernel(
    sz, normed, weight, chan, resp, table, inverse, mixed, proj, u, z, gb, spec, prod
):
    width = chan.shape[0]
    tiles = normed.shape[1] // LANES
    prompt_tiles = sz.prompt // LANES
    parts = block_parts(sz)
    n = sz.blocks

    @pl.loop(0, normed.shape[1] // BLOCK)
    def _(i):
        cols = pl.ds(pl.multiple_of(i * BLOCK, BLOCK), BLOCK)
        got = jnp.dot(weight[: 3 * width, :], normed[:, cols], preferred_element_type=f32)
        for k in range(3):
            z[k, :, cols] = got[k * width : (k + 1) * width]

    @pl.loop(0, width // ROWS)
    def _(c):
        rows = pl.ds(pl.multiple_of(c * ROWS, ROWS), ROWS)
        lane = lax.broadcasted_iota(jnp.int32, (ROWS, LANES), 1)
        biases = [column(chan, rows, BIAS_IN + k) for k in range(3)]

        def load(k, v):
            return z[k, rows, lane_slice(v)] + biases[k]

        streams = [conv_stream(load, chan, rows, k, lane, prompt_tiles, tiles) for k in range(3)]
        for first, second, third in zip(*streams):
            v = first[0]
            for k, item in enumerate((first, second, third)):
                proj[k, rows, lane_slice(v)] = item[1].astype(bf16)
            gated = second[2] * third[2]
            z[0, rows, lane_slice(v)] = first[2]
            z[1, rows, lane_slice(v)] = gated
            gb[rows, lane_slice(v)] = gated.astype(bf16)

    for i, (cols, length) in enumerate(parts):
        spec[i] = jnp.dot(gb[:, cols], table[:length, :], preferred_element_type=f32)

    @pl.loop(0, width // ROWS)
    def _(c):
        rows = pl.ds(pl.multiple_of(c * ROWS, ROWS), ROWS)
        for tile in range(BLOCK // LANES):
            xs = [freq_pair(spec, i, rows, tile) for i in range(n)]
            hs = [freq_pair(resp, j, rows, tile) for j in range(n + 1)]
            prior = None
            for m in range(n + 1):
                now = cadd([cmul(xs[i], hs[m - i]) for i in range(n) if 0 <= m - i <= n])
                out = now if prior is None else plus_i(now, prior)
                prior = now
                if m < n:
                    store_pair(prod, m, rows, tile, out)
            for q in range(sz.per):
                own = cmul(freq_pair(spec, n + q, rows, tile), hs[0])
                store_pair(prod, n + q, rows, tile, cadd([own, out]))

    skip = chan[:, SKIP : SKIP + 1]
    for i, (cols, length) in enumerate(parts):
        value = jnp.dot(prod[i], inverse[:, :length], preferred_element_type=f32)
        value = value + skip * z[1, :, cols]
        u[:, cols] = value.astype(bf16)
        mixed[:, cols] = (value * z[0, :, cols]).astype(bf16)


def mixer_bwd_kernel(
    sz,
    branch,
    weight,
    proj,
    u,
    chan,
    resp,
    table,
    inverse,
    gz,
    resp_grad,
    sums,
    dm,
    conv,
    gb,
    lb,
    gspec,
    xspec,
    prod,
    gg,
):
    width = chan.shape[0]
    tiles = branch.shape[1] // LANES
    prompt_tiles = sz.prompt // LANES
    parts = block_parts(sz)
    n = sz.blocks

    @pl.loop(0, branch.shape[1] // BLOCK)
    def _(i):
        cols = pl.ds(pl.multiple_of(i * BLOCK, BLOCK), BLOCK)
        dm[:, cols] = jnp.dot(
            weight[3 * width :, :], branch[:, cols], preferred_element_type=f32
        )

    def place_sum(rows, lane, at, value):
        total = jnp.sum(value, axis=1, keepdims=True)
        sums[rows, :] = jnp.where(lane == at, total, sums[rows, :])

    @pl.loop(0, width // ROWS)
    def _(c):
        rows = pl.ds(pl.multiple_of(c * ROWS, ROWS), ROWS)
        lane = lax.broadcasted_iota(jnp.int32, (ROWS, LANES), 1)

        def load(k, v):
            return proj[k, rows, lane_slice(v)].astype(f32)

        streams = [conv_stream(load, chan, rows, k, lane, prompt_tiles, tiles) for k in range(3)]
        skips = jnp.zeros((ROWS, LANES), f32)
        for first, second, third in zip(*streams):
            v = first[0]
            for k, item in enumerate((first, second, third)):
                conv[k, rows, lane_slice(v)] = item[2]
            gated = second[2] * third[2]
            long = dm[rows, lane_slice(v)] * first[2]
            skips = skips + long * gated
            gb[rows, lane_slice(v)] = gated.astype(bf16)
            lb[rows, lane_slice(v)] = long.astype(bf16)
        sums[rows, :] = jnp.zeros((ROWS, LANES), f32)
        place_sum(rows, lane, SKIP, skips)

    for i, (cols, length) in enumerate(parts):
        gspec[i] = jnp.dot(lb[:, cols], table[:length, :], preferred_element_type=f32)
        xspec[i] = jnp.dot(gb[:, cols], table[:length, :], preferred_element_type=f32)

    @pl.loop(0, width // ROWS)
    def _(c):
        rows = pl.ds(pl.multiple_of(c * ROWS, ROWS), ROWS)
        for tile in range(BLOCK // LANES):
            gs = [freq_pair(gspec, i, rows, tile) for i in range(n)]
            hs = [freq_pair(resp, j, rows, tile) for j in range(n + 1)]
            own, lags = [], []
            for q in range(sz.per):
                g = freq_pair(gspec, n + q, rows, tile)
                own.append(g)
                store_pair(prod, n + q, rows, tile, cmul_conj(g, hs[0]))
                lags.append(cmul_conj(g, freq_pair(xspec, n + q, rows, tile)))
            gs.append(cadd(own))
            after = cmul_conj(gs[n], hs[0])
            for i in reversed(range(n)):
                now = cadd([cmul_conj(gs[m], hs[m - i]) for m in range(i, n + 1)])
                store_pair(prod, i, rows, tile, minus_i(now, after))
                after = now
            xs = [freq_pair(xspec, i, rows, tile) for i in range(n)]
            after = None
            for j in reversed(range(n + 1)):
                items = [cmul_conj(gs[m], xs[m - j]) for m in range(j, n + 1) if m - j < n]
                now = cadd(items + (lags if j == 0 else []))
                out = now if after is None else minus_i(now, after)
                store_pair(prod, n + sz.per + j, rows, tile, out)
                after = now

    skip = chan[:, SKIP : SKIP + 1]
    for i, (cols, length) in enumerate(parts):
        value = jnp.dot(prod[i], inverse[:, :length], preferred_element_type=f32)
        gg[:, cols] = value + skip * (dm[:, cols] * conv[0, :, cols])
    for j in range(n + 1):
        resp_grad[:, j * BLOCK : (j + 1) * BLOCK] = jnp.dot(
            prod[n + sz.per + j], inverse[...], preferred_element_type=f32
        )

    @pl.loop(0, width // ROWS)
    def _(c):
        rows = pl.ds(pl.multiple_of(c * ROWS, ROWS), ROWS)
        lane = lax.broadcasted_iota(jnp.int32, (ROWS, LANES), 1)
        zero = jnp.zeros((ROWS, LANES), f32)
        for k in range(3):
            taps = [column(chan, rows, KERNEL + KER * k + j) for j in range(KER)]
            total_bias, total_out = zero, zero
            total_taps = [zero] * KER
            heads = zero
            after = None
            for v in list(range(prompt_tiles, tiles)) + list(reversed(range(prompt_tiles))):
                cols = lane_slice(v)
                if k == 0:
                    grad = dm[rows, cols] * u[rows, cols].astype(f32)
                else:
                    grad = gg[rows, cols] * conv[3 - k, rows, cols]
                rolled = [pltpu.roll(grad, LANES - j, 1) for j in range(1, KER)]
                if v >= prompt_tiles:
                    heads = heads + grad
                    following = [zero] * (KER - 1)
                else:
                    if after is None:
                        after = [pltpu.roll(heads, LANES - j, 1) for j in range(1, KER)]
                    following = after
                    after = rolled
                shifted = [grad] + [
                    jnp.where(lane < LANES - j, rolled[j - 1], following[j - 1])
                    for j in range(1, KER)
                ]
                value = proj[k, rows, cols].astype(f32)
                out = taps[0] * grad
                for j in range(1, KER):
                    out = out + taps[j] * shifted[j]
                low = out.astype(bf16)
                gz[k, rows, cols] = low
                total_bias = total_bias + grad
                total_out = total_out + low.astype(f32)
                total_taps = [t + value * s for t, s in zip(total_taps, shifted)]
            place_sum(rows, lane, BIAS_IN + k, total_out)
            place_sum(rows, lane, BIAS_CONV + k, total_bias)
            for j in range(KER):
                place_sum(rows, lane, KERNEL + KER * k + j, total_taps[j])


VMEM_SPEC = pl.BlockSpec(memory_space=pltpu.VMEM)


SMEM_SPEC = pl.BlockSpec(memory_space=pltpu.SMEM)

def cost(ins, outs, flops=0):
    nbytes = sum(math.prod(v.shape) * v.dtype.itemsize for v in list(ins) + list(outs))
    return pl.CostEstimate(flops=flops, bytes_accessed=nbytes, transcendentals=0)


def call(kernel, ins, outs, scratch, name, limit, scalars=0, flops=0):
    return pl.pallas_call(
        kernel,
        out_shape=tuple(outs),
        in_specs=[SMEM_SPEC] * scalars + [VMEM_SPEC] * (len(ins) - scalars),
        out_specs=tuple([VMEM_SPEC] * len(outs)),
        scratch_shapes=scratch,
        compiler_params=pltpu.CompilerParams(vmem_limit_bytes=limit << 20),
        cost_estimate=cost(ins, outs, flops),
        name=name,
    )(*ins)


def mixer_fwd(normed, weight, chan, resp, table, inverse, sz):
    width = chan.shape[0]
    cols = normed.shape[1]
    parts = sz.blocks + sz.per
    outs = [
        jax.ShapeDtypeStruct((width, cols), bf16),
        jax.ShapeDtypeStruct((3, width, cols), bf16),
        jax.ShapeDtypeStruct((width, cols), bf16),
    ]
    scratch = [
        pltpu.VMEM((3, width, cols), f32),
        pltpu.VMEM((width, cols), bf16),
        pltpu.VMEM((parts, width, 2 * BLOCK), f32),
        pltpu.VMEM((parts, width, 2 * BLOCK), bf16),
    ]
    return call(
        partial(mixer_fwd_kernel, sz),
        (normed, weight, chan, resp, table, inverse),
        outs,
        scratch,
        "mixer_fwd",
        32,
        flops=8 * width * cols * normed.shape[0],
    )


def mixer_bwd(branch, weight, proj, u, chan, resp, table, inverse, sz):
    width = chan.shape[0]
    cols = branch.shape[1]
    parts = sz.blocks + sz.per
    outs = [
        jax.ShapeDtypeStruct((3, width, cols), bf16),
        jax.ShapeDtypeStruct((width, (sz.blocks + 1) * BLOCK), f32),
        jax.ShapeDtypeStruct((width, LANES), f32),
    ]
    scratch = [
        pltpu.VMEM((width, cols), f32),
        pltpu.VMEM((3, width, cols), f32),
        pltpu.VMEM((width, cols), bf16),
        pltpu.VMEM((width, cols), bf16),
        pltpu.VMEM((parts, width, 2 * BLOCK), f32),
        pltpu.VMEM((parts, width, 2 * BLOCK), f32),
        pltpu.VMEM((parts + sz.blocks + 1, width, 2 * BLOCK), bf16),
        pltpu.VMEM((width, cols), f32),
    ]
    return call(
        partial(mixer_bwd_kernel, sz),
        (branch, weight, proj, u, chan, resp, table, inverse),
        outs,
        scratch,
        "mixer_bwd",
        40,
        flops=12 * width * cols * branch.shape[0],
    )


def each_cont(sz, group_map, run):
    y = lax.axis_index("tensor") // 2
    used = [jnp.int32(0), jnp.int32(0)]
    for c in range(sz.per * GRP_DEV):
        local = lax.rem(group_map[c], GRP_DEV)
        rank = jnp.minimum(jnp.where(local == 0, used[0], used[1]), sz.per - 1)
        used = [used[g] + (local == g).astype(jnp.int32) for g in range(GRP_DEV)]
        cols = pl.ds(pl.multiple_of(sz.prompt + rank * CONT, CONT), CONT)
        run(c, local == y, cols)
    return y


def pick_kernel(sz, group_map, lengths, prompt, cont, keep, send, live):
    live[...] = jnp.ones(live.shape, f32)

    def run(c, own, cols):
        @pl.when(own)
        def _():
            keep[:, cols] = cont[c]
            place = lax.broadcasted_iota(jnp.int32, (8, CONT), 1)
            live[:, cols] = jnp.where(place < lengths[c], 1.0, 0.0)

        @pl.when(jnp.logical_not(own))
        def _():
            send[:, cols] = cont[c]

    y = each_cont(sz, group_map, run)
    keep[:, : sz.prompt] = prompt[y]
    send[:, : sz.prompt] = prompt[1 - y]


def pick(group_map, lengths, prompt, cont, sz):
    shape = (prompt.shape[1], sz.prompt + sz.per * CONT)
    outs = [jax.ShapeDtypeStruct(shape, bf16)] * 2
    outs.append(jax.ShapeDtypeStruct((8, shape[1]), f32))
    ins = (group_map, lengths, prompt, cont)
    return call(partial(pick_kernel, sz), ins, outs, [], "pick", 16, 2)


def unpack_kernel(sz, group_map, own, other, prompts, conts):
    kind = prompts.dtype

    def run(c, here, cols):
        @pl.when(here)
        def _():
            conts[c] = own[:, cols].astype(kind)

        @pl.when(jnp.logical_not(here))
        def _():
            conts[c] = other[:, cols].astype(kind)

    y = each_cont(sz, group_map, run)
    prompts[y] = own[:, : sz.prompt].astype(kind)
    prompts[1 - y] = other[:, : sz.prompt].astype(kind)


def unpack(group_map, own, other, sz):
    width = own.shape[0]
    outs = [
        jax.ShapeDtypeStruct((GRP_DEV, width, sz.prompt), own.dtype),
        jax.ShapeDtypeStruct((GRP_DEV * sz.per, width, CONT), own.dtype),
    ]
    ins = (group_map, own, other)
    return call(partial(unpack_kernel, sz), ins, outs, [], "unpack", 24, 1)


def feature_rows(width, r):
    place = lax.axis_index("tensor") ^ r
    return pl.ds(pl.multiple_of(place * width, 64), width)


def norm_one_kernel(width, first, second, third, fourth, vectors, rows, normed, mid, factor):
    parts = (first, second, third, fourth)
    count = len(parts) * width
    total, square = 0.0, 0.0
    for part in parts:
        value = part[...].astype(f32)
        total = total + jnp.sum(value, axis=0, keepdims=True)
        square = square + jnp.sum(value * value, axis=0, keepdims=True)
    center = total / count
    scale = lax.rsqrt(square / count - center * center + epsilon)
    for r, part in enumerate(parts):
        at = feature_rows(width, r)
        value = (part[...].astype(f32) - center) * scale
        rows[at, :] = part[...]
        normed[at, :] = (value * vectors[at, 0:1] + vectors[at, 1:2]).astype(bf16)
    mid[...] = center
    factor[...] = scale


def lane_sum(values):
    return values[:, :LANES] + values[:, LANES:]


def add_sums(sums, width, parts):
    @pl.when(pl.program_id(0) == 0)
    def _():
        sums[...] = jnp.zeros(sums.shape, f32)

    for i, part in enumerate(parts):
        for b in range(2):
            at = slice((2 * i + b) * width, (2 * i + b + 1) * width)
            sums[at, :] = sums[at, :] + lane_sum(part[feature_rows(width, 2 * b), :])


def norm_backward(grad, normal, scale, gain):
    g = grad * gain
    count = g.shape[0]
    first = jnp.sum(g, axis=0, keepdims=True) / count
    second = jnp.sum(g * normal, axis=0, keepdims=True) / count
    return scale * (g - first - normal * second)


def back_two_kernel(
    width, grad, got, resid, mid, factor, base, vectors, low, own, other, sums, work
):
    value = grad[...] + got[...].astype(f32)
    normal = (resid[...] - mid[...]) * factor[...]
    start = base[...].astype(f32)
    result = start + norm_backward(value, normal, factor[...], vectors[:, 3:4])
    rounded = result.astype(bf16)
    low[...] = rounded
    for i, part in enumerate((value * normal, value, rounded.astype(f32), start, result)):
        work[i] = part
    own[...] = work[4, feature_rows(width, 0), :]
    other[...] = work[4, feature_rows(width, 2), :]
    add_sums(sums, width, [work.at[i] for i in range(4)])


def back_one_kernel(
    width, grad, got, rows, mid, factor, near, far, vectors, own, other, sums, work
):
    value = grad[...] + got[...].astype(f32)
    normal = (rows[...].astype(f32) - mid[...]) * factor[...]
    result = norm_backward(value, normal, factor[...], vectors[:, 0:1])
    for i, part in enumerate((value * normal, value, result)):
        work[i] = part
    own[...] = near[...] + work[2, feature_rows(width, 0), :]
    other[...] = (far[...] + work[2, feature_rows(width, 2), :]).astype(bf16)
    add_sums(sums, width, [work.at[i] for i in range(2)])


def grad_kernel(width, first, second, third, fourth, live, grad):
    for r, part in enumerate((first, second, third, fourth)):
        value = part[...].astype(f32) * live[0:1, :]
        grad[feature_rows(width, r), :] = value.astype(bf16)


def by_columns(kernel, ins, outs, name, scratch=()):
    count = outs[0].shape[1]

    def spec(v):
        if v.shape[1] == count:
            return pl.BlockSpec((v.shape[0], BLOCK), lambda i: (0, i))
        return pl.BlockSpec(v.shape, lambda i: (0, 0))

    return pl.pallas_call(
        kernel,
        grid=(count // BLOCK,),
        out_shape=tuple(outs),
        in_specs=[spec(v) for v in ins],
        out_specs=tuple(spec(v) for v in outs),
        scratch_shapes=list(scratch),
        compiler_params=pltpu.CompilerParams(vmem_limit_bytes=32 << 20),
        cost_estimate=cost(ins, outs),
        name=name,
    )(*ins)


def normalize(values):
    count = values.shape[0]
    center = jnp.sum(values, axis=0, keepdims=True) / count
    spread = jnp.sum(values * values, axis=0, keepdims=True) / count - center * center
    scale = lax.rsqrt(spread + epsilon)
    return ((values - center) * scale, center, scale)


def gelu_parts(hidden):
    cdf = 0.5 + 0.5 * lax.erf(hidden * math.sqrt(0.5))
    bell = jnp.exp(-0.5 * hidden * hidden) * (1.0 / math.sqrt(2.0 * math.pi))
    slope = cdf + hidden * bell
    return lax.optimization_barrier(((hidden * cdf).astype(bf16), slope.astype(bf16)))


def together(*values):
    return lax.optimization_barrier(values)


def swap(axis, count, bit):
    def run(values):
        return lax.ppermute(values, axis, [(i, i ^ bit) for i in range(count)])

    return run


over_y = swap("tensor", 4, 2)
over_c = swap("tensor", 4, 1)


def halves(values, high):
    half = values.shape[0] // 2
    low_part, high_part = values[:half], values[half:]
    give = jnp.where(high, low_part, high_part).astype(bf16)
    return (give, jnp.where(high, high_part, low_part))


def gathered(held, other, high):
    return jnp.where(
        high,
        jnp.concatenate([other, held], axis=0),
        jnp.concatenate([held, other], axis=0),
    )


def reduce_far(values, count, index, work=None, ins=()):
    bits = [1 << b for b in range(2, count.bit_length() - 1)]
    held, outs = values, None
    for bit in bits:
        give, keep = halves(held, (index & bit) != 0)
        if work is not None and outs is None:
            give, *ins = together(give, *ins)
            outs = work(*ins)
            got, *outs = together(swap("dp", count, bit)(give), *outs)
        else:
            got = swap("dp", count, bit)(give)
        held = keep + got.astype(f32)
    held = held.astype(bf16)
    for bit in reversed(bits):
        held = gathered(held, swap("dp", count, bit)(held), (index & bit) != 0)
    return (held, outs)


def reduce_small(values, count):
    bit = 1
    while bit < count:
        values = values + swap("dp", count, bit)(values)
        bit *= 2
    return values


def shards(dp_count, *args):
    (
        prompt_tokens,
        cont_tokens,
        group_map,
        cont_lengths,
        first_gain,
        first_bias,
        in_weight,
        in_bias,
        conv_kernel,
        conv_bias,
        embed_weight,
        embed_bias,
        inner_weight,
        inner_bias,
        sine_freq,
        filter_weight,
        decay_rate,
        skip_gain,
        out_weight,
        out_bias,
        second_gain,
        second_bias,
        up_weight,
        up_bias,
        down_weight,
        down_bias,
        prompt_cotan,
        cont_cotan,
    ) = args
    width = prompt_tokens.shape[1]
    sz = Sizes()
    sz.prompt = prompt_tokens.shape[2]
    sz.seq = sz.prompt + CONT
    sz.blocks = sz.prompt // BLOCK
    conts = cont_tokens.shape[0]
    sz.per = conts // GRP_DEV
    features = 4 * width
    t = lax.axis_index("tensor")
    y = t // 2
    dp = lax.axis_index("dp")
    table = jnp.asarray(block_table(), bf16)
    inverse = jnp.asarray(block_table().T / BLOCK, bf16)

    over_x = swap("dp", dp_count, 1)
    over_z = swap("dp", dp_count, 2)
    x = dp % 2
    high_x, high_z = x != 0, (dp & 2) != 0
    vectors = jnp.stack([first_gain, first_bias, out_bias, second_gain, second_bias, down_bias], 1)
    vectors_other = over_y(vectors)
    keep, send, live = pick(group_map, cont_lengths, prompt_tokens, cont_tokens, sz)
    got = over_y(send)
    near = over_c(keep)
    vectors = jnp.stack([vectors, vectors_other])
    vectors_near = over_c(vectors)
    odd = t % 2 != 0
    pairs = jnp.where(
        odd, jnp.stack([vectors_near, vectors], 1), jnp.stack([vectors, vectors_near], 1)
    )
    pairs = jnp.where(y != 0, jnp.stack([pairs[1], pairs[0]]), pairs)
    vectors = pairs.reshape(features, -1)
    first_gain, first_bias, out_bias, second_gain, second_bias, down_bias = [
        vectors[:, i : i + 1] for i in range(6)
    ]
    in_bias, conv_kernel, conv_bias, filter_weight, near = together(
        in_bias, conv_kernel, conv_bias, filter_weight, near
    )
    up_rows = up_bias.shape[0] // width
    channel = jnp.concatenate(
        [
            in_bias,
            conv_kernel.reshape(KER * 3, width),
            conv_bias,
            skip_gain[None],
            decay_rate[None],
            filter_weight,
            up_bias.reshape(up_rows, width),
        ],
        axis=0,
    )
    channels = [channel, over_y(channel)]
    up_b = [up_bias, channels[1][-up_rows:].reshape(-1)]
    channels = [value[:-up_rows] for value in channels]

    def half_of(weight):
        half = weight.shape[0] // 2
        return lax.dynamic_slice_in_dim(weight, x * half, half, 0)

    def whole_of(got, other):
        return jnp.where(
            x != 0,
            jnp.concatenate([other, got], axis=0),
            jnp.concatenate([got, other], axis=0),
        )

    mix_own = jnp.concatenate([in_weight.reshape(3 * width, features), out_weight], axis=0)
    mix_part, near = together(half_of(mix_own), near)
    mix_half = over_y(mix_part)
    keep_grad, send_grad, _ = pick(group_map, cont_lengths, prompt_cotan, cont_cotan, sz)
    embed_weight, near = together(embed_weight, near)

    embed = jnp.asarray(embedding_table(sz.seq))
    filter_second, filter_pull = jax.vjp(
        partial(filter_hidden, embed), embed_weight, embed_bias, inner_weight, inner_bias, sine_freq
    )
    steps = jnp.arange(sz.seq, dtype=f32) / (sz.seq - 1)
    resp, envelope = [], []
    for b in range(2):
        decay, weight = channels[b][16], channels[b][17:]
        env = jnp.exp(-decay[:, None] * steps[None, :]) + 0.05
        response = (
            lax.dot_general(weight, filter_second, (((0,), (1,)), ((), ())), precision=highest)
            * env
        )
        padded = jnp.pad(response, ((0, 0), (0, (sz.blocks + 1) * BLOCK - sz.seq)))
        resp.append(
            jnp.stack(
                [
                    spectrum(padded[:, j * BLOCK : (j + 1) * BLOCK], table)
                    for j in range(sz.blocks + 1)
                ]
            )
        )
        envelope.append(env)
    got, mix_half, resp[0] = together(got, mix_half, resp[0])
    got_near = over_c(got)
    up_part, down_part, send_grad, got = together(
        half_of(up_weight), half_of(down_weight), send_grad, got
    )
    got_grad = over_y(send_grad)
    token_blocks = [keep, near, got, got_near]
    rows, normed_one, center_one, scale_one = by_columns(
        partial(norm_one_kernel, width),
        (*token_blocks, vectors),
        [
            jax.ShapeDtypeStruct((features, keep.shape[1]), bf16),
            jax.ShapeDtypeStruct((features, keep.shape[1]), bf16),
            jax.ShapeDtypeStruct((1, keep.shape[1]), f32),
            jax.ShapeDtypeStruct((1, keep.shape[1]), f32),
        ],
        "norm_one",
    )
    mix_rest = over_x(mix_half)
    up_half = over_y(up_part)
    mix_w = [mix_own]
    down_half = over_y(down_part)

    chans = [jnp.pad(value.T, ((0, 0), (0, LANES - value.shape[0]))) for value in channels]
    mixed, saved = [], []
    for b in range(2):
        part, proj, u = mixer_fwd(
            normed_one, mix_w[b], chans[b], resp[b], table, inverse, sz
        )
        if b == 0:
            mix_rest, part = together(mix_rest, part)
            mix_w.append(whole_of(mix_half, mix_rest))
        mixed.append(part)
        saved.append((proj, u))
    out_w = [weight[3 * width :] for weight in mix_w]
    up_half, got_grad, mixed[1] = together(up_half, got_grad, mixed[1])
    up_w = [up_weight, whole_of(up_half, over_x(up_half))]
    grad_blocks = [keep_grad, over_c(keep_grad), got_grad, over_c(got_grad)]
    (grad_back,) = by_columns(
        partial(grad_kernel, width),
        (*grad_blocks, live),
        [jax.ShapeDtypeStruct((features, keep.shape[1]), bf16)],
        "place_grad",
    )
    live = live[0:1]
    mixed_near = [over_c(part) for part in mixed]
    mixed_all = mixed + mixed_near
    out_near = over_c(jnp.concatenate(out_w, axis=0))
    branch = jnp.einsum(
        "cd,cr->dr",
        jnp.concatenate([*out_w, out_near], axis=0),
        jnp.concatenate(mixed_all, axis=0),
        preferred_element_type=f32,
    )
    resid = rows.astype(f32) + branch + out_bias
    normal_two, center_two, scale_two = normalize(resid)
    normed_two = (normal_two * second_gain + second_bias).astype(bf16)
    two, actives = 0.0, []
    up_grad, down_grad, up_bias_grad = [], [], []
    for b in range(2):
        hidden = (
            jnp.einsum("df,dr->fr", up_w[b], normed_two, preferred_element_type=f32)
            + up_b[b][:, None]
        )
        active, slope = gelu_parts(hidden)
        if b == 0:
            down_half, active = together(down_half, active)
            down_w = [down_weight, whole_of(down_half, over_x(down_half))]
        actives.append(active)
        grad_active = jnp.einsum("fd,dr->fr", down_w[b], grad_back, preferred_element_type=f32)
        grad_hidden = (grad_active * slope).astype(bf16)
        up_bias_grad.append(jnp.sum(grad_hidden, axis=1, dtype=f32))
        two = two + jnp.einsum("df,fr->dr", up_w[b], grad_hidden, preferred_element_type=f32)
        down_grad.append(
            jnp.einsum("fr,dr->fd", active, grad_back, preferred_element_type=f32)
        )
        up_grad.append(
            jnp.einsum("dr,fr->df", normed_two, grad_hidden, preferred_element_type=f32)
        )

    block = jax.ShapeDtypeStruct((width, keep.shape[1]), f32)
    grad_branch, near_grad, far_grad, sums_two = by_columns(
        partial(back_two_kernel, width),
        (two, over_c(two.astype(bf16)), resid, center_two, scale_two, grad_back, vectors),
        [
            jax.ShapeDtypeStruct((features, keep.shape[1]), bf16),
            block,
            block,
            jax.ShapeDtypeStruct((8 * width, LANES), f32),
        ],
        "norm_two_back",
        [pltpu.VMEM((5, features, BLOCK), f32)],
    )
    up_gives, up_keeps = zip(*[halves(value, high_z) for value in up_grad])
    up_got = over_z(jnp.concatenate(up_gives, axis=0))
    down_got = over_y(down_grad[1].astype(bf16))

    def out_grad(b):
        return jnp.einsum("cr,dr->cd", mixed[b], grad_branch, preferred_element_type=f32)

    def in_grad(gz):
        return jnp.einsum("er,dr->ed", gz, normed_one, preferred_element_type=f32)

    def mixer_back(b, branch):
        proj, u = saved[b]
        gz, response, sums = mixer_bwd(
            branch, mix_w[b], proj, u, chans[b], resp[b], table, inverse, sz
        )
        return (gz.reshape(3 * width, -1), response, sums)

    def back_in(b, gz):
        return jnp.einsum("ed,er->dr", mix_w[b][: 3 * width], gz, preferred_element_type=f32)

    out_give, branch_now = together(out_grad(1).astype(bf16), grad_branch)
    out_got = over_y(out_give)
    gz_1, response_1, sums_1 = mixer_back(1, branch_now)
    down_got, up_got, out_got, gz_1 = together(down_got, up_got, out_got, gz_1)
    down_give, down_keep = halves(down_grad[0] + down_got.astype(f32), high_x)
    in_give, down_give, branch_now = together(in_grad(gz_1).astype(bf16), down_give, grad_branch)
    down_got, in_got = over_x(down_give), over_y(in_give)
    gz_0, response_0, sums_0 = mixer_back(0, branch_now)
    down_got, in_got, gz_0 = together(down_got, in_got, gz_0)
    up_held = jnp.concatenate(up_keeps, axis=0) + up_got.astype(f32)
    half = up_held.shape[0] // 2
    down_give, down_keep = halves(down_keep + down_got.astype(f32), high_z)
    mix_sum = jnp.concatenate([in_grad(gz_0), out_grad(0)], axis=0) + jnp.concatenate(
        [in_got, out_got], axis=0
    ).astype(f32)
    mix_give, mix_keep = halves(mix_sum, high_x)
    up_give, down_give, mix_give, gz_0 = together(
        up_held[half:].astype(bf16), down_give, mix_give, gz_0
    )
    up_got, down_got, mix_got = over_y(up_give), over_z(down_give), over_x(mix_give)
    pieces = back_in(1, gz_1) + back_in(0, gz_0)
    chan_grads, responses = [sums_1, sums_0], [response_1, response_0]
    pieces_near = over_c(pieces.astype(bf16))
    own_grad, other_grad, sums_one = by_columns(
        partial(back_one_kernel, width),
        (
            pieces,
            pieces_near,
            rows,
            center_one,
            scale_one,
            near_grad,
            far_grad,
            vectors,
        ),
        [
            block,
            jax.ShapeDtypeStruct((width, keep.shape[1]), bf16),
            jax.ShapeDtypeStruct((4 * width, LANES), f32),
        ],
        "norm_one_back",
        [pltpu.VMEM((3, features, BLOCK), f32)],
    )
    grad_pair = [own_grad, over_y(other_grad)]

    up_got, down_got, mix_got, sums_one = together(up_got, down_got, mix_got, sums_one)
    up_give, up_keep = halves(up_held[:half] + up_got.astype(f32), high_x)
    mix_give, mix_keep = halves(mix_keep + mix_got.astype(f32), high_z)
    up_give, mix_give, responses[0], responses[1] = together(up_give, mix_give, *responses)
    up_got, mix_got = over_x(up_give), over_z(mix_give)
    down_far, _ = reduce_far(down_keep + down_got.astype(f32), dp_count, dp)

    second_grads = 0.0
    for i, b in enumerate((1, 0)):
        grad_raw = responses[i][:, : sz.seq] * envelope[b]
        weight = channels[b][17:]
        weight_grad = lax.dot_general(
            filter_second, grad_raw, (((0,), (1,)), ((), ())), precision=highest
        )
        second_grads = second_grads + lax.dot_general(
            grad_raw, weight, (((0,), (1,)), ((), ())), precision=highest
        )
        chan_grads[i] = jnp.concatenate([chan_grads[i].T[:DECAY], weight_grad], axis=0)
    chan_grads = chan_grads[::-1]
    up_got, mix_got, down_far, second_grads = together(up_got, mix_got, down_far, second_grads)
    far_held = jnp.concatenate(
        [mix_keep + mix_got.astype(f32), up_keep + up_got.astype(f32)], axis=1
    )

    def beside(second, active):
        final = jnp.einsum("fd,fr->dr", down_w[0], active, preferred_element_type=f32)
        final = final + jnp.einsum(
            "fd,fr->dr", down_w[1], actives[1], preferred_element_type=f32
        )
        rows = [v if v.ndim == 2 else v[None] for v in filter_pull(second)]
        return (final, jnp.concatenate(rows, axis=0))

    far, (final, filter_rows) = reduce_far(
        far_held, dp_count, dp, beside, (second_grads, actives[0])
    )
    def mine(values, r):
        return lax.dynamic_slice_in_dim(values, width * (t ^ r), width, 0)

    passed = [over_c(mine(final, r).astype(bf16)) for r in (1, 3)]
    ends = []
    for value, r in zip(passed, (0, 2)):
        value = mine(resid, r) + mine(final, r) + value.astype(f32) + mine(down_bias, r)
        ends.append((value * live).astype(bf16))
    out_pair = [ends[0], over_y(ends[1])]
    mix_far, up_far = far[:, :features], far[:, features:]
    down_far = gathered(down_far, over_z(down_far), high_z)
    down_weight_grad = gathered(down_far, over_x(down_far), high_x).astype(f32)
    mix_far = gathered(mix_far, over_z(mix_far), high_z)
    mix_far = gathered(mix_far, over_x(mix_far), high_x).astype(f32)
    up_far = gathered(up_far, over_x(up_far), high_x)
    up_weight_grad = gathered(up_far, over_z(up_far), high_z).astype(f32)
    in_weight_grad = mix_far[: 3 * width].reshape(3, width, features)
    out_weight_grad = mix_far[3 * width :]

    sums_two = jnp.sum(sums_two, axis=1).reshape(4, 2, width)
    sums_one = jnp.sum(sums_one, axis=1).reshape(2, 2, width)
    filter_rows = filter_rows + over_c(filter_rows)
    filter_rows = jnp.pad(filter_rows, ((0, 0), (0, width - filter_rows.shape[1])))
    packs = [
        jnp.concatenate(
            [chan_grads[b], up_bias_grad[b].reshape(up_rows, width), sums_two[:, b], sums_one[:, b], filter_rows],
            axis=0,
        )
        for b in range(2)
    ]
    packed = reduce_small(packs[0] + over_y(packs[1]), dp_count)
    marks = np.cumsum([chan_grads[0].shape[0], up_rows, 6])
    chan_sum = packed[: marks[0]]
    up_bias_sum = packed[marks[0] : marks[1]].reshape(-1)
    vector_sum = packed[marks[1] : marks[2]]
    filter_out = []
    at = marks[2]
    for value in (embed_weight, embed_bias, inner_weight, inner_bias, sine_freq):
        count = value.size // value.shape[-1]
        filter_out.append(packed[at : at + count, : value.shape[-1]].reshape(value.shape))
        at += count

    prompt_out, cont_out = unpack(group_map, *out_pair, sz)
    prompt_grad, cont_grad = unpack(group_map, *grad_pair, sz)
    return (
        prompt_out,
        cont_out,
        prompt_grad,
        cont_grad,
        vector_sum[4],
        vector_sum[5],
        in_weight_grad,
        chan_sum[:3],
        chan_sum[3:12].reshape(3, KER, width),
        chan_sum[12:15],
        filter_out[0],
        filter_out[1],
        filter_out[2],
        filter_out[3],
        filter_out[4],
        chan_sum[16:],
        chan_sum[15],
        out_weight_grad,
        vector_sum[2],
        vector_sum[0],
        vector_sum[1],
        up_weight_grad,
        up_bias_sum,
        down_weight_grad,
        vector_sum[3],
    )


def solution(mesh):
    placed = (
        P("dp", "tensor", None),
        P("dp", "tensor", None),
        P("dp"),
        P("dp"),
        P("tensor"),
        P("tensor"),
        P(None, "tensor", None),
        P(None, "tensor"),
        P(None, None, "tensor"),
        P(None, "tensor"),
        P(),
        P(),
        P(),
        P(),
        P(),
        P(None, "tensor"),
        P("tensor"),
        P("tensor"),
        P("tensor", None),
        P("tensor"),
        P("tensor"),
        P("tensor"),
        P(None, "tensor"),
        P("tensor"),
        P("tensor", None),
        P("tensor"),
        P("dp", "tensor", None),
        P("dp", "tensor", None),
    )
    return jax.shard_map(
        partial(shards, mesh.shape["dp"]),
        mesh=mesh,
        in_specs=placed,
        out_specs=(
            P("dp", "tensor", None),
            P("dp", "tensor", None),
            P("dp", "tensor", None),
            P("dp", "tensor", None),
            P("tensor"),
            P("tensor"),
            P(None, "tensor", None),
            P(None, "tensor"),
            P(None, None, "tensor"),
            P(None, "tensor"),
            P(),
            P(),
            P(),
            P(),
            P(),
            P(None, "tensor"),
            P("tensor"),
            P("tensor", None),
            P("tensor"),
            P("tensor"),
            P("tensor"),
            P(None, "tensor"),
            P("tensor"),
            P("tensor", None),
            P("tensor"),
        ),
        check_vma=False,
    )
```
